128 devices in a mesh: dp: 16 (over z, x), mp: 8 (over y, core).
Axes of the slice: x: 4, y: 4, z: 4, core: 2. Of those that a mesh axis runs over, the one named last changes fastest.
Arguments:
- tokens: bfloat16 [32768, 2048], P('dp'), may hold values from -0.75 to 0.75
- out_grad: bfloat16 [32768, 2048], P('dp'), may hold values from -3 to 3
- down_rows: bfloat16 [8192, 2048], P(('dp', 'mp')), may hold values from -1 to 1
- up_rows: bfloat16 [8192, 2048], P(('dp', 'mp')), may hold values from -1 to 1
- requests: int32 [128, 128, 2], P(('dp', 'mp')), may hold values from 0 to 64, as said below
- places: int32 [8, 32768, 16], P('mp', 'dp'), may hold values from 0 to 255, as said below
- gate_weights: float32 [8, 32768, 16], P('mp', 'dp'), may hold values from 0.05 to 0.5
Outputs:
- input_grad: bfloat16 [32768, 2048], P(('dp', 'mp'))
- down_grad: float32 [8192, 2048], P(('dp', 'mp'))
- up_grad: float32 [8192, 2048], P(('dp', 'mp'))
The draws below stay inside these ranges and needn't reach their ends.
Inputs may be any that keep to these rules, and one draw needn't show every extreme that they name: requests[d, o] lists distinct rows, numbered within owner o's block of 64, that device d uses; the used ones come first and the rest of the 2 places hold 64. Every device uses at least one row of every owner, and all 2 places of some owner. The 16 entries of one head and token are distinct places, each of which names an expert in the request list of the device holding that head and token.
All inputs are finite; a program needn't handle non-finite values.
Results may differ from the reference program's by a relative error of at most 0.013.
Values may be sent and summed in bfloat16 or wider, within the bound.
No kernel may reach another device: no remote copies, remote signals or barrier semaphores. Data moves between devices by JAX's collectives and lax.ppermute only.
A program may use at most 128 MiB of HBM per device.

```python
import math
import jax
import jax.numpy as jnp
from jax import lax

D = 2048
HEADS = 8
TOPK = 16
TOK_DEV = 2048
HOT_DEV = 64
UCAP = 2
HEADS_DEV = 1
HOT = 8192
SLOTS = 256
TOKENS = 32768
N_MP = 8
DEVICES = 128


def request_lists(key):
    count_key, full_key, order_key = jax.random.split(jax.random.fold_in(key, 101), 3)
    counts = jax.random.randint(count_key, (DEVICES, DEVICES), 1, UCAP + 1)
    full_owner = jax.random.randint(full_key, (DEVICES,), 0, DEVICES)
    owner_index = jnp.arange(DEVICES)[None, :]
    counts = jnp.where(owner_index == full_owner[:, None], UCAP, counts)
    scores = jax.random.randint(order_key, (DEVICES, DEVICES, HOT_DEV), 0, 1 << 20) * HOT_DEV + jnp.arange(HOT_DEV)[None, None, :]
    chosen = jnp.argsort(scores, axis=-1)[:, :, :UCAP]
    position = jnp.arange(UCAP)[None, None, :]
    return jnp.where(position < counts[:, :, None], chosen, HOT_DEV).astype(jnp.int32)


def draw_requests(key, part):
    return request_lists(key)


def draw_places(key, part):
    lists = request_lists(key).reshape(DEVICES, SLOTS)
    live = lists < HOT_DEV
    popular_key, noise_key = jax.random.split(jax.random.fold_in(key, 202))
    popular = jax.random.randint(popular_key, (DEVICES, SLOTS), 0, 1 << 10)
    slot_index = jnp.arange(SLOTS)[None, :]

    def one_head(head):
        noise = jax.random.randint(jax.random.fold_in(noise_key, head), (TOKENS, SLOTS), 0, 1 << 10)
        device = jnp.arange(TOKENS) // TOK_DEV * N_MP + head // HEADS_DEV
        score = (popular[device] + noise) * SLOTS + slot_index
        score = jnp.where(live[device], score, -1 - slot_index)
        return lax.top_k(score, TOPK)[1].astype(jnp.int32)
    return lax.map(one_head, jnp.arange(HEADS))


def level_of(stream_key, dims, cuts, smallest, high):
    gain = 1.0
    for axis_at, shards_of in cuts:
        steps = jax.random.uniform(jax.random.fold_in(jax.random.fold_in(stream_key, 6), axis_at), (shards_of,), jnp.float32, smallest / len(cuts), high / len(cuts))
        gain = gain * jnp.repeat(jnp.exp(steps), dims[axis_at] // shards_of).reshape((-1,) + (1,) * (len(dims) - 1 - axis_at))
    return gain


def gaussian(stream_key, extent, spread, reach, cuts=(), kind=jnp.bfloat16):
    values = jax.random.normal(stream_key, extent, jnp.float32) * spread
    if len(cuts) > 0:
        values = level_of(stream_key, extent, cuts, -0.22, 0.18) * values
    return jnp.clip(values, min=-reach, max=reach).astype(kind)


def setup_inputs(seed: int = 0) -> dict:
    seeds = jax.random.split(jax.random.key(seed), 8)
    return {
        "tokens": gaussian(seeds[0], (TOKENS, D), 0.125, 0.75, ((0, 16),)),
        "out_grad": gaussian(seeds[1], (TOKENS, D), 0.5, 3.0, ((0, 16),)),
        "down_rows": gaussian(seeds[2], (HOT, D), (D // 64) ** -0.5, 1.0, ((0, 128),)),
        "up_rows": gaussian(seeds[3], (HOT, D), (D // 48) ** -0.5, 1.0, ((0, 128),)),
        "requests": draw_requests(jax.random.fold_in(seeds[7], 71), 0),
        "places": draw_places(jax.random.fold_in(seeds[7], 71), 0),
        "gate_weights": jnp.clip(jnp.exp(math.log(0.5) - 2.3025851 * jax.random.uniform(seeds[6], (HEADS, TOKENS, TOPK), jnp.float32) ** level_of(seeds[6], (HEADS, TOKENS, TOPK), ((0, 8), (1, 16)), -0.2, 0.2)), 0.05, 0.5),
    }


SQRT_HALF = 0.7071067811865476
INV_ROOT_TAU = 0.3989422804014327


def gelu_parts(pre):
    normal_cdf = 0.5 * (1.0 + lax.erf(pre * SQRT_HALF))
    density = INV_ROOT_TAU * jnp.exp(-0.5 * pre * pre)
    return pre * normal_cdf, normal_cdf + pre * density


def local_terms(block_tokens, block_grad, fetched_down, fetched_up, block_places, block_gates):
    token_count = block_tokens.shape[0]
    place_count = fetched_down.shape[0]
    chosen = jnp.transpose(block_places, (1, 0, 2)).reshape(token_count, -1)
    weights_in = jnp.transpose(block_gates, (1, 0, 2)).reshape(token_count, -1)
    columns = jnp.arange(place_count, dtype=jnp.int32)
    weight = jnp.sum(jnp.where(chosen[:, :, None] == columns[None, None, :], weights_in[:, :, None], jnp.zeros((), weights_in.dtype)), axis=1)
    pre = lax.dot_general(block_tokens, fetched_down, (((1,), (1,)), ((), ())), preferred_element_type=jnp.float32)
    back = lax.dot_general(block_grad, fetched_up, (((1,), (1,)), ((), ())), preferred_element_type=jnp.float32)
    active, slope = gelu_parts(pre)
    coef = (weight * slope * back).astype(jnp.bfloat16)
    gated = (weight * active).astype(jnp.bfloat16)
    part_down = lax.dot_general(coef, block_tokens, (((0,), (0,)), ((), ())), preferred_element_type=jnp.float32)
    part_up = lax.dot_general(gated, block_grad, (((0,), (0,)), ((), ())), preferred_element_type=jnp.float32)
    return coef, part_down, part_up


def reference(tokens, out_grad, down_rows, up_rows, requests, places, gate_weights):
    owner_base = jnp.arange(DEVICES, dtype=jnp.int32)[:, None] * HOT_DEV

    def visit(carry, device):
        down_acc, up_acc, input_acc = carry
        row_block = device // N_MP
        col_block = device % N_MP
        asked = lax.dynamic_index_in_dim(requests, device, 0, keepdims=False)
        live = (asked < HOT_DEV).reshape(-1)
        experts = (owner_base + jnp.minimum(asked, HOT_DEV - 1)).reshape(-1).astype(jnp.int32)
        fetched_down = jnp.where(live[:, None], down_rows[experts], jnp.zeros((), down_rows.dtype))
        fetched_up = jnp.where(live[:, None], up_rows[experts], jnp.zeros((), up_rows.dtype))
        token_start = (row_block * TOK_DEV).astype(jnp.int32)
        head_start = (col_block * HEADS_DEV).astype(jnp.int32)
        zero_index = jnp.zeros((), jnp.int32)
        block_tokens = lax.dynamic_slice_in_dim(tokens, token_start, TOK_DEV, 0)
        block_grad = lax.dynamic_slice_in_dim(out_grad, token_start, TOK_DEV, 0)
        block_places = lax.dynamic_slice(places, (head_start, token_start, zero_index), (HEADS_DEV, TOK_DEV, TOPK))
        block_gates = lax.dynamic_slice(gate_weights, (head_start, token_start, zero_index), (HEADS_DEV, TOK_DEV, TOPK))
        coef, part_down, part_up = local_terms(block_tokens, block_grad, fetched_down, fetched_up, block_places, block_gates)
        partial_value = jnp.dot(coef, fetched_down, preferred_element_type=jnp.float32).astype(jnp.bfloat16)
        targets = jnp.where(live, experts, HOT).astype(jnp.int32)
        down_acc = down_acc.at[targets].add(part_down, mode="drop")
        up_acc = up_acc.at[targets].add(part_up, mode="drop")
        previous = lax.dynamic_slice_in_dim(input_acc, token_start, TOK_DEV, 0)
        input_acc = lax.dynamic_update_slice_in_dim(input_acc, previous + partial_value.astype(jnp.float32), token_start, 0)
        return (down_acc, up_acc, input_acc), None

    start = (jnp.zeros((HOT, D), jnp.float32), jnp.zeros((HOT, D), jnp.float32), jnp.zeros((TOKENS, D), jnp.float32))
    final, _ = lax.scan(visit, start, jnp.arange(DEVICES, dtype=jnp.int32))
    down_grad, up_grad, input_acc = final
    return input_acc.astype(jnp.bfloat16), down_grad, up_grad
```

```python
import functools
import jax
import jax.numpy as jnp
from jax import lax
from jax.experimental import pallas as pl
from jax.experimental.pallas import tpu as pltpu
from jax.sharding import Mesh, PartitionSpec as P

SQRT_HALF = 0.7071067811865476
INV_ROOT_TAU = 0.3989422804014327
N_Y = 4
N_CORE = 2
F32 = jnp.float32
BF16 = jnp.bfloat16
NT = (((1,), (1,)), ((), ()))
NN = (((1,), (0,)), ((), ()))
TN = (((0,), (0,)), ((), ()))
VMEM = pl.BlockSpec(memory_space=pltpu.VMEM)
SMEM = pl.BlockSpec(memory_space=pltpu.SMEM)


def dot(a, b, dims):
    return lax.dot_general(a, b, dims, preferred_element_type=F32)


def iota(shape, axis):
    return lax.broadcasted_iota(jnp.int32, shape, axis)


def cost(flops, bytes_accessed, transcendentals=0):
    return pl.CostEstimate(flops=flops, bytes_accessed=bytes_accessed, transcendentals=transcendentals)


def ids_kernel(req_ref, out_ref):
    capacity, owners = req_ref.shape
    slots = out_ref.shape[0]
    row = iota((slots, owners), 0)
    lane = iota((slots, owners), 1)
    per_peer = N_Y * capacity
    peer = row // per_peer
    owner = (peer // N_CORE) * (N_Y * N_CORE) + ((row % per_peer) // capacity) * N_CORE + peer % N_CORE
    total = jnp.zeros((slots, 1), jnp.int32)
    for r in range(capacity):
        hit = (lane == owner) & (row % capacity == r)
        picked = jnp.where(hit, req_ref[r : r + 1, :], 0)
        total = total + jnp.sum(picked, axis=1, keepdims=True)
    out_ref[...] = jnp.broadcast_to(total, out_ref.shape)


def expand_ids(wanted):
    owners, capacity = wanted.shape
    slots = owners * capacity
    return pl.pallas_call(
        ids_kernel,
        out_shape=jax.ShapeDtypeStruct((slots, 128), jnp.int32),
        in_specs=[VMEM],
        out_specs=VMEM,
        cost_estimate=cost(10**5, 10**5),
        name="ids",
    )(jnp.transpose(wanted))


def gather_kernel(y_ref, asked_ref, t0, t1, t2, t3, out_ref):
    y = y_ref[0]
    slots = asked_ref.shape[0]
    rows = t0.shape[0]
    col = iota((slots, rows), 1)
    owner_y = (iota((slots, rows), 0) % (N_Y * 2)) // 2
    same = asked_ref[:, :rows] == col
    total = jnp.zeros(out_ref.shape, F32)
    for r, table in enumerate((t0, t1, t2, t3)):
        hit = same & (owner_y == (y + r) % N_Y)
        total = total + dot(hit.astype(F32).astype(BF16), table[...], NN)
    out_ref[...] = total.astype(BF16)


def gather_rows(y, asked, tables, name):
    slots = asked.shape[0]
    width = tables[0].shape[1]
    return pl.pallas_call(
        gather_kernel,
        out_shape=jax.ShapeDtypeStruct((slots, width), BF16),
        in_specs=[SMEM] + [VMEM] * 5,
        out_specs=VMEM,
        cost_estimate=cost(2 * 256 * 256 * 2048, 3 * 10**6),
        name=name,
    )(y, asked, *tables)


def weight_kernel(places_ref, gates_ref, out_ref):
    topk, block = places_ref.shape
    slots = out_ref.shape[0]
    slot = places_ref[...]
    slot = (slot & ~15) | (((slot >> 1) & 1) << 3) | (((slot >> 2) & 3) << 1) | (slot & 1)
    gates = gates_ref[...]
    for s in range(0, slots, 32):
        row = iota((32, block), 0) + s
        total = jnp.zeros((32, block), F32)
        for k in range(topk):
            total = jnp.where(row == slot[k : k + 1, :], gates[k : k + 1, :], total)
        out_ref[s : s + 32, :] = total


def build_weight(places, gates, slots):
    topk, tokens = places.shape
    block = 512
    return pl.pallas_call(
        weight_kernel,
        grid=(tokens // block,),
        out_shape=jax.ShapeDtypeStruct((slots, tokens), F32),
        in_specs=[pl.BlockSpec((topk, block), lambda i: (0, i))] * 2,
        out_specs=pl.BlockSpec((slots, block), lambda i: (0, i)),
        cost_estimate=cost(3 * topk * slots * tokens, 4 * slots * tokens),
        name="weight",
    )(places, gates)


def first_kernel(tok_ref, grad_ref, down_ref, weight_ref, slope_ref, part_ref, acc):
    i = pl.program_id(0)

    @pl.when(i == 0)
    def _():
        acc[...] = jnp.zeros_like(acc)

    pre = dot(down_ref[...], tok_ref[...], NT)
    weight = weight_ref[...]
    cdf = 0.5 * (1.0 + lax.erf(pre * SQRT_HALF))
    density = INV_ROOT_TAU * jnp.exp(-0.5 * pre * pre)
    gated = (weight * (pre * cdf)).astype(BF16)
    slope_ref[...] = weight * (cdf + pre * density)
    acc[...] += dot(gated, grad_ref[...], NN)

    @pl.when(i == pl.num_programs(0) - 1)
    def _():
        part_ref[...] = acc[...].astype(BF16)


def first_terms(tokens, grads, down, weight):
    count, width = tokens.shape
    slots = down.shape[0]
    block = 256
    return pl.pallas_call(
        first_kernel,
        grid=(count // block,),
        out_shape=(
            jax.ShapeDtypeStruct((slots, count), F32),
            jax.ShapeDtypeStruct((slots, width), BF16),
        ),
        in_specs=[
            pl.BlockSpec((block, width), lambda i: (i, 0)),
            pl.BlockSpec((block, width), lambda i: (i, 0)),
            pl.BlockSpec((slots, width), lambda i: (0, 0)),
            pl.BlockSpec((slots, block), lambda i: (0, i)),
        ],
        out_specs=(
            pl.BlockSpec((slots, block), lambda i: (0, i)),
            pl.BlockSpec((slots, width), lambda i: (0, 0)),
        ),
        scratch_shapes=[pltpu.VMEM((slots, width), F32)],
        compiler_params=pltpu.CompilerParams(vmem_limit_bytes=32 << 20),
        cost_estimate=cost(4 * count * width * slots, 20 << 20),
        name="first",
    )(tokens, grads, down, weight)


def second_kernel(tok_ref, grad_ref, up_ref, slope_ref, coef_ref, part_ref, acc):
    i = pl.program_id(0)

    @pl.when(i == 0)
    def _():
        acc[...] = jnp.zeros_like(acc)

    back = dot(up_ref[...], grad_ref[...], NT)
    coef = (slope_ref[...] * back).astype(BF16)
    coef_ref[0] = coef
    acc[...] += dot(coef, tok_ref[...], NN)

    @pl.when(i == pl.num_programs(0) - 1)
    def _():
        part_ref[...] = acc[...].astype(BF16)


def second_terms(tokens, grads, up, slope):
    count, width = tokens.shape
    slots = up.shape[0]
    block = 256
    per_chip = count // N_Y // block
    return pl.pallas_call(
        second_kernel,
        grid=(count // block,),
        out_shape=(
            jax.ShapeDtypeStruct((N_Y, slots, count // N_Y), BF16),
            jax.ShapeDtypeStruct((slots, width), BF16),
        ),
        in_specs=[
            pl.BlockSpec((block, width), lambda i: (i, 0)),
            pl.BlockSpec((block, width), lambda i: (i, 0)),
            pl.BlockSpec((slots, width), lambda i: (0, 0)),
            pl.BlockSpec((slots, block), lambda i: (0, i)),
        ],
        out_specs=(
            pl.BlockSpec((1, slots, block), lambda i: (i // per_chip, 0, i % per_chip)),
            pl.BlockSpec((slots, width), lambda i: (0, 0)),
        ),
        scratch_shapes=[pltpu.VMEM((slots, width), F32)],
        compiler_params=pltpu.CompilerParams(vmem_limit_bytes=32 << 20),
        cost_estimate=cost(4 * count * width * slots, 20 << 20),
        name="second",
    )(tokens, grads, up, slope)


def scatter_kernel(asked_ref, got_ref, out_ref):
    slots = asked_ref.shape[0]
    rows = out_ref.shape[1]
    col = iota((slots, rows), 1)
    owner_y = (iota((slots, rows), 0) % (N_Y * 2)) // 2
    same = asked_ref[:, :rows] == col
    for y in range(N_Y):
        hit = (same & (owner_y == y)).astype(F32).astype(BF16)
        out_ref[y] = dot(hit, got_ref[...], TN).astype(BF16)


def scatter_rows(asked, got, rows, name):
    width = got.shape[1]
    return pl.pallas_call(
        scatter_kernel,
        out_shape=jax.ShapeDtypeStruct((N_Y, rows, width), BF16),
        in_specs=[VMEM] * 2,
        out_specs=VMEM,
        cost_estimate=cost(2 * 256 * 256 * 2048, 2 * 10**6),
        name=name,
    )(asked, got)


def final_kernel(pos_ref, coef_ref, d0, d1, d2, d3, keep_ref, give_ref):
    y = pos_ref[0]
    core = pos_ref[1]
    half = keep_ref.shape[0]

    def product(which):
        total = jnp.zeros(keep_ref.shape, F32)
        for r, rows in enumerate((d0, d1, d2, d3)):
            block = coef_ref[(y + r) % N_Y, :, pl.ds(pl.multiple_of(which * half, half), half)]
            total = total + dot(block, rows[...], TN)
        return total

    give_ref[...] = product(1 - core).astype(BF16)
    keep_ref[...] = product(core)


def final_product(pos, coef, rows):
    slots, width = rows[0].shape
    half = coef.shape[2] // N_CORE
    block = 512
    return pl.pallas_call(
        final_kernel,
        grid=(width // block,),
        out_shape=(
            jax.ShapeDtypeStruct((half, width), F32),
            jax.ShapeDtypeStruct((half, width), BF16),
        ),
        in_specs=[SMEM, pl.BlockSpec(coef.shape, lambda j: (0, 0, 0))]
        + [pl.BlockSpec((slots, block), lambda j: (0, j))] * 4,
        out_specs=(
            pl.BlockSpec((half, block), lambda j: (0, j)),
            pl.BlockSpec((half, block), lambda j: (0, j)),
        ),
        cost_estimate=cost(2 * 512 * 1024 * 2048, 8 << 20),
        name="final",
    )(pos, coef, *rows)


def around(x):
    return (x,) + tuple(
        lax.ppermute(x, "y", [(i, (i - r) % N_Y) for i in range(N_Y)]) for r in range(1, N_Y)
    )


def exchange(x):
    return lax.all_to_all(x, ("dp", "core"), split_axis=0, concat_axis=0, tiled=True)


def shards(tokens, out_grad, down_rows, up_rows, requests, places, gate_weights):
    peers = lax.axis_size("dp") * N_CORE
    row_count, width = down_rows.shape
    y = lax.axis_index("y").astype(jnp.int32)
    core = lax.axis_index("core").astype(jnp.int32)
    y_at = jnp.stack([y])
    pos = jnp.stack([y, core])

    down_tables = around(down_rows)
    up_tables = around(up_rows)
    ids = expand_ids(requests[0])
    slots = ids.shape[0]
    per_peer = slots // peers
    asked = exchange(ids.reshape(peers, per_peer, 128)).reshape(slots, 128)

    def fetch(tables, name):
        rows = gather_rows(y_at, asked, tables, name)
        return exchange(rows.reshape(peers, per_peer, width)).reshape(slots, width)

    down = fetch(down_tables, "gather_down")
    up = fetch(up_tables, "gather_up")
    weight = build_weight(jnp.transpose(places[0]), jnp.transpose(gate_weights[0]), slots)
    down_all = around(down)
    slope, part_up = first_terms(tokens, out_grad, down, weight)
    coef, part_down = second_terms(tokens, out_grad, up, slope)

    def give_back(part, name):
        got = exchange(part.reshape(peers, per_peer, width)).reshape(slots, width)
        sums = scatter_rows(asked, got, row_count, name)
        shared = lax.all_to_all(sums, "y", split_axis=0, concat_axis=0, tiled=True)
        return jnp.sum(shared.astype(F32), axis=0)

    up_grad = give_back(part_up, "scatter_up")
    down_grad = give_back(part_down, "scatter_down")
    coef_all = lax.all_to_all(coef, "y", split_axis=0, concat_axis=0, tiled=True)
    keep, give = final_product(pos, coef_all, down_all)
    other = lax.ppermute(give, "core", [(0, 1), (1, 0)])
    input_grad = (keep + other.astype(F32)).astype(BF16)
    return (input_grad, down_grad, up_grad)


def solution(mesh):
    axes = ("dp", "y", "core")
    fine = Mesh(mesh.devices.reshape(mesh.devices.shape[0], N_Y, N_CORE), axes)
    in_specs = (
        P("dp", None),
        P("dp", None),
        P(axes, None),
        P(axes, None),
        P(axes, None, None),
        P(("y", "core"), "dp", None),
        P(("y", "core"), "dp", None),
    )
    out_specs = (P(axes, None), P(axes, None), P(axes, None))
    return jax.shard_map(shards, mesh=fine, in_specs=in_specs, out_specs=out_specs, check_vma=False)
```

```python
import functools
import jax
import jax.numpy as jnp
from jax import lax
from jax.experimental import pallas as pl
from jax.experimental.pallas import tpu as pltpu
from jax.sharding import Mesh, PartitionSpec as P

SQRT_HALF = 0.7071067811865476
INV_ROOT_TAU = 0.3989422804014327
N_Y = 4
N_CORE = 2
F32 = jnp.float32
BF16 = jnp.bfloat16
NT = (((1,), (1,)), ((), ()))
NN = (((1,), (0,)), ((), ()))
TN = (((0,), (0,)), ((), ()))
ANY = pl.BlockSpec(memory_space=pl.ANY)
VMEM = pl.BlockSpec(memory_space=pltpu.VMEM)
DMA = pltpu.SemaphoreType.DMA


def dot(a, b, dims):
    return lax.dot_general(a, b, dims, preferred_element_type=F32)


def iota(shape, axis):
    return lax.broadcasted_iota(jnp.int32, shape, axis)


def cost(flops, bytes_accessed, transcendentals=0):
    return pl.CostEstimate(flops=flops, bytes_accessed=bytes_accessed, transcendentals=transcendentals)


def ids_kernel(req_ref, out_ref):
    capacity, owners = req_ref.shape
    slots = out_ref.shape[0]
    row = iota((slots, owners), 0)
    lane = iota((slots, owners), 1)
    per_peer = N_Y * capacity
    peer = row // per_peer
    owner = (peer // N_CORE) * (N_Y * N_CORE) + ((row % per_peer) // capacity) * N_CORE + peer % N_CORE
    total = jnp.zeros((slots, 1), jnp.int32)
    for r in range(capacity):
        hit = (lane == owner) & (row % capacity == r)
        picked = jnp.where(hit, req_ref[r : r + 1, :], 0)
        total = total + jnp.sum(picked, axis=1, keepdims=True)
    out_ref[...] = jnp.broadcast_to(total, out_ref.shape)


def expand_ids(wanted):
    owners, capacity = wanted.shape
    slots = owners * capacity
    return pl.pallas_call(
        ids_kernel,
        out_shape=jax.ShapeDtypeStruct((slots, 128), jnp.int32),
        in_specs=[VMEM],
        out_specs=VMEM,
        cost_estimate=cost(10**5, 10**5),
        name="ids",
    )(jnp.transpose(wanted))


def copy(src, dst, sem):
    return pltpu.make_async_copy(src, dst, sem)


def params(mib):
    return pltpu.CompilerParams(vmem_limit_bytes=mib << 20)


def column_hits(asked, rows):
    y = lax.axis_index("y")
    slots = asked.shape[0]
    shape = (slots, N_Y * rows)
    at = iota(shape, 1)
    owner_y = (iota(shape, 0) % (N_Y * 2)) // 2
    twice = jnp.concatenate([asked] * (N_Y * rows // asked.shape[1]), axis=1)
    hit = (twice == at % rows) & (owner_y == (y + at // rows) % N_Y)
    return hit.astype(F32).astype(BF16)


def gather_kernel(asked_ref, t0, t1, t2, t3, out_hbm, table, out, sems, out_sems):
    rows = t0.shape[0]
    copies = [
        copy(t, table.at[pl.ds(r * rows, rows), :], sems.at[r]) for r, t in enumerate((t0, t1, t2, t3))
    ]
    for c in copies:
        c.start()
    hits = column_hits(asked_ref[...], rows)
    for c in copies:
        c.wait()
    width = out.shape[1]
    block = width // 4
    sent = []
    for j in range(4):
        cols = pl.ds(j * block, block)
        out[:, cols] = dot(hits, table[:, cols], NN).astype(BF16)
        c = copy(out.at[:, cols], out_hbm.at[:, cols], out_sems.at[j])
        c.start()
        sent.append(c)
    for c in sent:
        c.wait()


def gather_rows(asked, tables):
    slots = asked.shape[0]
    rows, width = tables[0].shape
    return pl.pallas_call(
        gather_kernel,
        out_shape=jax.ShapeDtypeStruct((slots, width), BF16),
        in_specs=[VMEM] + [ANY] * 4,
        out_specs=ANY,
        scratch_shapes=[
            pltpu.VMEM((N_Y * rows, width), BF16),
            pltpu.VMEM((slots, width), BF16),
            DMA((4,)),
            DMA((4,)),
        ],
        compiler_params=params(8),
        cost_estimate=cost(2 * 256 * 256 * 2048, 3 * 10**6),
    )(asked, *tables)


def weight_kernel(places_ref, gates_ref, out_ref):
    topk, block = places_ref.shape
    slots = out_ref.shape[1]
    slot = places_ref[...]
    slot = (slot & ~15) | (((slot >> 1) & 1) << 3) | (((slot >> 2) & 3) << 1) | (slot & 1)
    gates = gates_ref[...]
    for s in range(0, slots, 32):
        row = iota((32, block), 0) + s
        total = jnp.zeros((32, block), F32)
        for k in range(topk):
            total = jnp.where(row == slot[k : k + 1, :], gates[k : k + 1, :], total)
        out_ref[0, s : s + 32, :] = total


def build_weight(places, gates, slots):
    topk, tokens = places.shape
    block = tokens // N_Y
    return pl.pallas_call(
        weight_kernel,
        grid=(N_Y,),
        out_shape=jax.ShapeDtypeStruct((N_Y, slots, block), F32),
        in_specs=[pl.BlockSpec((topk, block), lambda i: (0, i))] * 2,
        out_specs=pl.BlockSpec((1, slots, block), lambda i: (i, 0, 0)),
        compiler_params=params(8),
        cost_estimate=cost(3 * topk * slots * tokens, 4 * slots * tokens),
        name="weight",
    )(places, gates)


def load_rows(src, dst, sems, pieces):
    rows = src.shape[0] // pieces
    return [
        copy(src.at[pl.ds(i * rows, rows), :], dst.at[pl.ds(i * rows, rows), :], sems.at[i])
        for i in range(pieces)
    ]


def part_columns(left, right, part, part_hbm, sems):
    width = part.shape[1]
    block = width // N_Y
    sent = []
    for j in range(N_Y):
        cols = pl.ds(j * block, block)
        part[:, cols] = dot(left[...], right[:, cols], NN).astype(BF16)
        c = copy(part.at[:, cols], part_hbm.at[:, cols], sems.at[j])
        c.start()
        sent.append(c)
    return sent


def first_kernel(
    tok_hbm, grad_hbm, down_hbm, weight_hbm, slope_hbm, part_hbm,
    tok, grad, down, weight, slope, gated, part,
    tok_sems, grad_sems, down_sem, weight_sems, slope_sems, part_sems,
):
    block = weight.shape[2]
    down_in = copy(down_hbm, down, down_sem)
    weight_in = [copy(weight_hbm.at[c], weight.at[c], weight_sems.at[c]) for c in range(N_Y)]
    tok_in = load_rows(tok_hbm, tok, tok_sems, 8)
    grad_in = load_rows(grad_hbm, grad, grad_sems, 8)
    down_in.start()
    for c in range(N_Y):
        tok_in[2 * c].start()
        tok_in[2 * c + 1].start()
        weight_in[c].start()
    for g in grad_in:
        g.start()
    down_in.wait()
    sent = []
    for c in range(N_Y):
        tok_in[2 * c].wait()
        tok_in[2 * c + 1].wait()
        pre = dot(down[...], tok[pl.ds(c * block, block), :], NT)
        weight_in[c].wait()
        here = weight[c]
        cdf = 0.5 * (1.0 + lax.erf(pre * SQRT_HALF))
        density = INV_ROOT_TAU * jnp.exp(-0.5 * pre * pre)
        gated[:, pl.ds(c * block, block)] = (here * (pre * cdf)).astype(BF16)
        slope[c] = here * (cdf + pre * density)
        out = copy(slope.at[c], slope_hbm.at[c], slope_sems.at[c])
        out.start()
        sent.append(out)
    for g in grad_in:
        g.wait()
    sent += part_columns(gated, grad, part, part_hbm, part_sems)
    for s in sent:
        s.wait()


def first_terms(tokens, grads, down, weight):
    count, width = tokens.shape
    slots = down.shape[0]
    return pl.pallas_call(
        first_kernel,
        out_shape=(
            jax.ShapeDtypeStruct(weight.shape, F32),
            jax.ShapeDtypeStruct((slots, width), BF16),
        ),
        in_specs=[ANY] * 4,
        out_specs=(ANY, ANY),
        scratch_shapes=[
            pltpu.VMEM((count, width), BF16),
            pltpu.VMEM((count, width), BF16),
            pltpu.VMEM((slots, width), BF16),
            pltpu.VMEM(weight.shape, F32),
            pltpu.VMEM(weight.shape, F32),
            pltpu.VMEM((slots, count), BF16),
            pltpu.VMEM((slots, width), BF16),
            DMA((8,)), DMA((8,)), DMA, DMA((4,)), DMA((4,)), DMA((4,)),
        ],
        compiler_params=params(56),
        cost_estimate=cost(4 * count * width * slots, 20 << 20),
        name="first",
    )(tokens, grads, down, weight)


def second_kernel(
    tok_hbm, grad_hbm, up_hbm, slope_hbm, c0, c1, c2, c3, part_hbm,
    tok, grad, up, slope, coef, part,
    tok_sems, grad_sems, up_sem, slope_sems, coef_sems, part_sems,
):
    block = slope.shape[2]
    y = lax.axis_index("y")
    up_in = copy(up_hbm, up, up_sem)
    slope_in = [copy(slope_hbm.at[c], slope.at[c], slope_sems.at[c]) for c in range(N_Y)]
    grad_in = load_rows(grad_hbm, grad, grad_sems, 8)
    tok_in = load_rows(tok_hbm, tok, tok_sems, 8)
    up_in.start()
    for c in range(N_Y):
        grad_in[2 * c].start()
        grad_in[2 * c + 1].start()
        slope_in[c].start()
    for t in tok_in:
        t.start()
    up_in.wait()
    for c in range(N_Y):
        grad_in[2 * c].wait()
        grad_in[2 * c + 1].wait()
        back = dot(up[...], grad[pl.ds(c * block, block), :], NT)
        slope_in[c].wait()
        coef[:, pl.ds(c * block, block)] = (slope[c] * back).astype(BF16)
    sent = []
    for r, out in enumerate((c0, c1, c2, c3)):
        start = pl.multiple_of(((y + r) % N_Y) * block, block)
        c = copy(coef.at[:, pl.ds(start, block)], out, coef_sems.at[r])
        c.start()
        sent.append(c)
    for t in tok_in:
        t.wait()
    sent += part_columns(coef, tok, part, part_hbm, part_sems)
    for s in sent:
        s.wait()


def second_terms(tokens, grads, up, slope):
    count, width = tokens.shape
    slots = up.shape[0]
    return pl.pallas_call(
        second_kernel,
        out_shape=tuple(jax.ShapeDtypeStruct((slots, count // N_Y), BF16) for _ in range(N_Y))
        + (jax.ShapeDtypeStruct((slots, width), BF16),),
        in_specs=[ANY] * 4,
        out_specs=(ANY,) * 5,
        scratch_shapes=[
            pltpu.VMEM((count, width), BF16),
            pltpu.VMEM((count, width), BF16),
            pltpu.VMEM((slots, width), BF16),
            pltpu.VMEM(slope.shape, F32),
            pltpu.VMEM((slots, count), BF16),
            pltpu.VMEM((slots, width), BF16),
            DMA((8,)), DMA((8,)), DMA, DMA((4,)), DMA((4,)), DMA((4,)),
        ],
        compiler_params=params(56),
        cost_estimate=cost(4 * count * width * slots, 20 << 20),
        name="second",
    )(tokens, grads, up, slope)


def scatter_kernel(asked_ref, got_hbm, o0, o1, o2, o3, got, sums, sems, out_sems):
    rows = o0.shape[0]
    width = got.shape[1]
    block = width // 4
    copies = [
        copy(got_hbm.at[:, pl.ds(j * block, block)], got.at[:, pl.ds(j * block, block)], sems.at[j])
        for j in range(4)
    ]
    for c in copies:
        c.start()
    hits = column_hits(asked_ref[...], rows)
    for j in range(4):
        copies[j].wait()
        cols = pl.ds(j * block, block)
        sums[:, cols] = dot(hits, got[:, cols], TN).astype(BF16)
    sent = []
    for r, out in enumerate((o0, o1, o2, o3)):
        c = copy(sums.at[pl.ds(r * rows, rows), :], out, out_sems.at[r])
        c.start()
        sent.append(c)
    for c in sent:
        c.wait()


def scatter_rows(asked, got, rows):
    slots, width = got.shape
    return pl.pallas_call(
        scatter_kernel,
        out_shape=tuple(jax.ShapeDtypeStruct((rows, width), BF16) for _ in range(N_Y)),
        in_specs=[VMEM, ANY],
        out_specs=(ANY,) * N_Y,
        scratch_shapes=[
            pltpu.VMEM((slots, width), BF16),
            pltpu.VMEM((N_Y * rows, width), BF16),
            DMA((4,)),
            DMA((4,)),
        ],
        compiler_params=params(8),
        cost_estimate=cost(2 * 256 * 256 * 2048, 2 * 10**6),
    )(asked, got)


def final_kernel(mine, c0, c1, c2, c3, d0, d1, d2, d3, out_hbm, coef, rows, out, c_sems, d_sems, out_sems):
    core = lax.axis_index("core")
    which = core if mine else 1 - core
    slots = c0.shape[0]
    half = out.shape[0]
    loads = []
    for r in range(N_Y):
        cols = pl.ds(pl.multiple_of(which * half, half), half)
        place = pl.ds(r * slots, slots)
        loads.append(copy((c0, c1, c2, c3)[r].at[:, cols], coef.at[place, :], c_sems.at[r]))
        loads.append(copy((d0, d1, d2, d3)[r], rows.at[place, :], d_sems.at[r]))
    for c in loads:
        c.start()
    for c in loads:
        c.wait()
    width = out.shape[1]
    block = width // 4
    sent = []
    for j in range(4):
        cols = pl.ds(j * block, block)
        out[:, cols] = dot(coef[...], rows[:, cols], TN).astype(BF16)
        c = copy(out.at[:, cols], out_hbm.at[:, cols], out_sems.at[j])
        c.start()
        sent.append(c)
    for c in sent:
        c.wait()


def final_product(mine, coef, rows):
    slots, width = rows[0].shape
    half = coef[0].shape[1] // N_CORE
    return pl.pallas_call(
        functools.partial(final_kernel, mine),
        out_shape=jax.ShapeDtypeStruct((half, width), BF16),
        in_specs=[ANY] * 8,
        out_specs=ANY,
        scratch_shapes=[
            pltpu.VMEM((N_Y * slots, half), BF16),
            pltpu.VMEM((N_Y * slots, width), BF16),
            pltpu.VMEM((half, width), BF16),
            DMA((4,)), DMA((4,)), DMA((4,)),
        ],
        compiler_params=params(16),
        cost_estimate=cost(2 * half * 1024 * 2048, 6 << 20),
        name="keep" if mine else "give",
    )(*coef, *rows)


def turn(x, r):
    return lax.ppermute(x, "y", [(i, (i - r) % N_Y) for i in range(N_Y)])


def around(x):
    return (x,) + tuple(turn(x, r) for r in range(1, N_Y))


def exchange(x):
    return lax.all_to_all(x, ("dp", "core"), split_axis=0, concat_axis=0, tiled=True)


def program(tokens, out_grad, down_rows, up_rows, requests, places, gate_weights):
    peers = lax.axis_size("dp") * N_CORE
    row_count, width = down_rows.shape

    down_tables = around(down_rows)
    ids = expand_ids(requests[0])
    slots = ids.shape[0]
    per_peer = slots // peers
    asked = exchange(ids.reshape(peers, per_peer, 128)).reshape(slots, 128)
    up_tables = around(up_rows)
    weight = build_weight(jnp.transpose(places[0]), jnp.transpose(gate_weights[0]), slots)

    def fetch(tables):
        rows = gather_rows(asked, tables)
        return exchange(rows.reshape(peers, per_peer, width)).reshape(slots, width)

    down = fetch(down_tables)
    up = fetch(up_tables)
    down_all = around(down)
    slope, part_up = first_terms(tokens, out_grad, down, weight)
    *coef, part_down = second_terms(tokens, out_grad, up, slope)

    def give_back(part):
        return exchange(part.reshape(peers, per_peer, width)).reshape(slots, width)

    got_up = give_back(part_up)
    got_down = give_back(part_down)
    coef_in = (coef[0],) + tuple(turn(coef[(N_Y - r) % N_Y], r) for r in range(1, N_Y))

    def total(got):
        sums = scatter_rows(asked, got, row_count)
        found = [sums[0]] + [turn(sums[N_Y - r], r) for r in range(1, N_Y)]
        return sum(f.astype(F32) for f in found)

    up_grad = total(got_up)
    give = final_product(False, coef_in, down_all)
    other = lax.ppermute(give, "core", [(0, 1), (1, 0)])
    keep = final_product(True, coef_in, down_all)
    input_grad = (keep.astype(F32) + other.astype(F32)).astype(BF16)
    down_grad = total(got_down)
    return (input_grad, down_grad, up_grad)


def solution(mesh):
    axes = ("dp", "y", "core")
    fine = Mesh(mesh.devices.reshape(mesh.devices.shape[0], N_Y, N_CORE), axes)
    in_specs = (
        P("dp", None),
        P("dp", None),
        P(axes, None),
        P(axes, None),
        P(axes, None, None),
        P(("y", "core"), "dp", None),
        P(("y", "core"), "dp", None),
    )
    out_specs = (P(axes, None), P(axes, None), P(axes, None))
    return jax.shard_map(program, mesh=fine, in_specs=in_specs, out_specs=out_specs, check_vma=False)
```

```python
import functools
import jax
import jax.numpy as jnp
from jax import lax
from jax.experimental import pallas as pl
from jax.experimental.pallas import tpu as pltpu
from jax.sharding import Mesh, PartitionSpec as P

SQRT_HALF = 0.7071067811865476
INV_ROOT_TAU = 0.3989422804014327
N_Y = 4
N_CORE = 2
F32 = jnp.float32
BF16 = jnp.bfloat16
NT = (((1,), (1,)), ((), ()))
NN = (((1,), (0,)), ((), ()))
TN = (((0,), (0,)), ((), ()))
ANY = pl.BlockSpec(memory_space=pl.ANY)
VMEM = pl.BlockSpec(memory_space=pltpu.VMEM)
DMA = pltpu.SemaphoreType.DMA


def dot(a, b, dims):
    return lax.dot_general(a, b, dims, preferred_element_type=F32)


def iota(shape, axis):
    return lax.broadcasted_iota(jnp.int32, shape, axis)


def cost(flops, bytes_accessed, transcendentals=0):
    return pl.CostEstimate(flops=flops, bytes_accessed=bytes_accessed, transcendentals=transcendentals)


def copy(src, dst, sem):
    return pltpu.make_async_copy(src, dst, sem)


def params(mib):
    return pltpu.CompilerParams(vmem_limit_bytes=mib << 20)


def load_rows(src, dst, sems, pieces):
    rows = src.shape[0] // pieces
    return [
        copy(src.at[pl.ds(i * rows, rows), :], dst.at[pl.ds(i * rows, rows), :], sems.at[i])
        for i in range(pieces)
    ]


def ids_kernel(req_ref, out_ref):
    capacity, owners = req_ref.shape
    row = iota((owners, owners), 0)
    lane = iota((owners, owners), 1)
    total = jnp.zeros(out_ref.shape, jnp.int32)
    at = iota(out_ref.shape, 1)
    for r in range(capacity):
        picked = jnp.where(lane == row, req_ref[r : r + 1, :], 0)
        column = jnp.sum(picked, axis=1, keepdims=True)
        total = jnp.where(at == r, column, total)
    out_ref[...] = total


def turn_ids(wanted):
    owners, _ = wanted.shape
    return pl.pallas_call(
        ids_kernel,
        out_shape=jax.ShapeDtypeStruct((owners, 128), jnp.int32),
        in_specs=[VMEM],
        out_specs=VMEM,
        cost_estimate=cost(10**5, 10**5),
        name="ids",
    )(jnp.transpose(wanted))


def asked_hits(asked, capacity, rows):
    devices = asked.shape[0]
    slots = devices * capacity
    at = iota((devices, rows), 1)
    place = iota((slots, devices), 0)
    device = iota((slots, devices), 1)
    total = jnp.zeros((slots, rows), F32)
    for r in range(capacity):
        hit = (asked[:, r : r + 1] == at).astype(F32).astype(BF16)
        spread = (place == device * capacity + r).astype(F32).astype(BF16)
        total = total + dot(spread, hit, NN)
    return total.astype(BF16)


def gather_kernel(capacity, asked_ref, down_ref, up_ref, out_hbm, out, out_sems):
    hits = asked_hits(asked_ref[...], capacity, down_ref.shape[0])
    block = 1024
    per_table = down_ref.shape[1] // block
    sent = []
    for j in range(2 * per_table):
        table = (down_ref, up_ref)[j // per_table]
        cols = pl.ds(j * block, block)
        out[:, cols] = dot(hits, table[:, pl.ds(j % per_table * block, block)], NN).astype(BF16)
        c = copy(out.at[:, cols], out_hbm.at[:, cols], out_sems.at[j])
        c.start()
        sent.append(c)
    for c in sent:
        c.wait()


def gather_rows(asked, capacity, down_rows, up_rows):
    slots = asked.shape[0] * capacity
    width = down_rows.shape[1]
    return pl.pallas_call(
        functools.partial(gather_kernel, capacity),
        out_shape=jax.ShapeDtypeStruct((slots, 2 * width), BF16),
        in_specs=[VMEM] * 3,
        out_specs=ANY,
        scratch_shapes=[pltpu.VMEM((slots, 2 * width), BF16), DMA((4,))],
        compiler_params=params(8),
        cost_estimate=cost(2 * 256 * 256 * 2048, 3 * 10**6),
        name="gather",
    )(asked, down_rows, up_rows)


def weight_kernel(places_ref, gates_ref, out_ref):
    topk, block = places_ref.shape
    slots = out_ref.shape[1]
    slot = places_ref[...]
    gates = gates_ref[...]
    for s in range(0, slots, 32):
        row = iota((32, block), 0) + s
        total = jnp.zeros((32, block), F32)
        for k in range(topk):
            total = jnp.where(row == slot[k : k + 1, :], gates[k : k + 1, :], total)
        out_ref[0, s : s + 32, :] = total


def build_weight(places, gates, slots):
    topk, tokens = places.shape
    block = tokens // N_Y
    return pl.pallas_call(
        weight_kernel,
        grid=(N_Y,),
        out_shape=jax.ShapeDtypeStruct((N_Y, slots, block), F32),
        in_specs=[pl.BlockSpec((topk, block), lambda i: (0, i))] * 2,
        out_specs=pl.BlockSpec((1, slots, block), lambda i: (i, 0, 0)),
        compiler_params=params(8),
        cost_estimate=cost(3 * topk * slots * tokens, 4 * slots * tokens),
        name="weight",
    )(places, gates)


def local_kernel(
    tok_hbm, grad_hbm, down_hbm, up_hbm, weight_hbm, places_ref, c0, c1, c2, c3, part_hbm,
    tok, grad, down, up, weight, gated, coef, small, part,
    tok_sems, grad_sems, row_sems, weight_sems, small_sems, part_sems,
):
    block = weight.shape[2]
    topk = places_ref.shape[0]
    slots, width = down.shape
    y = lax.axis_index("y")
    down_in = copy(down_hbm, down, row_sems.at[0])
    up_in = copy(up_hbm, up, row_sems.at[1])
    weight_in = [copy(weight_hbm.at[c], weight.at[c], weight_sems.at[c]) for c in range(N_Y)]
    tok_in = load_rows(tok_hbm, tok, tok_sems, 8)
    grad_in = load_rows(grad_hbm, grad, grad_sems, 8)
    down_in.start()
    for c in range(N_Y):
        tok_in[2 * c].start()
        tok_in[2 * c + 1].start()
        if c == 0:
            up_in.start()
        grad_in[2 * c].start()
        grad_in[2 * c + 1].start()
        weight_in[c].start()
    down_in.wait()
    for c in range(N_Y):
        here = pl.ds(c * block, block)
        tok_in[2 * c].wait()
        tok_in[2 * c + 1].wait()
        pre = dot(down[...], tok[here, :], NT)
        if c == 0:
            up_in.wait()
        grad_in[2 * c].wait()
        grad_in[2 * c + 1].wait()
        back = dot(up[...], grad[here, :], NT)
        weight_in[c].wait()
        gate = weight[c]
        cdf = 0.5 * (1.0 + lax.erf(pre * SQRT_HALF))
        density = INV_ROOT_TAU * jnp.exp(-0.5 * pre * pre)
        gated[:, here] = (gate * (pre * cdf)).astype(BF16)
        product = gate * (cdf + pre * density) * back
        coef[:, here] = product.astype(BF16)
        slot = places_ref[:, here]
        lines = []
        for k in range(topk):
            hit = iota((slots, block), 0) == slot[k : k + 1, :]
            lines.append(jnp.sum(jnp.where(hit, product, 0.0), axis=0, keepdims=True))
        small[c] = jnp.concatenate(lines, axis=0).astype(BF16)
    sent = []
    for r, out in enumerate((c0, c1, c2, c3)):
        c = copy(small.at[(y + r) % N_Y], out, small_sems.at[r])
        c.start()
        sent.append(c)
    step = width // N_Y
    for j in range(2 * N_Y):
        left, right = ((coef, tok), (gated, grad))[j // N_Y]
        cols = pl.ds(j * step, step)
        part[:, cols] = dot(left[...], right[:, pl.ds(j % N_Y * step, step)], NN).astype(BF16)
        c = copy(part.at[:, cols], part_hbm.at[:, cols], part_sems.at[j])
        c.start()
        sent.append(c)
    for s in sent:
        s.wait()


def local_terms(tokens, grads, down, up, weight, places):
    count, width = tokens.shape
    slots = down.shape[0]
    topk = places.shape[0]
    block = count // N_Y
    return pl.pallas_call(
        local_kernel,
        out_shape=tuple(jax.ShapeDtypeStruct((topk, block), BF16) for _ in range(N_Y))
        + (jax.ShapeDtypeStruct((slots, 2 * width), BF16),),
        in_specs=[ANY] * 5 + [VMEM],
        out_specs=(ANY,) * 5,
        scratch_shapes=[
            pltpu.VMEM((count, width), BF16),
            pltpu.VMEM((count, width), BF16),
            pltpu.VMEM((slots, width), BF16),
            pltpu.VMEM((slots, width), BF16),
            pltpu.VMEM(weight.shape, F32),
            pltpu.VMEM((slots, count), BF16),
            pltpu.VMEM((slots, count), BF16),
            pltpu.VMEM((N_Y, topk, block), BF16),
            pltpu.VMEM((slots, 2 * width), BF16),
            DMA((8,)), DMA((8,)), DMA((2,)), DMA((4,)), DMA((4,)), DMA((8,)),
        ],
        compiler_params=params(56),
        cost_estimate=cost(8 * count * width * slots, 24 << 20),
        name="local",
    )(tokens, grads, down, up, weight, places)


def sums_kernel(capacity, asked_ref, got_hbm, down_hbm, up_hbm, got, sums, sems, out_sems):
    rows, width = down_hbm.shape
    block = 1024
    pieces = 2 * width // block
    copies = [
        copy(got_hbm.at[:, pl.ds(j * block, block)], got.at[:, pl.ds(j * block, block)], sems.at[j])
        for j in range(pieces)
    ]
    for c in copies:
        c.start()
    hits = asked_hits(asked_ref[...], capacity, rows)
    sent = []
    for j in range(pieces):
        copies[j].wait()
        cols = pl.ds(j * block, block)
        sums[:, cols] = dot(hits, got[:, cols], TN)
        out = (down_hbm, up_hbm)[2 * j // pieces]
        c = copy(sums.at[:, cols], out.at[:, pl.ds(j * block % width, block)], out_sems.at[j])
        c.start()
        sent.append(c)
    for c in sent:
        c.wait()


def sum_rows(asked, capacity, got, rows):
    slots, both = got.shape
    out = jax.ShapeDtypeStruct((rows, both // 2), F32)
    return pl.pallas_call(
        functools.partial(sums_kernel, capacity),
        out_shape=(out, out),
        in_specs=[VMEM, ANY],
        out_specs=(ANY, ANY),
        scratch_shapes=[
            pltpu.VMEM((slots, both), BF16),
            pltpu.VMEM((rows, both), F32),
            DMA((4,)),
            DMA((4,)),
        ],
        compiler_params=params(8),
        cost_estimate=cost(2 * 256 * 256 * 2048, 4 * 10**6),
        name="sums",
    )(asked, got)


def final_kernel(
    mine, c0, c1, c2, c3, p0, p1, p2, p3, d0, d1, d2a, d2b, d3, out_hbm, coef, rows, out, d_sems, out_sems
):
    core = lax.axis_index("core")
    which = core if mine else 1 - core
    half = out.shape[0]
    slots = coef.shape[0] // N_Y
    topk = c0.shape[0]
    loads = []
    start = 0
    for i, d in enumerate((d0, d1, d2a, d2b, d3)):
        loads.append(copy(d, rows.at[pl.ds(start, d.shape[0]), :], d_sems.at[i]))
        start += d.shape[0]
    for c in loads:
        c.start()
    cols = pl.ds(pl.multiple_of(which * half, half), half)
    for r, (small, places) in enumerate(((c0, p0), (c1, p1), (c2, p2), (c3, p3))):
        values = small[:, cols].astype(F32)
        slot = places[:, cols]
        for s in range(0, slots, 64):
            row = iota((64, half), 0) + s
            total = jnp.zeros((64, half), F32)
            for k in range(topk):
                total = jnp.where(row == slot[k : k + 1, :], values[k : k + 1, :], total)
            coef[r * slots + s : r * slots + s + 64, :] = total.astype(BF16)
    for c in loads:
        c.wait()
    width = out.shape[1]
    block = width // 4
    sent = []
    for j in range(4):
        cols = pl.ds(j * block, block)
        out[:, cols] = dot(coef[...], rows[:, cols], TN).astype(BF16)
        c = copy(out.at[:, cols], out_hbm.at[:, cols], out_sems.at[j])
        c.start()
        sent.append(c)
    for c in sent:
        c.wait()


def final_product(mine, coef, places, rows):
    slots, width = rows[0].shape
    half = coef[0].shape[1] // N_CORE
    return pl.pallas_call(
        functools.partial(final_kernel, mine),
        out_shape=jax.ShapeDtypeStruct((half, width), BF16),
        in_specs=[VMEM] * 8 + [ANY] * 5,
        out_specs=ANY,
        scratch_shapes=[
            pltpu.VMEM((N_Y * slots, half), BF16),
            pltpu.VMEM((N_Y * slots, width), BF16),
            pltpu.VMEM((half, width), BF16),
            DMA((5,)), DMA((4,)),
        ],
        compiler_params=params(16),
        cost_estimate=cost(2 * half * 1024 * 2048, 6 << 20),
        name="keep" if mine else "give",
    )(*coef, *places, *rows)


def turn(x, r):
    return lax.ppermute(x, "y", [(i, (i - r) % N_Y) for i in range(N_Y)])


def gathered(blocks):
    return (blocks[0],) + tuple(turn(blocks[N_Y - r], r) for r in range(1, N_Y))


def exchange(x):
    return lax.all_to_all(x, ("dp", "y", "core"), split_axis=0, concat_axis=0, tiled=True)


def program(tokens, out_grad, down_rows, up_rows, requests, places, gate_weights):
    row_count, width = down_rows.shape
    _, devices, capacity = requests.shape
    slots = devices * capacity
    y = lax.axis_index("y")

    asked = exchange(turn_ids(requests[0]))
    slot_of = jnp.transpose(places[0])
    weight = build_weight(slot_of, jnp.transpose(gate_weights[0]), slots)
    block = slot_of.shape[1] // N_Y
    blocks = [
        lax.dynamic_slice_in_dim(slot_of, ((y + r) & (N_Y - 1)) * block, block, 1) for r in range(N_Y)
    ]
    chip_places = gathered(blocks)
    outgoing = gather_rows(asked, capacity, down_rows, up_rows)
    arrived = exchange(outgoing.reshape(devices, capacity, 2 * width))
    down = arrived[:, :, :width].reshape(slots, width)
    up = arrived[:, :, width:].reshape(slots, width)
    above, below = turn(down, 1), turn(down, 3)
    *coef, part = local_terms(tokens, out_grad, down, up, weight, slot_of)
    chip_coef = gathered(coef)
    got = exchange(part.reshape(devices, capacity, 2 * width)).reshape(slots, 2 * width)
    far = (turn(above[: slots // 2], 1), turn(below[slots // 2 :], 3))
    down_all = (down, above, *far, below)
    give = final_product(False, chip_coef, chip_places, down_all)
    other = lax.ppermute(give, "core", [(0, 1), (1, 0)])
    keep = final_product(True, chip_coef, chip_places, down_all)
    input_grad = (keep.astype(F32) + other.astype(F32)).astype(BF16)
    down_grad, up_grad = sum_rows(asked, capacity, got, row_count)
    return (input_grad, down_grad, up_grad)


def solution(mesh):
    axes = ("dp", "y", "core")
    fine = Mesh(mesh.devices.reshape(mesh.devices.shape[0], N_Y, N_CORE), axes)
    in_specs = (
        P("dp", None),
        P("dp", None),
        P(axes, None),
        P(axes, None),
        P(axes, None, None),
        P(("y", "core"), "dp", None),
        P(("y", "core"), "dp", None),
    )
    out_specs = (P(axes, None), P(axes, None), P(axes, None))
    return jax.shard_map(program, mesh=fine, in_specs=in_specs, out_specs=out_specs, check_vma=False)
```

```python
import functools
import jax
import jax.numpy as jnp
from jax import lax
from jax.experimental import pallas as pl
from jax.experimental.pallas import tpu as pltpu
from jax.sharding import Mesh, PartitionSpec as P

SQRT_HALF = 0.7071067811865476
INV_ROOT_TAU = 0.3989422804014327
N_Y = 4
N_CORE = 2
F32 = jnp.float32
BF16 = jnp.bfloat16
NT = (((1,), (1,)), ((), ()))
NN = (((1,), (0,)), ((), ()))
TN = (((0,), (0,)), ((), ()))
ANY = pl.BlockSpec(memory_space=pl.ANY)
VMEM = pl.BlockSpec(memory_space=pltpu.VMEM)
DMA = pltpu.SemaphoreType.DMA


def dot(a, b, dims):
    return lax.dot_general(a, b, dims, preferred_element_type=F32)


def iota(shape, axis):
    return lax.broadcasted_iota(jnp.int32, shape, axis)


def cost(flops, bytes_accessed, transcendentals=0):
    return pl.CostEstimate(flops=flops, bytes_accessed=bytes_accessed, transcendentals=transcendentals)


def copy(src, dst, sem):
    return pltpu.make_async_copy(src, dst, sem)


def params(mib):
    return pltpu.CompilerParams(vmem_limit_bytes=mib << 20)


def stay(x):
    return pltpu.with_memory_space_constraint(x, pltpu.HBM)


def load_rows(src, dst, sems, pieces):
    rows = src.shape[0] // pieces
    return [
        copy(src.at[pl.ds(i * rows, rows), :], dst.at[pl.ds(i * rows, rows), :], sems.at[i])
        for i in range(pieces)
    ]


def ids_kernel(req_ref, out_ref):
    capacity, owners = req_ref.shape
    slots = out_ref.shape[0]
    row = iota((slots, owners), 0)
    lane = iota((slots, owners), 1)
    per_peer = N_Y * capacity
    peer = row // per_peer
    owner = (peer // N_CORE) * (N_Y * N_CORE) + ((row % per_peer) // capacity) * N_CORE + peer % N_CORE
    total = jnp.zeros((slots, 1), jnp.int32)
    for r in range(capacity):
        hit = (lane == owner) & (row % capacity == r)
        picked = jnp.where(hit, req_ref[r : r + 1, :], 0)
        total = total + jnp.sum(picked, axis=1, keepdims=True)
    out_ref[...] = jnp.broadcast_to(total, out_ref.shape)


def expand_ids(wanted):
    owners, capacity = wanted.shape
    slots = owners * capacity
    return pl.pallas_call(
        ids_kernel,
        out_shape=jax.ShapeDtypeStruct((slots, 128), jnp.int32),
        in_specs=[VMEM],
        out_specs=VMEM,
        cost_estimate=cost(10**5, 10**5),
        name="ids",
    )(jnp.transpose(wanted))


def column_hits(asked, rows):
    y = lax.axis_index("y")
    slots = asked.shape[0]
    shape = (slots, N_Y * rows)
    at = iota(shape, 1)
    owner_y = (iota(shape, 0) % (N_Y * 2)) // 2
    twice = jnp.concatenate([asked] * (N_Y * rows // asked.shape[1]), axis=1)
    hit = (twice == at % rows) & (owner_y == (y + at // rows) % N_Y)
    return hit.astype(F32).astype(BF16)


def gather_kernel(asked_ref, t0, t1, t2, t3, out_hbm, table, out, sems, out_sems):
    rows = t0.shape[0]
    width = out.shape[1]
    copies = [
        copy(t.at[:, pl.ds(0, width)], table.at[pl.ds(r * rows, rows), :], sems.at[r])
        for r, t in enumerate((t0, t1, t2, t3))
    ]
    for c in copies:
        c.start()
    hits = column_hits(asked_ref[...], rows)
    for c in copies:
        c.wait()
    block = width // 4
    sent = []
    for j in range(4):
        cols = pl.ds(j * block, block)
        out[:, cols] = dot(hits, table[:, cols], NN).astype(BF16)
        c = copy(out.at[:, cols], out_hbm.at[:, cols], out_sems.at[j])
        c.start()
        sent.append(c)
    for c in sent:
        c.wait()


def gather_rows(asked, tables, width):
    slots = asked.shape[0]
    rows = tables[0].shape[0]
    return pl.pallas_call(
        gather_kernel,
        out_shape=jax.ShapeDtypeStruct((slots, width), BF16),
        in_specs=[VMEM] + [ANY] * 4,
        out_specs=ANY,
        scratch_shapes=[
            pltpu.VMEM((N_Y * rows, width), BF16),
            pltpu.VMEM((slots, width), BF16),
            DMA((4,)),
            DMA((4,)),
        ],
        compiler_params=params(8),
        cost_estimate=cost(2 * 256 * 256 * 2048, 3 * 10**6),
    )(asked, *tables)


def weight_kernel(places_ref, gates_ref, out_ref):
    topk, block = places_ref.shape
    slots = out_ref.shape[1]
    slot = places_ref[...]
    gates = gates_ref[...]
    for s in range(0, slots, 32):
        row = iota((32, block), 0) + s
        total = jnp.zeros((32, block), F32)
        for k in range(topk):
            total = jnp.where(row == slot[k : k + 1, :], gates[k : k + 1, :], total)
        out_ref[0, s : s + 32, :] = total


def build_weight(places, gates, slots):
    topk, tokens = places.shape
    block = tokens // N_Y
    return pl.pallas_call(
        weight_kernel,
        grid=(N_Y,),
        out_shape=jax.ShapeDtypeStruct((N_Y, slots, block), F32),
        in_specs=[pl.BlockSpec((topk, block), lambda i: (0, i))] * 2,
        out_specs=pl.BlockSpec((1, slots, block), lambda i: (i, 0, 0)),
        compiler_params=params(8),
        cost_estimate=cost(3 * topk * slots * tokens, 4 * slots * tokens),
        name="weight",
    )(places, gates)


def local_kernel(
    tok_hbm, grad_hbm, rows_hbm, weight_hbm, coef_hbm, part_hbm,
    tok, grad, rows, weight, gated, coef, half, part,
    tok_sems, grad_sems, row_sems, weight_sems, coef_sem, part_sems,
):
    block = weight.shape[2]
    width = tok.shape[1]
    down = rows.at[0]
    up = rows.at[1]
    row_in = [
        copy(rows_hbm.at[:, pl.ds(i * width, width)], rows.at[i], row_sems.at[i]) for i in range(2)
    ]
    weight_in = [copy(weight_hbm.at[c], weight.at[c], weight_sems.at[c]) for c in range(N_Y)]
    tok_in = load_rows(tok_hbm, tok, tok_sems, 8)
    grad_in = load_rows(grad_hbm, grad, grad_sems, 8)

    def begin(c):
        tok_in[2 * c].start()
        tok_in[2 * c + 1].start()
        if c == 0:
            row_in[1].start()
        grad_in[2 * c].start()
        grad_in[2 * c + 1].start()
        weight_in[c].start()

    step = width // N_Y
    sent = []

    def parts(tokens, last):
        for j in range(2 * N_Y):
            left, right = ((coef, tok), (gated, grad))[j // N_Y]
            cols = pl.ds(j * step, step)
            here = dot(left[:, tokens], right[tokens, pl.ds(j % N_Y * step, step)], NN)
            if not last:
                half[:, cols] = here
                continue
            part[:, cols] = (half[:, cols] + here).astype(BF16)
            c = copy(part.at[:, cols], part_hbm.at[:, cols], part_sems.at[j])
            c.start()
            sent.append(c)

    row_in[0].start()
    begin(0)
    begin(1)
    row_in[0].wait()
    for c in range(N_Y):
        here = pl.ds(c * block, block)
        tok_in[2 * c].wait()
        tok_in[2 * c + 1].wait()
        pre = dot(down[...], tok[here, :], NT)
        if c == 0:
            row_in[1].wait()
        grad_in[2 * c].wait()
        grad_in[2 * c + 1].wait()
        weight_in[c].wait()
        if c + 2 < N_Y:
            begin(c + 2)
        back = dot(up[...], grad[here, :], NT)
        gate = weight[c]
        cdf = 0.5 * (1.0 + lax.erf(pre * SQRT_HALF))
        density = INV_ROOT_TAU * jnp.exp(-0.5 * pre * pre)
        gated[:, here] = (gate * (pre * cdf)).astype(BF16)
        coef[:, here] = (gate * (cdf + pre * density) * back).astype(BF16)
        if c == N_Y // 2 - 1:
            parts(pl.ds(0, N_Y // 2 * block), False)
    out = copy(coef, coef_hbm, coef_sem)
    out.start()
    sent.append(out)
    parts(pl.ds(N_Y // 2 * block, N_Y // 2 * block), True)
    for c in sent:
        c.wait()


def local_terms(tokens, grads, rows, weight):
    count, width = tokens.shape
    slots = rows.shape[0]
    return pl.pallas_call(
        local_kernel,
        out_shape=(
            jax.ShapeDtypeStruct((slots, count), BF16),
            jax.ShapeDtypeStruct((slots, 2 * width), BF16),
        ),
        in_specs=[ANY] * 4,
        out_specs=(ANY,) * 2,
        scratch_shapes=[
            pltpu.VMEM((count, width), BF16),
            pltpu.VMEM((count, width), BF16),
            pltpu.VMEM((2, slots, width), BF16),
            pltpu.VMEM(weight.shape, F32),
            pltpu.VMEM((slots, count), BF16),
            pltpu.VMEM((slots, count), BF16),
            pltpu.VMEM((slots, 2 * width), F32),
            pltpu.VMEM((slots, 2 * width), BF16),
            DMA((8,)), DMA((8,)), DMA((2,)), DMA((4,)), DMA, DMA((8,)),
        ],
        compiler_params=params(56),
        cost_estimate=cost(8 * count * width * slots, 24 << 20),
        name="local",
    )(tokens, grads, stay(rows), stay(weight))


def compact_kernel(coef_ref, places_ref, c0, c1, c2, c3):
    slots, count = coef_ref.shape
    topk = places_ref.shape[0]
    block = count // N_Y
    y = lax.axis_index("y")
    for r, out in enumerate((c0, c1, c2, c3)):
        here = pl.ds(pl.multiple_of(((y + r) % N_Y) * block, block), block)
        slot = places_ref[:, here]
        lines = []
        row = iota((16, block), 0)
        for k in range(topk):
            want = slot[k : k + 1, :] - row
            found = jnp.zeros((16, block), F32)
            for g in range(0, slots, 16):
                found = jnp.where(want == g, coef_ref[g : g + 16, here].astype(F32), found)
            lines.append(jnp.sum(found, axis=0, keepdims=True))
        out[...] = jnp.concatenate(lines, axis=0).astype(BF16)


def compact(coef, places):
    topk, count = places.shape
    return pl.pallas_call(
        compact_kernel,
        out_shape=tuple(jax.ShapeDtypeStruct((topk, count // N_Y), BF16) for _ in range(N_Y)),
        in_specs=[VMEM] * 2,
        out_specs=(VMEM,) * N_Y,
        compiler_params=params(8),
        cost_estimate=cost(2 * topk * coef.size, 2 * coef.size),
        name="compact",
    )(coef, places)


def own_hits(lists, rows):
    y = lax.axis_index("y")
    slots = lists[0].shape[0]
    i = iota((slots, slots), 0)
    j = iota((slots, slots), 1)
    source = ((i >> 3) << 3) + 2 * y + (i & 1)
    total = jnp.zeros((slots, rows), F32)
    for k, ids in enumerate(lists):
        take = (j == source) & (((i >> 1) & 3) == (y + k) % N_Y)
        hit = (ids[:, :rows] == iota((slots, rows), 1)).astype(F32).astype(BF16)
        total = total + dot(take.astype(F32).astype(BF16), hit, NN)
    return total.astype(BF16)


def sums_kernel(a0, a1, a2, a3, got_hbm, down_hbm, up_hbm, got, sums, sems, out_sems):
    rows, width = down_hbm.shape
    block = 1024
    pieces = 2 * width // block
    copies = [
        copy(got_hbm.at[:, pl.ds(j * block, block)], got.at[:, pl.ds(j * block, block)], sems.at[j])
        for j in range(pieces)
    ]
    for c in copies:
        c.start()
    hits = own_hits([a[...] for a in (a0, a1, a2, a3)], rows)
    sent = []
    for j in range(pieces):
        copies[j].wait()
        cols = pl.ds(j * block, block)
        sums[:, cols] = dot(hits, got[:, cols], TN)
        out = (down_hbm, up_hbm)[2 * j // pieces]
        c = copy(sums.at[:, cols], out.at[:, pl.ds(j * block % width, block)], out_sems.at[j])
        c.start()
        sent.append(c)
    for c in sent:
        c.wait()


def sum_rows(lists, got, rows):
    slots, both = got.shape
    out = jax.ShapeDtypeStruct((rows, both // 2), F32)
    return pl.pallas_call(
        sums_kernel,
        out_shape=(out, out),
        in_specs=[VMEM] * N_Y + [ANY],
        out_specs=(ANY, ANY),
        scratch_shapes=[
            pltpu.VMEM((slots, both), BF16),
            pltpu.VMEM((rows, both), F32),
            DMA((4,)),
            DMA((4,)),
        ],
        compiler_params=params(8),
        cost_estimate=cost(2 * 256 * 256 * 2048, 4 * 10**6),
        name="sums",
    )(*lists, got)


def final_kernel(
    mine, c0, c1, c2, c3, p0, p1, p2, p3, d0, d1, d2, d3, out_hbm, coef, rows, out, d_sems, out_sems
):
    core = lax.axis_index("core")
    which = core if mine else 1 - core
    half = out.shape[0]
    slots = coef.shape[0] // N_Y
    topk = c0.shape[0]
    loads = []
    start = 0
    for i, d in enumerate((d0, d1, d2, d3)):
        loads.append(copy(d, rows.at[pl.ds(start, d.shape[0]), :], d_sems.at[i]))
        start += d.shape[0]
    for c in loads:
        c.start()
    cols = pl.ds(pl.multiple_of(which * half, half), half)
    for r, (small, places) in enumerate(((c0, p0), (c1, p1), (c2, p2), (c3, p3))):
        values = small[:, cols].astype(F32)
        slot = places[:, cols]
        for s in range(0, slots, 64):
            row = iota((64, half), 0) + s
            total = jnp.zeros((64, half), F32)
            for k in range(topk):
                total = jnp.where(row == slot[k : k + 1, :], values[k : k + 1, :], total)
            coef[r * slots + s : r * slots + s + 64, :] = total.astype(BF16)
    for c in loads:
        c.wait()
    width = out.shape[1]
    block = width // 4
    sent = []
    for j in range(4):
        cols = pl.ds(j * block, block)
        out[:, cols] = dot(coef[...], rows[:, cols], TN).astype(BF16)
        c = copy(out.at[:, cols], out_hbm.at[:, cols], out_sems.at[j])
        c.start()
        sent.append(c)
    for c in sent:
        c.wait()


def final_product(mine, coef, places, rows):
    slots, width = rows[0].shape
    half = coef[0].shape[1] // N_CORE
    return pl.pallas_call(
        functools.partial(final_kernel, mine),
        out_shape=jax.ShapeDtypeStruct((half, width), BF16),
        in_specs=[VMEM] * 8 + [ANY] * 4,
        out_specs=ANY,
        scratch_shapes=[
            pltpu.VMEM((N_Y * slots, half), BF16),
            pltpu.VMEM((N_Y * slots, width), BF16),
            pltpu.VMEM((half, width), BF16),
            DMA((4,)), DMA((4,)),
        ],
        compiler_params=params(16),
        cost_estimate=cost(2 * half * 1024 * 2048, 6 << 20),
        name="keep" if mine else "give",
    )(*coef, *places, *rows)


def turn(x, r):
    return lax.ppermute(x, "y", [(i, (i - r) % N_Y) for i in range(N_Y)])


def gathered(blocks):
    return (blocks[0],) + tuple(turn(blocks[N_Y - r], r) for r in range(1, N_Y))


def exchange(x, axes):
    return lax.all_to_all(x, axes, split_axis=0, concat_axis=0, tiled=True)


def program(tokens, out_grad, down_rows, up_rows, requests, places, gate_weights):
    row_count, width = down_rows.shape
    _, devices, capacity = requests.shape
    slots = devices * capacity
    peers = devices // N_Y
    y = lax.axis_index("y")

    def column(x):
        wide = x.reshape(peers, slots // peers, x.shape[1])
        return exchange(wide, ("dp", "core")).reshape(x.shape)

    tables = gathered([jnp.concatenate([down_rows, up_rows], axis=1)] * N_Y)
    asked = column(expand_ids(requests[0]))
    slot_of = jnp.transpose(places[0])
    slot_of = (slot_of & ~15) | ((slot_of & 2) << 2) | ((slot_of & 12) >> 1) | (slot_of & 1)
    weight = build_weight(slot_of, jnp.transpose(gate_weights[0]), slots)
    rows = gather_rows(asked, tables, 2 * width)
    arrived = column(rows)
    lists = gathered([asked] * N_Y)
    block = slot_of.shape[1] // N_Y
    blocks = [
        lax.dynamic_slice_in_dim(slot_of, ((y + r) & (N_Y - 1)) * block, block, 1) for r in range(N_Y)
    ]
    chip_places = gathered(blocks)
    far = gather_rows(lists[2], tables, width)
    opposite = column(far)
    down = arrived[:, :width]
    above, below = turn(down, 1), turn(down, 3)
    coef, part = local_terms(tokens, out_grad, arrived, weight)
    part = part.reshape(devices, capacity, 2 * width)
    got = exchange(part, ("dp", "core", "y")).reshape(slots, 2 * width)
    small = compact(coef, slot_of)
    chip_coef = gathered(small)
    down_all = (down, above, opposite, below)
    give = final_product(False, chip_coef, chip_places, down_all)
    other = lax.ppermute(give, "core", [(0, 1), (1, 0)])
    keep = final_product(True, chip_coef, chip_places, down_all)
    input_grad = (keep.astype(F32) + other.astype(F32)).astype(BF16)
    down_grad, up_grad = sum_rows(lists, got, row_count)
    return (input_grad, down_grad, up_grad)


def solution(mesh):
    axes = ("dp", "y", "core")
    fine = Mesh(mesh.devices.reshape(mesh.devices.shape[0], N_Y, N_CORE), axes)
    in_specs = (
        P("dp", None),
        P("dp", None),
        P(axes, None),
        P(axes, None),
        P(axes, None, None),
        P(("y", "core"), "dp", None),
        P(("y", "core"), "dp", None),
    )
    out_specs = (P(axes, None), P(axes, None), P(axes, None))
    return jax.shard_map(program, mesh=fine, in_specs=in_specs, out_specs=out_specs, check_vma=False)
```

```python
import functools
import jax
import jax.numpy as jnp
from jax import lax
from jax.experimental import pallas as pl
from jax.experimental.pallas import tpu as pltpu
from jax.sharding import Mesh, PartitionSpec as P

SQRT_HALF = 0.7071067811865476
INV_ROOT_TAU = 0.3989422804014327
N_Y = 4
N_CORE = 2
F32 = jnp.float32
BF16 = jnp.bfloat16
NT = (((1,), (1,)), ((), ()))
NN = (((1,), (0,)), ((), ()))
TN = (((0,), (0,)), ((), ()))
ANY = pl.BlockSpec(memory_space=pl.ANY)
VMEM = pl.BlockSpec(memory_space=pltpu.VMEM)
DMA = pltpu.SemaphoreType.DMA


def dot(a, b, dims):
    return lax.dot_general(a, b, dims, preferred_element_type=F32)


def iota(shape, axis):
    return lax.broadcasted_iota(jnp.int32, shape, axis)


def cost(flops, bytes_accessed, transcendentals=0):
    return pl.CostEstimate(flops=flops, bytes_accessed=bytes_accessed, transcendentals=transcendentals)


def copy(src, dst, sem):
    return pltpu.make_async_copy(src, dst, sem)


def params(mib):
    return pltpu.CompilerParams(vmem_limit_bytes=mib << 20)


def stay(x):
    return pltpu.with_memory_space_constraint(x, pltpu.HBM)


def load_rows(src, dst, sems, pieces):
    rows = src.shape[0] // pieces
    return [
        copy(src.at[pl.ds(i * rows, rows), :], dst.at[pl.ds(i * rows, rows), :], sems.at[i])
        for i in range(pieces)
    ]


def ids_kernel(req_ref, out_ref):
    capacity, owners = req_ref.shape
    row = iota((owners, owners), 0)
    lane = iota((owners, owners), 1)
    total = jnp.zeros(out_ref.shape, jnp.int32)
    at = iota(out_ref.shape, 1)
    for r in range(capacity):
        picked = jnp.where(lane == row, req_ref[r : r + 1, :], 0)
        column = jnp.sum(picked, axis=1, keepdims=True)
        total = jnp.where(at == r, column, total)
    out_ref[...] = total


def turn_ids(wanted):
    owners, _ = wanted.shape
    return pl.pallas_call(
        ids_kernel,
        out_shape=jax.ShapeDtypeStruct((owners, 128), jnp.int32),
        in_specs=[VMEM],
        out_specs=VMEM,
        cost_estimate=cost(10**5, 10**5),
        name="ids",
    )(jnp.transpose(wanted))


def asked_hits(asked, capacity, rows, flip):
    devices = asked.shape[0]
    slots = devices * capacity
    at = iota((devices, rows), 1)
    place = iota((slots, devices), 0)
    device = iota((slots, devices), 1) ^ flip
    total = jnp.zeros((slots, rows), F32)
    for r in range(capacity):
        hit = (asked[:, r : r + 1] == at).astype(F32).astype(BF16)
        spread = (place == device * capacity + r).astype(F32).astype(BF16)
        total = total + dot(spread, hit, NN)
    return total.astype(BF16)


def gather_kernel(asked_ref, down_ref, up_ref, out_hbm, far_hbm, out, far, out_sems):
    devices, capacity, _ = out.shape
    rows, width = down_ref.shape
    asked = asked_ref[...]
    block = 512
    sent = []

    def fill(hits, tables, buf, hbm, base):
        for j in range(buf.shape[2] // block):
            table = tables[j * block // width]
            cols = pl.ds(j * block, block)
            found = dot(hits, table[:, pl.ds(j * block % width, block)], NN).astype(BF16)
            buf[:, :, cols] = found.reshape(devices, capacity, block)
            c = copy(buf.at[:, :, cols], hbm.at[:, :, cols], out_sems.at[base + j])
            c.start()
            sent.append(c)

    fill(asked_hits(asked, capacity, rows, 0), (down_ref, up_ref), out, out_hbm, 0)
    fill(asked_hits(asked, capacity, rows, 2 * N_CORE), (down_ref,), far, far_hbm, 8)
    for c in sent:
        c.wait()


def gather_rows(asked, capacity, down_rows, up_rows):
    devices = asked.shape[0]
    width = down_rows.shape[1]
    shapes = ((devices, capacity, 2 * width), (devices, capacity, width))
    return pl.pallas_call(
        gather_kernel,
        out_shape=tuple(jax.ShapeDtypeStruct(x, BF16) for x in shapes),
        in_specs=[VMEM] * 3,
        out_specs=(ANY, ANY),
        scratch_shapes=[pltpu.VMEM(x, BF16) for x in shapes] + [DMA((12,))],
        compiler_params=params(8),
        cost_estimate=cost(3 * 256 * 256 * 2048, 4 * 10**6),
        name="gather",
    )(asked, stay(down_rows), stay(up_rows))


def weight_kernel(places_ref, gates_ref, out_ref):
    topk, block = places_ref.shape
    slots = out_ref.shape[1]
    slot = places_ref[...]
    gates = gates_ref[...]
    for s in range(0, slots, 32):
        row = iota((32, block), 0) + s
        total = jnp.zeros((32, block), F32)
        for k in range(topk):
            total = jnp.where(row == slot[k : k + 1, :], gates[k : k + 1, :], total)
        out_ref[0, s : s + 32, :] = total


def build_weight(places, gates, slots):
    topk, tokens = places.shape
    block = tokens // N_Y
    return pl.pallas_call(
        weight_kernel,
        grid=(N_Y,),
        out_shape=jax.ShapeDtypeStruct((N_Y, slots, block), F32),
        in_specs=[pl.BlockSpec((topk, block), lambda i: (0, i))] * 2,
        out_specs=pl.BlockSpec((1, slots, block), lambda i: (i, 0, 0)),
        compiler_params=params(8),
        cost_estimate=cost(3 * topk * slots * tokens, 4 * slots * tokens),
        name="weight",
    )(places, gates)


def local_kernel(
    tok_hbm, grad_hbm, rows_hbm, weight_hbm, coef_hbm, part_hbm,
    tok, grad, raw, rows, weight, gated, coef, half, part,
    tok_sems, grad_sems, row_sems, weight_sems, coef_sem, part_sems,
):
    block = weight.shape[2]
    width = tok.shape[1]
    down = rows.at[0]
    up = rows.at[1]
    row_in = [
        copy(rows_hbm.at[:, :, pl.ds(i * width, width)], raw.at[i], row_sems.at[i]) for i in range(2)
    ]
    weight_in = [copy(weight_hbm.at[c], weight.at[c], weight_sems.at[c]) for c in range(N_Y)]
    tok_in = load_rows(tok_hbm, tok, tok_sems, 8)
    grad_in = load_rows(grad_hbm, grad, grad_sems, 8)

    def begin(c):
        tok_in[2 * c].start()
        tok_in[2 * c + 1].start()
        if c == 0:
            row_in[1].start()
        grad_in[2 * c].start()
        grad_in[2 * c + 1].start()
        weight_in[c].start()

    step = width // N_Y
    slots = rows.shape[1]
    chunk = part.shape[:2] + (step,)
    sent = []

    def unpack(i):
        row_in[i].wait()
        for j in range(N_Y):
            cols = pl.ds(j * step, step)
            rows[i, :, cols] = raw[i, :, :, cols].reshape(slots, step)

    def parts(tokens, last):
        for j in range(2 * N_Y):
            left, right = ((coef, tok), (gated, grad))[j // N_Y]
            cols = pl.ds(j * step, step)
            here = dot(left[:, tokens], right[tokens, pl.ds(j % N_Y * step, step)], NN)
            if not last:
                half[:, cols] = here
                continue
            part[:, :, cols] = (half[:, cols] + here).astype(BF16).reshape(chunk)
            c = copy(part.at[:, :, cols], part_hbm.at[:, :, cols], part_sems.at[j])
            c.start()
            sent.append(c)

    row_in[0].start()
    begin(0)
    begin(1)
    unpack(0)
    for c in range(N_Y):
        here = pl.ds(c * block, block)
        tok_in[2 * c].wait()
        tok_in[2 * c + 1].wait()
        pre = dot(down[...], tok[here, :], NT)
        if c == 0:
            unpack(1)
        grad_in[2 * c].wait()
        grad_in[2 * c + 1].wait()
        weight_in[c].wait()
        if c + 2 < N_Y:
            begin(c + 2)
        back = dot(up[...], grad[here, :], NT)
        gate = weight[c]
        cdf = 0.5 * (1.0 + lax.erf(pre * SQRT_HALF))
        density = INV_ROOT_TAU * jnp.exp(-0.5 * pre * pre)
        gated[:, here] = (gate * (pre * cdf)).astype(BF16)
        coef[:, here] = (gate * (cdf + pre * density) * back).astype(BF16)
        if c == N_Y // 2 - 1:
            parts(pl.ds(0, N_Y // 2 * block), False)
    out = copy(coef, coef_hbm, coef_sem)
    out.start()
    sent.append(out)
    parts(pl.ds(N_Y // 2 * block, N_Y // 2 * block), True)
    for c in sent:
        c.wait()


def local_terms(tokens, grads, rows, weight):
    count, width = tokens.shape
    slots = rows.shape[0] * rows.shape[1]
    return pl.pallas_call(
        local_kernel,
        out_shape=(
            jax.ShapeDtypeStruct((slots, count), BF16),
            jax.ShapeDtypeStruct(rows.shape, BF16),
        ),
        in_specs=[ANY] * 4,
        out_specs=(ANY,) * 2,
        scratch_shapes=[
            pltpu.VMEM((count, width), BF16),
            pltpu.VMEM((count, width), BF16),
            pltpu.VMEM((2,) + rows.shape[:2] + (width,), BF16),
            pltpu.VMEM((2, slots, width), BF16),
            pltpu.VMEM(weight.shape, F32),
            pltpu.VMEM((slots, count), BF16),
            pltpu.VMEM((slots, count), BF16),
            pltpu.VMEM((slots, 2 * width), F32),
            pltpu.VMEM(rows.shape, BF16),
            DMA((8,)), DMA((8,)), DMA((2,)), DMA((4,)), DMA, DMA((8,)),
        ],
        compiler_params=params(56),
        cost_estimate=cost(8 * count * width * slots, 24 << 20),
        name="local",
    )(tokens, grads, stay(rows), stay(weight))


def compact_kernel(coef_ref, places_ref, c0, c1, c2, c3):
    slots, count = coef_ref.shape
    topk = places_ref.shape[0]
    block = count // N_Y
    y = lax.axis_index("y")
    for r, out in enumerate((c0, c1, c2, c3)):
        here = pl.ds(pl.multiple_of(((y + r) % N_Y) * block, block), block)
        slot = places_ref[:, here]
        lines = []
        row = iota((16, block), 0)
        for k in range(topk):
            want = slot[k : k + 1, :] - row
            found = jnp.zeros((16, block), F32)
            for g in range(0, slots, 16):
                found = jnp.where(want == g, coef_ref[g : g + 16, here].astype(F32), found)
            lines.append(jnp.sum(found, axis=0, keepdims=True))
        out[...] = jnp.concatenate(lines, axis=0).astype(BF16)


def compact(coef, places):
    topk, count = places.shape
    return pl.pallas_call(
        compact_kernel,
        out_shape=tuple(jax.ShapeDtypeStruct((topk, count // N_Y), BF16) for _ in range(N_Y)),
        in_specs=[VMEM] * 2,
        out_specs=(VMEM,) * N_Y,
        compiler_params=params(8),
        cost_estimate=cost(2 * topk * coef.size, 2 * coef.size),
        name="compact",
    )(coef, places)


def sums_kernel(asked_ref, got_hbm, down_hbm, up_hbm, got, sums, sems, out_sems):
    rows, width = down_hbm.shape
    devices, capacity, both = got.shape
    block = 512
    pieces = both // block
    copies = []
    for j in range(pieces):
        cols = pl.ds(j * block, block)
        copies.append(copy(got_hbm.at[:, :, cols], got.at[:, :, cols], sems.at[j]))
        copies[j].start()
    hits = asked_hits(asked_ref[...], capacity, rows, 0)
    sent = []
    for j in range(pieces):
        copies[j].wait()
        cols = pl.ds(j * block, block)
        sums[:, cols] = dot(hits, got[:, :, cols].reshape(devices * capacity, block), TN)
        out = (down_hbm, up_hbm)[2 * j // pieces]
        c = copy(sums.at[:, cols], out.at[:, pl.ds(j * block % width, block)], out_sems.at[j])
        c.start()
        sent.append(c)
    for c in sent:
        c.wait()


def sum_rows(asked, got, rows):
    both = got.shape[2]
    out = jax.ShapeDtypeStruct((rows, both // 2), F32)
    return pl.pallas_call(
        sums_kernel,
        out_shape=(out, out),
        in_specs=[VMEM, ANY],
        out_specs=(ANY, ANY),
        scratch_shapes=[
            pltpu.VMEM(got.shape, BF16),
            pltpu.VMEM((rows, both), F32),
            DMA((8,)),
            DMA((8,)),
        ],
        compiler_params=params(12),
        cost_estimate=cost(2 * 256 * 256 * 2048, 4 * 10**6),
        name="sums",
    )(asked, stay(got))


def final_kernel(
    mine, c0, c1, c2, c3, p0, p1, p2, p3, d0, d1, d2, d3, out_hbm, coef, rows, out, d_sems, out_sems
):
    core = lax.axis_index("core")
    which = core if mine else 1 - core
    half = out.shape[0]
    slots = coef.shape[0] // N_Y
    topk = c0.shape[0]
    loads = []
    start = 0
    for i, d in enumerate((d0, d1, d2, d3)):
        loads.append(copy(d, rows.at[pl.ds(start, d.shape[0]), :], d_sems.at[i]))
        start += d.shape[0]
    for c in loads:
        c.start()
    cols = pl.ds(pl.multiple_of(which * half, half), half)
    for r, (small, places) in enumerate(((c0, p0), (c1, p1), (c2, p2), (c3, p3))):
        values = small[:, cols].astype(F32)
        slot = places[:, cols]
        for s in range(0, slots, 64):
            row = iota((64, half), 0) + s
            total = jnp.zeros((64, half), F32)
            for k in range(topk):
                total = jnp.where(row == slot[k : k + 1, :], values[k : k + 1, :], total)
            coef[r * slots + s : r * slots + s + 64, :] = total.astype(BF16)
    for c in loads:
        c.wait()
    width = out.shape[1]
    block = width // 4
    sent = []
    for j in range(4):
        cols = pl.ds(j * block, block)
        out[:, cols] = dot(coef[...], rows[:, cols], TN).astype(BF16)
        c = copy(out.at[:, cols], out_hbm.at[:, cols], out_sems.at[j])
        c.start()
        sent.append(c)
    for c in sent:
        c.wait()


def final_product(mine, coef, places, rows):
    slots, width = rows[0].shape
    half = coef[0].shape[1] // N_CORE
    return pl.pallas_call(
        functools.partial(final_kernel, mine),
        out_shape=jax.ShapeDtypeStruct((half, width), BF16),
        in_specs=[VMEM] * 8 + [ANY] * 4,
        out_specs=ANY,
        scratch_shapes=[
            pltpu.VMEM((N_Y * slots, half), BF16),
            pltpu.VMEM((N_Y * slots, width), BF16),
            pltpu.VMEM((half, width), BF16),
            DMA((4,)), DMA((4,)),
        ],
        compiler_params=params(16),
        cost_estimate=cost(2 * half * 1024 * 2048, 6 << 20),
        name="keep" if mine else "give",
    )(*coef, *places, *rows)


def turn(x, r):
    return lax.ppermute(x, "y", [(i, (i - r) % N_Y) for i in range(N_Y)])


def gathered(blocks):
    return (blocks[0],) + tuple(turn(blocks[N_Y - r], r) for r in range(1, N_Y))


def exchange(x):
    return lax.all_to_all(x, ("dp", "y", "core"), split_axis=0, concat_axis=0, tiled=True)


def program(tokens, out_grad, down_rows, up_rows, requests, places, gate_weights):
    row_count, width = down_rows.shape
    _, devices, capacity = requests.shape
    slots = devices * capacity
    y = lax.axis_index("y")

    asked = exchange(turn_ids(requests[0]))
    slot_of = jnp.transpose(places[0])
    weight = build_weight(slot_of, jnp.transpose(gate_weights[0]), slots)
    block = slot_of.shape[1] // N_Y
    blocks = [
        lax.dynamic_slice_in_dim(slot_of, ((y + r) & (N_Y - 1)) * block, block, 1) for r in range(N_Y)
    ]
    chip_places = gathered(blocks)
    outgoing, far = gather_rows(asked, capacity, down_rows, up_rows)
    arrived = exchange(outgoing)
    down = arrived[:, :, :width]
    above, below = turn(down, 1), turn(down, 3)
    opposite = exchange(far)
    coef, part = local_terms(tokens, out_grad, arrived, weight)
    small = compact(coef, slot_of)
    chip_coef = gathered(small)
    got = exchange(part)
    down_all = [x.reshape(slots, width) for x in (down, above, opposite, below)]
    give = final_product(False, chip_coef, chip_places, down_all)
    other = lax.ppermute(give, "core", [(0, 1), (1, 0)])
    keep = final_product(True, chip_coef, chip_places, down_all)
    input_grad = (keep.astype(F32) + other.astype(F32)).astype(BF16)
    down_grad, up_grad = sum_rows(asked, got, row_count)
    return (input_grad, down_grad, up_grad)


def solution(mesh):
    axes = ("dp", "y", "core")
    fine = Mesh(mesh.devices.reshape(mesh.devices.shape[0], N_Y, N_CORE), axes)
    in_specs = (
        P("dp", None),
        P("dp", None),
        P(axes, None),
        P(axes, None),
        P(axes, None, None),
        P(("y", "core"), "dp", None),
        P(("y", "core"), "dp", None),
    )
    out_specs = (P(axes, None), P(axes, None), P(axes, None))
    return jax.shard_map(program, mesh=fine, in_specs=in_specs, out_specs=out_specs, check_vma=False)
```

```python
import functools
import jax
import jax.numpy as jnp
from jax import lax
from jax.experimental import pallas as pl
from jax.experimental.pallas import tpu as pltpu
from jax.sharding import Mesh, PartitionSpec as P

SQRT_HALF = 0.7071067811865476
INV_ROOT_TAU = 0.3989422804014327
N_Y = 4
N_CORE = 2
F32 = jnp.float32
BF16 = jnp.bfloat16
NT = (((1,), (1,)), ((), ()))
NN = (((1,), (0,)), ((), ()))
TN = (((0,), (0,)), ((), ()))
ANY = pl.BlockSpec(memory_space=pl.ANY)
VMEM = pl.BlockSpec(memory_space=pltpu.VMEM)
DMA = pltpu.SemaphoreType.DMA


def dot(a, b, dims):
    return lax.dot_general(a, b, dims, preferred_element_type=F32)


def iota(shape, axis):
    return lax.broadcasted_iota(jnp.int32, shape, axis)


def cost(flops, bytes_accessed, transcendentals=0):
    return pl.CostEstimate(flops=flops, bytes_accessed=bytes_accessed, transcendentals=transcendentals)


def copy(src, dst, sem):
    return pltpu.make_async_copy(src, dst, sem)


def params(mib):
    return pltpu.CompilerParams(vmem_limit_bytes=mib << 20)


def stay(x):
    return pltpu.with_memory_space_constraint(x, pltpu.HBM)


def load_rows(src, dst, sems, pieces):
    rows = src.shape[0] // pieces
    return [
        copy(src.at[pl.ds(i * rows, rows), :], dst.at[pl.ds(i * rows, rows), :], sems.at[i])
        for i in range(pieces)
    ]


def ids_kernel(req_ref, out_ref):
    capacity, owners = req_ref.shape
    slots = out_ref.shape[0]
    row = iota((slots, owners), 0)
    lane = iota((slots, owners), 1)
    per_peer = N_Y * capacity
    peer = row // per_peer
    owner = (peer // N_CORE) * (N_Y * N_CORE) + ((row % per_peer) // capacity) * N_CORE + peer % N_CORE
    total = jnp.zeros((slots, 1), jnp.int32)
    for r in range(capacity):
        hit = (lane == owner) & (row % capacity == r)
        picked = jnp.where(hit, req_ref[r : r + 1, :], 0)
        total = total + jnp.sum(picked, axis=1, keepdims=True)
    out_ref[...] = jnp.broadcast_to(total, out_ref.shape)


def expand_ids(wanted):
    owners, capacity = wanted.shape
    slots = owners * capacity
    return pl.pallas_call(
        ids_kernel,
        out_shape=jax.ShapeDtypeStruct((slots, 128), jnp.int32),
        in_specs=[VMEM],
        out_specs=VMEM,
        cost_estimate=cost(10**5, 10**5),
        name="ids",
    )(jnp.transpose(wanted))


def column_hits(asked, rows):
    y = lax.axis_index("y")
    slots = asked.shape[0]
    shape = (slots, N_Y * rows)
    at = iota(shape, 1)
    owner_y = (iota(shape, 0) % (N_Y * 2)) // 2
    twice = jnp.concatenate([asked] * (N_Y * rows // asked.shape[1]), axis=1)
    hit = (twice == at % rows) & (owner_y == (y + at // rows) % N_Y)
    return hit.astype(F32).astype(BF16)


def gather_kernel(asked_ref, t0, t1, t2, t3, out_hbm, table, out, sems, out_sems):
    rows = t0.shape[0]
    width = out.shape[1]
    copies = [
        copy(t.at[:, pl.ds(0, width)], table.at[pl.ds(r * rows, rows), :], sems.at[r])
        for r, t in enumerate((t0, t1, t2, t3))
    ]
    for c in copies:
        c.start()
    hits = column_hits(asked_ref[...], rows)
    for c in copies:
        c.wait()
    block = width // 4
    sent = []
    for j in range(4):
        cols = pl.ds(j * block, block)
        out[:, cols] = dot(hits, table[:, cols], NN).astype(BF16)
        c = copy(out.at[:, cols], out_hbm.at[:, cols], out_sems.at[j])
        c.start()
        sent.append(c)
    for c in sent:
        c.wait()


def gather_rows(asked, tables, width):
    slots = asked.shape[0]
    rows = tables[0].shape[0]
    return pl.pallas_call(
        gather_kernel,
        out_shape=jax.ShapeDtypeStruct((slots, width), BF16),
        in_specs=[VMEM] + [ANY] * 4,
        out_specs=ANY,
        scratch_shapes=[
            pltpu.VMEM((N_Y * rows, width), BF16),
            pltpu.VMEM((slots, width), BF16),
            DMA((4,)),
            DMA((4,)),
        ],
        compiler_params=params(8),
        cost_estimate=cost(2 * 256 * 256 * 2048, 3 * 10**6),
    )(asked, *tables)


def weight_kernel(places_ref, gates_ref, out_ref):
    topk, block = places_ref.shape
    slots = out_ref.shape[1]
    slot = places_ref[...]
    gates = gates_ref[...]
    for s in range(0, slots, 32):
        row = iota((32, block), 0) + s
        total = jnp.zeros((32, block), F32)
        for k in range(topk):
            total = jnp.where(row == slot[k : k + 1, :], gates[k : k + 1, :], total)
        out_ref[0, s : s + 32, :] = total


def build_weight(places, gates, slots):
    topk, tokens = places.shape
    block = tokens // N_Y
    return pl.pallas_call(
        weight_kernel,
        grid=(N_Y,),
        out_shape=jax.ShapeDtypeStruct((N_Y, slots, block), F32),
        in_specs=[pl.BlockSpec((topk, block), lambda i: (0, i))] * 2,
        out_specs=pl.BlockSpec((1, slots, block), lambda i: (i, 0, 0)),
        compiler_params=params(8),
        cost_estimate=cost(3 * topk * slots * tokens, 4 * slots * tokens),
        name="weight",
    )(places, gates)


def half_kernel(
    first, lead_hbm, other_hbm, rows_hbm, side_hbm, extra_hbm, part_hbm,
    lead, other, rows, side, left, slope, half, part,
    lead_sems, other_sems, row_sem, side_sems, extra_sems, part_sems,
):
    block = side.shape[2]
    width = lead.shape[1]
    step = width // N_Y
    chunk = part.shape[:2] + (step,)
    rows_in = copy(rows_hbm, rows, row_sem)
    side_in = [copy(side_hbm.at[c], side.at[c], side_sems.at[c]) for c in range(N_Y)]
    lead_in = load_rows(lead_hbm, lead, lead_sems, 8)
    other_in = load_rows(other_hbm, other, other_sems, 8)
    sent = []

    def begin(c):
        for i in (2 * c, 2 * c + 1):
            lead_in[i].start()
        side_in[c].start()
        for i in (2 * c, 2 * c + 1):
            other_in[i].start()

    def parts(c, last):
        tokens = pl.ds((c - 1) * block, 2 * block)
        for i in range(2 * c - 2, 2 * c + 2):
            other_in[i].wait()
        for j in range(N_Y):
            cols = pl.ds(j * step, step)
            here = dot(left[:, tokens], other[tokens, cols], NN)
            if not last:
                half[:, cols] = here
                continue
            part[:, :, cols] = (half[:, cols] + here).astype(BF16).reshape(chunk)
            out = copy(part.at[:, :, cols], part_hbm.at[:, :, cols], part_sems.at[j])
            out.start()
            sent.append(out)

    rows_in.start()
    begin(0)
    begin(1)
    rows_in.wait()
    for c in range(N_Y):
        here = pl.ds(c * block, block)
        lead_in[2 * c].wait()
        lead_in[2 * c + 1].wait()
        side_in[c].wait()
        if c + 2 < N_Y:
            begin(c + 2)
        found = dot(rows[...], lead[here, :], NT)
        if first:
            cdf = 0.5 * (1.0 + lax.erf(found * SQRT_HALF))
            density = INV_ROOT_TAU * jnp.exp(-0.5 * found * found)
            left[:, here] = (side[c] * (found * cdf)).astype(BF16)
            slope[c] = side[c] * (cdf + found * density)
            out = copy(slope.at[c], extra_hbm.at[c], extra_sems.at[c])
        else:
            left[:, here] = (side[c] * found).astype(BF16)
            out = copy(left.at[:, here], extra_hbm.at[:, here], extra_sems.at[c])
        out.start()
        sent.append(out)
        if c == N_Y // 2 - 1:
            parts(c, False)
    parts(N_Y - 1, True)
    for out in sent:
        out.wait()


def half_terms(first, lead, other, rows, side, devices):
    count, width = lead.shape
    slots = rows.shape[0]
    chunks = (devices, slots // devices, width)
    extra = (side.shape, F32) if first else ((slots, count), BF16)
    return pl.pallas_call(
        functools.partial(half_kernel, first),
        out_shape=(jax.ShapeDtypeStruct(*extra), jax.ShapeDtypeStruct(chunks, BF16)),
        in_specs=[ANY] * 4,
        out_specs=(ANY,) * 2,
        scratch_shapes=[
            pltpu.VMEM((count, width), BF16),
            pltpu.VMEM((count, width), BF16),
            pltpu.VMEM((slots, width), BF16),
            pltpu.VMEM(side.shape, F32),
            pltpu.VMEM((slots, count), BF16),
            pltpu.VMEM(side.shape, F32),
            pltpu.VMEM((slots, width), F32),
            pltpu.VMEM(chunks, BF16),
            DMA((8,)), DMA((8,)), DMA, DMA((4,)), DMA((4,)), DMA((4,)),
        ],
        compiler_params=params(56),
        cost_estimate=cost(4 * count * width * slots, 24 << 20),
        name="first" if first else "second",
    )(lead, other, stay(rows), stay(side))


def compact_kernel(coef_ref, places_ref, c0, c1, c2, c3):
    slots, count = coef_ref.shape
    topk = places_ref.shape[0]
    block = count // N_Y
    y = lax.axis_index("y")
    for r, out in enumerate((c0, c1, c2, c3)):
        here = pl.ds(pl.multiple_of(((y + r) % N_Y) * block, block), block)
        slot = places_ref[:, here]
        lines = []
        row = iota((16, block), 0)
        for k in range(topk):
            want = slot[k : k + 1, :] - row
            found = jnp.zeros((16, block), F32)
            for g in range(0, slots, 16):
                found = jnp.where(want == g, coef_ref[g : g + 16, here].astype(F32), found)
            lines.append(jnp.sum(found, axis=0, keepdims=True))
        out[...] = jnp.concatenate(lines, axis=0).astype(BF16)


def compact(coef, places):
    topk, count = places.shape
    return pl.pallas_call(
        compact_kernel,
        out_shape=tuple(jax.ShapeDtypeStruct((topk, count // N_Y), BF16) for _ in range(N_Y)),
        in_specs=[VMEM] * 2,
        out_specs=(VMEM,) * N_Y,
        compiler_params=params(8),
        cost_estimate=cost(2 * topk * coef.size, 2 * coef.size),
        name="compact",
    )(coef, places)


def own_hits(lists, rows):
    y = lax.axis_index("y")
    slots = lists[0].shape[0]
    i = iota((slots, slots), 0)
    j = iota((slots, slots), 1)
    source = ((i >> 3) << 3) + 2 * y + (i & 1)
    total = jnp.zeros((slots, rows), F32)
    for k, ids in enumerate(lists):
        take = (j == source) & (((i >> 1) & 3) == (y + k) % N_Y)
        hit = (ids[:, :rows] == iota((slots, rows), 1)).astype(F32).astype(BF16)
        total = total + dot(take.astype(F32).astype(BF16), hit, NN)
    return total.astype(BF16)


def sums_kernel(a0, a1, a2, a3, got_hbm, out_hbm, got, sums, sems, out_sems):
    rows, width = sums.shape
    devices, capacity, _ = got.shape
    block = 512
    copies = []
    for j in range(width // block):
        cols = pl.ds(j * block, block)
        copies.append(copy(got_hbm.at[:, :, cols], got.at[:, :, cols], sems.at[j]))
        copies[j].start()
    hits = own_hits([a[...] for a in (a0, a1, a2, a3)], rows)
    sent = []
    for j in range(width // block):
        copies[j].wait()
        cols = pl.ds(j * block, block)
        sums[:, cols] = dot(hits, got[:, :, cols].reshape(devices * capacity, block), TN)
        c = copy(sums.at[:, cols], out_hbm.at[:, cols], out_sems.at[j])
        c.start()
        sent.append(c)
    for c in sent:
        c.wait()


def sum_rows(lists, got, rows):
    width = got.shape[2]
    return pl.pallas_call(
        sums_kernel,
        out_shape=jax.ShapeDtypeStruct((rows, width), F32),
        in_specs=[VMEM] * N_Y + [ANY],
        out_specs=ANY,
        scratch_shapes=[
            pltpu.VMEM(got.shape, BF16),
            pltpu.VMEM((rows, width), F32),
            DMA((4,)),
            DMA((4,)),
        ],
        compiler_params=params(12),
        cost_estimate=cost(2 * 256 * 256 * 2048, 2 * 10**6),
    )(*lists, stay(got))


def final_kernel(
    mine, c0, c1, c2, c3, p0, p1, p2, p3, d0, d1, d2a, d2b, d3, out_hbm, coef, rows, out, d_sems, out_sems
):
    core = lax.axis_index("core")
    which = core if mine else 1 - core
    half = out.shape[0]
    slots = coef.shape[0] // N_Y
    topk = c0.shape[0]
    loads = []
    start = 0
    for i, d in enumerate((d0, d1, d2a, d2b, d3)):
        loads.append(copy(d, rows.at[pl.ds(start, d.shape[0]), :], d_sems.at[i]))
        start += d.shape[0]
    for c in loads:
        c.start()
    cols = pl.ds(pl.multiple_of(which * half, half), half)
    for r, (small, places) in enumerate(((c0, p0), (c1, p1), (c2, p2), (c3, p3))):
        values = small[:, cols].astype(F32)
        slot = places[:, cols]
        for s in range(0, slots, 64):
            row = iota((64, half), 0) + s
            total = jnp.zeros((64, half), F32)
            for k in range(topk):
                total = jnp.where(row == slot[k : k + 1, :], values[k : k + 1, :], total)
            coef[r * slots + s : r * slots + s + 64, :] = total.astype(BF16)
    for c in loads:
        c.wait()
    width = out.shape[1]
    block = width // 4
    sent = []
    for j in range(4):
        cols = pl.ds(j * block, block)
        out[:, cols] = dot(coef[...], rows[:, cols], TN).astype(BF16)
        c = copy(out.at[:, cols], out_hbm.at[:, cols], out_sems.at[j])
        c.start()
        sent.append(c)
    for c in sent:
        c.wait()


def final_product(mine, coef, places, rows):
    slots, width = rows[0].shape
    half = coef[0].shape[1] // N_CORE
    return pl.pallas_call(
        functools.partial(final_kernel, mine),
        out_shape=jax.ShapeDtypeStruct((half, width), BF16),
        in_specs=[VMEM] * 8 + [ANY] * 5,
        out_specs=ANY,
        scratch_shapes=[
            pltpu.VMEM((N_Y * slots, half), BF16),
            pltpu.VMEM((N_Y * slots, width), BF16),
            pltpu.VMEM((half, width), BF16),
            DMA((5,)), DMA((4,)),
        ],
        compiler_params=params(16),
        cost_estimate=cost(2 * half * 1024 * 2048, 6 << 20),
        name="keep" if mine else "give",
    )(*coef, *places, *rows)


def turn(x, r):
    return lax.ppermute(x, "y", [(i, (i - r) % N_Y) for i in range(N_Y)])


def gathered(blocks):
    return (blocks[0],) + tuple(turn(blocks[N_Y - r], r) for r in range(1, N_Y))


def exchange(x, axes):
    return lax.all_to_all(x, axes, split_axis=0, concat_axis=0, tiled=True)


def program(tokens, out_grad, down_rows, up_rows, requests, places, gate_weights):
    row_count, width = down_rows.shape
    _, devices, capacity = requests.shape
    slots = devices * capacity
    peers = devices // N_Y
    y = lax.axis_index("y")

    def column(x):
        wide = x.reshape(peers, slots // peers, x.shape[1])
        return exchange(wide, ("dp", "core")).reshape(x.shape)

    down_tables = gathered([down_rows] * N_Y)
    asked = column(expand_ids(requests[0]))
    up_tables = gathered([up_rows] * N_Y)
    slot_of = jnp.transpose(places[0])
    slot_of = (slot_of & ~15) | ((slot_of & 2) << 2) | ((slot_of & 12) >> 1) | (slot_of & 1)
    weight = build_weight(slot_of, jnp.transpose(gate_weights[0]), slots)
    down = column(gather_rows(asked, down_tables, width))
    lists = gathered([asked] * N_Y)
    block = slot_of.shape[1] // N_Y
    blocks = [
        lax.dynamic_slice_in_dim(slot_of, ((y + r) & (N_Y - 1)) * block, block, 1) for r in range(N_Y)
    ]
    chip_places = gathered(blocks)
    up = column(gather_rows(asked, up_tables, width))
    above, below = turn(down, 1), turn(down, 3)
    slope, part_up = half_terms(True, tokens, out_grad, down, weight, devices)
    got_up = exchange(part_up, ("dp", "core", "y"))
    far = (turn(above[: slots // 2], 1), turn(below[slots // 2 :], 3))
    coef, part_down = half_terms(False, out_grad, tokens, up, slope, devices)
    small = compact(coef, slot_of)
    chip_coef = gathered(small)
    got_down = exchange(part_down, ("dp", "core", "y"))
    up_grad = sum_rows(lists, got_up, row_count)
    down_all = (down, above, *far, below)
    give = final_product(False, chip_coef, chip_places, down_all)
    other = lax.ppermute(give, "core", [(0, 1), (1, 0)])
    keep = final_product(True, chip_coef, chip_places, down_all)
    input_grad = (keep.astype(F32) + other.astype(F32)).astype(BF16)
    down_grad = sum_rows(lists, got_down, row_count)
    return (input_grad, down_grad, up_grad)


def solution(mesh):
    axes = ("dp", "y", "core")
    fine = Mesh(mesh.devices.reshape(mesh.devices.shape[0], N_Y, N_CORE), axes)
    in_specs = (
        P("dp", None),
        P("dp", None),
        P(axes, None),
        P(axes, None),
        P(axes, None, None),
        P(("y", "core"), "dp", None),
        P(("y", "core"), "dp", None),
    )
    out_specs = (P(axes, None), P(axes, None), P(axes, None))
    return jax.shard_map(program, mesh=fine, in_specs=in_specs, out_specs=out_specs, check_vma=False)
```

```python
import functools
import jax
import jax.numpy as jnp
from jax import lax
from jax.experimental import pallas as pl
from jax.experimental.pallas import tpu as pltpu
from jax.sharding import Mesh, PartitionSpec as P

SQRT_HALF = 0.7071067811865476
INV_ROOT_TAU = 0.3989422804014327
N_Y = 4
N_CORE = 2
F32 = jnp.float32
BF16 = jnp.bfloat16
NT = (((1,), (1,)), ((), ()))
NN = (((1,), (0,)), ((), ()))
TN = (((0,), (0,)), ((), ()))
ANY = pl.BlockSpec(memory_space=pl.ANY)
VMEM = pl.BlockSpec(memory_space=pltpu.VMEM)
DMA = pltpu.SemaphoreType.DMA


def dot(a, b, dims):
    return lax.dot_general(a, b, dims, preferred_element_type=F32)


def iota(shape, axis):
    return lax.broadcasted_iota(jnp.int32, shape, axis)


def cost(flops, bytes_accessed, transcendentals=0):
    return pl.CostEstimate(flops=flops, bytes_accessed=bytes_accessed, transcendentals=transcendentals)


def copy(src, dst, sem):
    return pltpu.make_async_copy(src, dst, sem)


def params(mib):
    return pltpu.CompilerParams(vmem_limit_bytes=mib << 20)


def stay(x):
    return pltpu.with_memory_space_constraint(x, pltpu.HBM)


def load_rows(src, dst, sems, pieces):
    rows = src.shape[0] // pieces
    return [
        copy(src.at[pl.ds(i * rows, rows), :], dst.at[pl.ds(i * rows, rows), :], sems.at[i])
        for i in range(pieces)
    ]


def ids_kernel(req_ref, out_ref):
    capacity, owners = req_ref.shape
    slots = out_ref.shape[0]
    row = iota((slots, owners), 0)
    lane = iota((slots, owners), 1)
    per_peer = N_Y * capacity
    peer = row // per_peer
    owner = (peer // N_CORE) * (N_Y * N_CORE) + ((row % per_peer) // capacity) * N_CORE + peer % N_CORE
    total = jnp.zeros((slots, 1), jnp.int32)
    for r in range(capacity):
        hit = (lane == owner) & (row % capacity == r)
        picked = jnp.where(hit, req_ref[r : r + 1, :], 0)
        total = total + jnp.sum(picked, axis=1, keepdims=True)
    out_ref[...] = jnp.broadcast_to(total, out_ref.shape)


def expand_ids(wanted):
    owners, capacity = wanted.shape
    slots = owners * capacity
    return pl.pallas_call(
        ids_kernel,
        out_shape=jax.ShapeDtypeStruct((slots, 128), jnp.int32),
        in_specs=[VMEM],
        out_specs=VMEM,
        cost_estimate=cost(10**5, 10**5),
        name="ids",
    )(jnp.transpose(wanted))


def column_hits(asked, rows):
    y = lax.axis_index("y")
    slots = asked.shape[0]
    shape = (slots, N_Y * rows)
    at = iota(shape, 1)
    owner_y = (iota(shape, 0) % (N_Y * 2)) // 2
    twice = jnp.concatenate([asked] * (N_Y * rows // asked.shape[1]), axis=1)
    hit = (twice == at % rows) & (owner_y == (y + at // rows) % N_Y)
    return hit.astype(F32).astype(BF16)


def gather_kernel(asked_ref, t0, t1, t2, t3, out_hbm, table, out, sems, out_sems):
    rows = t0.shape[0]
    width = out.shape[1]
    copies = [
        copy(t.at[:, pl.ds(0, width)], table.at[pl.ds(r * rows, rows), :], sems.at[r])
        for r, t in enumerate((t0, t1, t2, t3))
    ]
    for c in copies:
        c.start()
    hits = column_hits(asked_ref[...], rows)
    for c in copies:
        c.wait()
    block = width // 4
    sent = []
    for j in range(4):
        cols = pl.ds(j * block, block)
        out[:, cols] = dot(hits, table[:, cols], NN).astype(BF16)
        c = copy(out.at[:, cols], out_hbm.at[:, cols], out_sems.at[j])
        c.start()
        sent.append(c)
    for c in sent:
        c.wait()


def gather_rows(asked, tables, width):
    slots = asked.shape[0]
    rows = tables[0].shape[0]
    return pl.pallas_call(
        gather_kernel,
        out_shape=jax.ShapeDtypeStruct((slots, width), BF16),
        in_specs=[VMEM] + [ANY] * 4,
        out_specs=ANY,
        scratch_shapes=[
            pltpu.VMEM((N_Y * rows, width), BF16),
            pltpu.VMEM((slots, width), BF16),
            DMA((4,)),
            DMA((4,)),
        ],
        compiler_params=params(8),
        cost_estimate=cost(2 * 256 * 256 * 2048, 3 * 10**6),
    )(asked, stay(tables[0]), *tables[1:])


def weight_kernel(places_ref, gates_ref, out_ref):
    topk, block = places_ref.shape
    slots = out_ref.shape[1]
    slot = places_ref[...]
    gates = gates_ref[...]
    for s in range(0, slots, 32):
        row = iota((32, block), 0) + s
        total = jnp.zeros((32, block), F32)
        for k in range(topk):
            total = jnp.where(row == slot[k : k + 1, :], gates[k : k + 1, :], total)
        out_ref[0, s : s + 32, :] = total


def build_weight(places, gates, slots):
    topk, tokens = places.shape
    block = tokens // N_Y
    return pl.pallas_call(
        weight_kernel,
        grid=(N_Y,),
        out_shape=jax.ShapeDtypeStruct((N_Y, slots, block), F32),
        in_specs=[pl.BlockSpec((topk, block), lambda i: (0, i))] * 2,
        out_specs=pl.BlockSpec((1, slots, block), lambda i: (i, 0, 0)),
        compiler_params=params(8),
        cost_estimate=cost(3 * topk * slots * tokens, 4 * slots * tokens),
        name="weight",
    )(places, gates)


def at_places(left, here, slot):
    topk, block = slot.shape
    row = iota((16, block), 0)
    lines = []
    for k in range(topk):
        want = slot[k : k + 1, :] - row
        found = jnp.zeros((16, block), F32)
        for g in range(0, left.shape[0], 16):
            found = jnp.where(want == g, left[g : g + 16, here].astype(F32), found)
        lines.append(jnp.sum(found, axis=0, keepdims=True))
    return jnp.concatenate(lines, axis=0).astype(BF16)


def half_kernel(first, lead_hbm, other_hbm, rows_hbm, side_hbm, *refs):
    places = None if first else refs[0]
    extra_hbm = refs[:1] if first else refs[1 : 1 + N_Y]
    (
        part_hbm, lead, other, rows, side, left, extra, half, part,
        lead_sems, other_sems, row_sem, side_sems, extra_sems, part_sems,
    ) = refs[-15:]
    block = side.shape[2]
    width = lead.shape[1]
    step = width // N_Y
    chunk = part.shape[:2] + (step,)
    rows_in = copy(rows_hbm, rows, row_sem)
    side_in = [copy(side_hbm.at[c], side.at[c], side_sems.at[c]) for c in range(N_Y)]
    lead_in = load_rows(lead_hbm, lead, lead_sems, 8)
    other_in = load_rows(other_hbm, other, other_sems, 8)
    sent = []

    def begin(c):
        for i in (2 * c, 2 * c + 1):
            lead_in[i].start()
        side_in[c].start()
        for i in (2 * c, 2 * c + 1):
            other_in[i].start()

    def parts(c, last):
        tokens = pl.ds((c - 1) * block, 2 * block)
        for i in range(2 * c - 2, 2 * c + 2):
            other_in[i].wait()
        for j in range(N_Y):
            cols = pl.ds(j * step, step)
            here = dot(left[:, tokens], other[tokens, cols], NN)
            if not last:
                half[:, cols] = here
                continue
            part[:, :, cols] = (half[:, cols] + here).astype(BF16).reshape(chunk)
            out = copy(part.at[:, :, cols], part_hbm.at[:, :, cols], part_sems.at[j])
            out.start()
            sent.append(out)

    rows_in.start()
    begin(0)
    begin(1)
    rows_in.wait()
    for c in range(N_Y):
        here = pl.ds(c * block, block)
        lead_in[2 * c].wait()
        lead_in[2 * c + 1].wait()
        side_in[c].wait()
        if c + 2 < N_Y:
            begin(c + 2)
        found = dot(rows[...], lead[here, :], NT)
        if first:
            cdf = 0.5 * (1.0 + lax.erf(found * SQRT_HALF))
            density = INV_ROOT_TAU * jnp.exp(-0.5 * found * found)
            left[:, here] = (side[c] * (found * cdf)).astype(BF16)
            extra[c] = side[c] * (cdf + found * density)
            out = copy(extra.at[c], extra_hbm[0].at[c], extra_sems.at[c])
            out.start()
            sent.append(out)
        else:
            left[:, here] = (side[c] * found).astype(BF16)
            extra[c] = at_places(left, here, places[:, here])
        if c == N_Y // 2 - 1:
            parts(c, False)
    if not first:
        y = lax.axis_index("y")
        for r in range(N_Y):
            out = copy(extra.at[(y + r) % N_Y], extra_hbm[r], extra_sems.at[r])
            out.start()
            sent.append(out)
    parts(N_Y - 1, True)
    for out in sent:
        out.wait()


def half_terms(lead, other, rows, side, devices, places=None):
    first = places is None
    count, width = lead.shape
    slots = rows.shape[0]
    chunks = jax.ShapeDtypeStruct((devices, slots // devices, width), BF16)
    if first:
        extra = (jax.ShapeDtypeStruct(side.shape, F32),)
        held = pltpu.VMEM(side.shape, F32)
    else:
        topk = places.shape[0]
        extra = (jax.ShapeDtypeStruct((topk, count // N_Y), BF16),) * N_Y
        held = pltpu.VMEM((N_Y, topk, count // N_Y), BF16)
    return pl.pallas_call(
        functools.partial(half_kernel, first),
        out_shape=extra + (chunks,),
        in_specs=[ANY] * 4 + ([] if first else [VMEM]),
        out_specs=(ANY,) * (len(extra) + 1),
        scratch_shapes=[
            pltpu.VMEM((count, width), BF16),
            pltpu.VMEM((count, width), BF16),
            pltpu.VMEM((slots, width), BF16),
            pltpu.VMEM(side.shape, F32),
            pltpu.VMEM((slots, count), BF16),
            held,
            pltpu.VMEM((slots, width), F32),
            pltpu.VMEM(chunks.shape, BF16),
            DMA((8,)), DMA((8,)), DMA, DMA((4,)), DMA((4,)), DMA((4,)),
        ],
        compiler_params=params(56),
        cost_estimate=cost(4 * count * width * slots, 24 << 20),
        name="first" if first else "second",
    )(lead, other, stay(rows), stay(side), *(() if first else (places,)))


def own_hits(lists, rows):
    y = lax.axis_index("y")
    slots = lists[0].shape[0]
    i = iota((slots, slots), 0)
    j = iota((slots, slots), 1)
    source = ((i >> 3) << 3) + 2 * y + (i & 1)
    total = jnp.zeros((slots, rows), F32)
    for k, ids in enumerate(lists):
        take = (j == source) & (((i >> 1) & 3) == (y + k) % N_Y)
        hit = (ids[:, :rows] == iota((slots, rows), 1)).astype(F32).astype(BF16)
        total = total + dot(take.astype(F32).astype(BF16), hit, NN)
    return total.astype(BF16)


def hits_kernel(a0, a1, a2, a3, out_ref):
    out_ref[...] = own_hits([a[...] for a in (a0, a1, a2, a3)], out_ref.shape[1])


def hit_rows(lists, rows):
    return pl.pallas_call(
        hits_kernel,
        out_shape=jax.ShapeDtypeStruct((lists[0].shape[0], rows), BF16),
        in_specs=[VMEM] * N_Y,
        out_specs=VMEM,
        compiler_params=params(8),
        cost_estimate=cost(10**7, 10**6),
        name="hits",
    )(*lists)


def sums_kernel(hits_ref, got_hbm, out_hbm, got, sums, sems, out_sems):
    _, width = sums.shape
    devices, capacity, _ = got.shape
    block = 512
    copies = []
    for j in range(width // block):
        cols = pl.ds(j * block, block)
        copies.append(copy(got_hbm.at[:, :, cols], got.at[:, :, cols], sems.at[j]))
        copies[j].start()
    hits = hits_ref[...]
    sent = []
    for j in range(width // block):
        copies[j].wait()
        cols = pl.ds(j * block, block)
        sums[:, cols] = dot(hits, got[:, :, cols].reshape(devices * capacity, block), TN)
        c = copy(sums.at[:, cols], out_hbm.at[:, cols], out_sems.at[j])
        c.start()
        sent.append(c)
    for c in sent:
        c.wait()


def sum_rows(hits, got):
    width = got.shape[2]
    rows = hits.shape[1]
    return pl.pallas_call(
        sums_kernel,
        out_shape=jax.ShapeDtypeStruct((rows, width), F32),
        in_specs=[VMEM, ANY],
        out_specs=ANY,
        scratch_shapes=[
            pltpu.VMEM(got.shape, BF16),
            pltpu.VMEM((rows, width), F32),
            DMA((4,)),
            DMA((4,)),
        ],
        compiler_params=params(12),
        cost_estimate=cost(2 * 256 * 256 * 2048, 2 * 10**6),
    )(hits, stay(got))


def final_kernel(
    mine, c0, c1, c2, c3, p0, p1, p2, p3, d0, d1, d2a, d2b, d3, out_hbm, coef, rows, out, d_sems, out_sems
):
    core = lax.axis_index("core")
    which = core if mine else 1 - core
    half = out.shape[0]
    slots = coef.shape[0] // N_Y
    topk = c0.shape[0]
    loads = []
    start = 0
    for i, d in enumerate((d0, d1, d2a, d2b, d3)):
        loads.append(copy(d, rows.at[pl.ds(start, d.shape[0]), :], d_sems.at[i]))
        start += d.shape[0]
    for c in loads:
        c.start()
    cols = pl.ds(pl.multiple_of(which * half, half), half)
    for r, (small, places) in enumerate(((c0, p0), (c1, p1), (c2, p2), (c3, p3))):
        values = small[:, cols].astype(F32)
        slot = places[:, cols]
        for s in range(0, slots, 64):
            row = iota((64, half), 0) + s
            total = jnp.zeros((64, half), F32)
            for k in range(topk):
                total = jnp.where(row == slot[k : k + 1, :], values[k : k + 1, :], total)
            coef[r * slots + s : r * slots + s + 64, :] = total.astype(BF16)
    for c in loads:
        c.wait()
    width = out.shape[1]
    block = width // 4
    sent = []
    for j in range(4):
        cols = pl.ds(j * block, block)
        out[:, cols] = dot(coef[...], rows[:, cols], TN).astype(BF16)
        c = copy(out.at[:, cols], out_hbm.at[:, cols], out_sems.at[j])
        c.start()
        sent.append(c)
    for c in sent:
        c.wait()


def final_product(mine, coef, places, rows):
    slots, width = rows[0].shape
    half = coef[0].shape[1] // N_CORE
    return pl.pallas_call(
        functools.partial(final_kernel, mine),
        out_shape=jax.ShapeDtypeStruct((half, width), BF16),
        in_specs=[VMEM] * 8 + [ANY] * 5,
        out_specs=ANY,
        scratch_shapes=[
            pltpu.VMEM((N_Y * slots, half), BF16),
            pltpu.VMEM((N_Y * slots, width), BF16),
            pltpu.VMEM((half, width), BF16),
            DMA((5,)), DMA((4,)),
        ],
        compiler_params=params(16),
        cost_estimate=cost(2 * half * 1024 * 2048, 6 << 20),
        name="keep" if mine else "give",
    )(*coef, *places, *rows)


def turn(x, r):
    return lax.ppermute(x, "y", [(i, (i - r) % N_Y) for i in range(N_Y)])


def gathered(blocks):
    return (blocks[0],) + tuple(turn(blocks[N_Y - r], r) for r in range(1, N_Y))


def exchange(x, axes):
    return lax.all_to_all(x, axes, split_axis=0, concat_axis=0, tiled=True)


def program(tokens, out_grad, down_rows, up_rows, requests, places, gate_weights):
    row_count, width = down_rows.shape
    _, devices, capacity = requests.shape
    slots = devices * capacity
    peers = devices // N_Y
    y = lax.axis_index("y")

    def column(x):
        wide = x.reshape(peers, slots // peers, x.shape[1])
        return exchange(wide, ("dp", "core")).reshape(x.shape)

    down_tables = gathered([down_rows] * N_Y)
    asked = column(expand_ids(requests[0]))
    up_tables = gathered([up_rows] * N_Y)
    slot_of = jnp.transpose(places[0])
    slot_of = (slot_of & ~15) | ((slot_of & 2) << 2) | ((slot_of & 12) >> 1) | (slot_of & 1)
    weight = build_weight(slot_of, jnp.transpose(gate_weights[0]), slots)
    down = column(gather_rows(asked, down_tables, width))
    lists = gathered([asked] * N_Y)
    hits = hit_rows(lists, row_count)
    block = slot_of.shape[1] // N_Y
    blocks = [
        lax.dynamic_slice_in_dim(slot_of, ((y + r) & (N_Y - 1)) * block, block, 1) for r in range(N_Y)
    ]
    chip_places = gathered(blocks)
    up = column(gather_rows(asked, up_tables, width))
    above, below = turn(down, 1), turn(down, 3)
    slope, part_up = half_terms(tokens, out_grad, down, weight, devices)
    got_up = exchange(part_up, ("dp", "core", "y"))
    far = (turn(above[: slots // 2], 1), turn(below[slots // 2 :], 3))
    *small, part_down = half_terms(out_grad, tokens, up, slope, devices, slot_of)
    chip_coef = gathered(small)
    got_down = exchange(part_down, ("dp", "core", "y"))
    up_grad = sum_rows(hits, got_up)
    down_all = (down, above, *far, below)
    give = final_product(False, chip_coef, chip_places, down_all)
    other = lax.ppermute(give, "core", [(0, 1), (1, 0)])
    keep = final_product(True, chip_coef, chip_places, down_all)
    input_grad = (keep.astype(F32) + other.astype(F32)).astype(BF16)
    down_grad = sum_rows(hits, got_down)
    return (input_grad, down_grad, up_grad)


def solution(mesh):
    axes = ("dp", "y", "core")
    fine = Mesh(mesh.devices.reshape(mesh.devices.shape[0], N_Y, N_CORE), axes)
    in_specs = (
        P("dp", None),
        P("dp", None),
        P(axes, None),
        P(axes, None),
        P(axes, None, None),
        P(("y", "core"), "dp", None),
        P(("y", "core"), "dp", None),
    )
    out_specs = (P(axes, None), P(axes, None), P(axes, None))
    return jax.shard_map(program, mesh=fine, in_specs=in_specs, out_specs=out_specs, check_vma=False)
```

```python
import functools
import jax
import jax.numpy as jnp
from jax import lax
from jax.experimental import pallas as pl
from jax.experimental.pallas import tpu as pltpu
from jax.sharding import Mesh, PartitionSpec as P

SQRT_HALF = 0.7071067811865476
INV_ROOT_TAU = 0.3989422804014327
N_Y = 4
N_CORE = 2
F32 = jnp.float32
BF16 = jnp.bfloat16
NT = (((1,), (1,)), ((), ()))
NN = (((1,), (0,)), ((), ()))
TN = (((0,), (0,)), ((), ()))
ANY = pl.BlockSpec(memory_space=pl.ANY)
VMEM = pl.BlockSpec(memory_space=pltpu.VMEM)
DMA = pltpu.SemaphoreType.DMA


def dot(a, b, dims):
    return lax.dot_general(a, b, dims, preferred_element_type=F32)


def iota(shape, axis):
    return lax.broadcasted_iota(jnp.int32, shape, axis)


def cost(flops, bytes_accessed, transcendentals=0):
    return pl.CostEstimate(flops=flops, bytes_accessed=bytes_accessed, transcendentals=transcendentals)


def copy(src, dst, sem):
    return pltpu.make_async_copy(src, dst, sem)


def params(mib):
    return pltpu.CompilerParams(vmem_limit_bytes=mib << 20)


def stay(x):
    return pltpu.with_memory_space_constraint(x, pltpu.HBM)


def load_rows(src, dst, sems, pieces):
    rows = src.shape[0] // pieces
    return [
        copy(src.at[pl.ds(i * rows, rows), :], dst.at[pl.ds(i * rows, rows), :], sems.at[i])
        for i in range(pieces)
    ]


def ids_kernel(req_ref, out_ref):
    capacity, owners = req_ref.shape
    slots = out_ref.shape[0]
    row = iota((slots, owners), 0)
    lane = iota((slots, owners), 1)
    per_peer = N_Y * capacity
    peer = row // per_peer
    owner = (peer // N_CORE) * (N_Y * N_CORE) + ((row % per_peer) // capacity) * N_CORE + peer % N_CORE
    total = jnp.zeros((slots, 1), jnp.int32)
    for r in range(capacity):
        hit = (lane == owner) & (row % capacity == r)
        picked = jnp.where(hit, req_ref[r : r + 1, :], 0)
        total = total + jnp.sum(picked, axis=1, keepdims=True)
    out_ref[...] = jnp.broadcast_to(total, out_ref.shape)


def expand_ids(wanted):
    owners, capacity = wanted.shape
    slots = owners * capacity
    return pl.pallas_call(
        ids_kernel,
        out_shape=jax.ShapeDtypeStruct((slots, 128), jnp.int32),
        in_specs=[VMEM],
        out_specs=VMEM,
        cost_estimate=cost(10**5, 10**5),
        name="ids",
    )(jnp.transpose(wanted))


def column_hits(asked, rows):
    y = lax.axis_index("y")
    slots = asked.shape[0]
    shape = (slots, N_Y * rows)
    at = iota(shape, 1)
    owner_y = (iota(shape, 0) % (N_Y * 2)) // 2
    twice = jnp.concatenate([asked] * (N_Y * rows // asked.shape[1]), axis=1)
    hit = (twice == at % rows) & (owner_y == (y + at // rows) % N_Y)
    return hit.astype(F32).astype(BF16)


def gather_kernel(asked_ref, t0, t1, t2, t3, out_hbm, table, out, sems, out_sems):
    rows = t0.shape[0]
    width = out.shape[1]
    copies = [
        copy(t.at[:, pl.ds(0, width)], table.at[pl.ds(r * rows, rows), :], sems.at[r])
        for r, t in enumerate((t0, t1, t2, t3))
    ]
    for c in copies:
        c.start()
    hits = column_hits(asked_ref[...], rows)
    for c in copies:
        c.wait()
    block = width // 4
    sent = []
    for j in range(4):
        cols = pl.ds(j * block, block)
        out[:, cols] = dot(hits, table[:, cols], NN).astype(BF16)
        c = copy(out.at[:, cols], out_hbm.at[:, cols], out_sems.at[j])
        c.start()
        sent.append(c)
    for c in sent:
        c.wait()


def gather_rows(asked, tables, width):
    slots = asked.shape[0]
    rows = tables[0].shape[0]
    return pl.pallas_call(
        gather_kernel,
        out_shape=jax.ShapeDtypeStruct((slots, width), BF16),
        in_specs=[VMEM] + [ANY] * 4,
        out_specs=ANY,
        scratch_shapes=[
            pltpu.VMEM((N_Y * rows, width), BF16),
            pltpu.VMEM((slots, width), BF16),
            DMA((4,)),
            DMA((4,)),
        ],
        compiler_params=params(8),
        cost_estimate=cost(2 * 256 * 256 * 2048, 3 * 10**6),
    )(asked, stay(tables[0]), *tables[1:])


def weight_kernel(places_ref, gates_ref, out_ref):
    topk, block = places_ref.shape
    slots = out_ref.shape[1]
    slot = places_ref[...]
    gates = gates_ref[...]
    for s in range(0, slots, 32):
        row = iota((32, block), 0) + s
        total = jnp.zeros((32, block), F32)
        for k in range(topk):
            total = jnp.where(row == slot[k : k + 1, :], gates[k : k + 1, :], total)
        out_ref[0, s : s + 32, :] = total


def build_weight(places, gates, slots):
    topk, tokens = places.shape
    block = tokens // N_Y
    return pl.pallas_call(
        weight_kernel,
        grid=(N_Y,),
        out_shape=jax.ShapeDtypeStruct((N_Y, slots, block), F32),
        in_specs=[pl.BlockSpec((topk, block), lambda i: (0, i))] * 2,
        out_specs=pl.BlockSpec((1, slots, block), lambda i: (i, 0, 0)),
        compiler_params=params(8),
        cost_estimate=cost(3 * topk * slots * tokens, 4 * slots * tokens),
        name="weight",
    )(places, gates)


def half_kernel(
    first, lead_hbm, other_hbm, rows_hbm, side_hbm, *refs
):
    (
        extra_hbm, part_hbm, lead, other, rows, side, left, slope, half, part,
        lead_sems, other_sems, row_sem, side_sems, extra_sems, part_sems,
    ) = refs[-16:]
    block = side.shape[2]
    width = lead.shape[1]
    step = width // N_Y
    chunk = part.shape[:2] + (step,)
    rows_in = copy(rows_hbm, rows, row_sem)
    side_in = [copy(side_hbm.at[c], side.at[c], side_sems.at[c]) for c in range(N_Y)]
    lead_in = load_rows(lead_hbm, lead, lead_sems, 8)
    other_in = load_rows(other_hbm, other, other_sems, 8)
    sent = []

    def begin(c):
        for i in (2 * c, 2 * c + 1):
            lead_in[i].start()
        side_in[c].start()
        for i in (2 * c, 2 * c + 1):
            other_in[i].start()

    def parts(c, last):
        tokens = pl.ds((c - 1) * block, 2 * block)
        for i in range(2 * c - 2, 2 * c + 2):
            other_in[i].wait()
        for j in range(N_Y):
            cols = pl.ds(j * step, step)
            here = dot(left[:, tokens], other[tokens, cols], NN)
            if not last:
                half[:, cols] = here
                continue
            part[:, :, cols] = (half[:, cols] + here).astype(BF16).reshape(chunk)
            there = pl.ds((width if first else 0) + j * step, step)
            out = copy(part.at[:, :, cols], part_hbm.at[:, :, there], part_sems.at[j])
            out.start()
            sent.append(out)

    rows_in.start()
    begin(0)
    begin(1)
    rows_in.wait()
    for c in range(N_Y):
        here = pl.ds(c * block, block)
        lead_in[2 * c].wait()
        lead_in[2 * c + 1].wait()
        side_in[c].wait()
        if c + 2 < N_Y:
            begin(c + 2)
        found = dot(rows[...], lead[here, :], NT)
        if first:
            cdf = 0.5 * (1.0 + lax.erf(found * SQRT_HALF))
            density = INV_ROOT_TAU * jnp.exp(-0.5 * found * found)
            left[:, here] = (side[c] * (found * cdf)).astype(BF16)
            slope[c] = side[c] * (cdf + found * density)
            out = copy(slope.at[c], extra_hbm.at[c], extra_sems.at[c])
        else:
            left[:, here] = (side[c] * found).astype(BF16)
            out = copy(left.at[:, here], extra_hbm.at[:, here], extra_sems.at[c])
        out.start()
        sent.append(out)
        if c == N_Y // 2 - 1:
            parts(c, False)
    parts(N_Y - 1, True)
    for out in sent:
        out.wait()


def half_terms(lead, other, rows, side, devices, parts=None):
    first = parts is None
    count, width = lead.shape
    slots = rows.shape[0]
    capacity = slots // devices
    extra = (side.shape, F32) if first else ((slots, count), BF16)
    return pl.pallas_call(
        functools.partial(half_kernel, first),
        out_shape=(
            jax.ShapeDtypeStruct(*extra),
            jax.ShapeDtypeStruct((devices, capacity, 2 * width), BF16),
        ),
        in_specs=[ANY] * (4 if first else 5),
        out_specs=(ANY,) * 2,
        scratch_shapes=[
            pltpu.VMEM((count, width), BF16),
            pltpu.VMEM((count, width), BF16),
            pltpu.VMEM((slots, width), BF16),
            pltpu.VMEM(side.shape, F32),
            pltpu.VMEM((slots, count), BF16),
            pltpu.VMEM(side.shape, F32),
            pltpu.VMEM((slots, width), F32),
            pltpu.VMEM((devices, capacity, width), BF16),
            DMA((8,)), DMA((8,)), DMA, DMA((4,)), DMA((4,)), DMA((4,)),
        ],
        input_output_aliases={} if first else {4: 1},
        compiler_params=params(56),
        cost_estimate=cost(4 * count * width * slots, 24 << 20),
        name="first" if first else "second",
    )(lead, other, stay(rows), stay(side), *(() if first else (parts,)))


def compact_kernel(coef_ref, places_ref, c0, c1, c2, c3):
    slots, count = coef_ref.shape
    topk = places_ref.shape[0]
    block = count // N_Y
    y = lax.axis_index("y")
    for r, out in enumerate((c0, c1, c2, c3)):
        here = pl.ds(pl.multiple_of(((y + r) % N_Y) * block, block), block)
        slot = places_ref[:, here]
        lines = []
        row = iota((16, block), 0)
        for k in range(topk):
            want = slot[k : k + 1, :] - row
            found = jnp.zeros((16, block), F32)
            for g in range(0, slots, 16):
                found = jnp.where(want == g, coef_ref[g : g + 16, here].astype(F32), found)
            lines.append(jnp.sum(found, axis=0, keepdims=True))
        out[...] = jnp.concatenate(lines, axis=0).astype(BF16)


def compact(coef, places):
    topk, count = places.shape
    return pl.pallas_call(
        compact_kernel,
        out_shape=tuple(jax.ShapeDtypeStruct((topk, count // N_Y), BF16) for _ in range(N_Y)),
        in_specs=[VMEM] * 2,
        out_specs=(VMEM,) * N_Y,
        compiler_params=params(8),
        cost_estimate=cost(2 * topk * coef.size, 2 * coef.size),
        name="compact",
    )(stay(coef), places)


def own_hits(lists, rows):
    y = lax.axis_index("y")
    slots = lists[0].shape[0]
    i = iota((slots, slots), 0)
    j = iota((slots, slots), 1)
    source = ((i >> 3) << 3) + 2 * y + (i & 1)
    total = jnp.zeros((slots, rows), F32)
    for k, ids in enumerate(lists):
        take = (j == source) & (((i >> 1) & 3) == (y + k) % N_Y)
        hit = (ids[:, :rows] == iota((slots, rows), 1)).astype(F32).astype(BF16)
        total = total + dot(take.astype(F32).astype(BF16), hit, NN)
    return total.astype(BF16)


def hits_kernel(a0, a1, a2, a3, out_ref):
    out_ref[...] = own_hits([a[...] for a in (a0, a1, a2, a3)], out_ref.shape[1])


def hit_rows(lists, rows):
    return pl.pallas_call(
        hits_kernel,
        out_shape=jax.ShapeDtypeStruct((lists[0].shape[0], rows), BF16),
        in_specs=[VMEM] * N_Y,
        out_specs=VMEM,
        compiler_params=params(8),
        cost_estimate=cost(10**7, 10**6),
        name="hits",
    )(*lists)


def sums_kernel(hits_ref, got_hbm, down_hbm, up_hbm, got, sums, sems, out_sems):
    width = down_hbm.shape[1]
    devices, capacity, both = got.shape
    block = 512
    pieces = both // block
    copies = []
    for j in range(pieces):
        cols = pl.ds(j * block, block)
        copies.append(copy(got_hbm.at[:, :, cols], got.at[:, :, cols], sems.at[j]))
        copies[j].start()
    hits = hits_ref[...]
    sent = []
    for j in range(pieces):
        copies[j].wait()
        cols = pl.ds(j * block, block)
        sums[:, cols] = dot(hits, got[:, :, cols].reshape(devices * capacity, block), TN)
        out = (down_hbm, up_hbm)[2 * j // pieces]
        c = copy(sums.at[:, cols], out.at[:, pl.ds(j * block % width, block)], out_sems.at[j])
        c.start()
        sent.append(c)
    for c in sent:
        c.wait()


def sum_rows(hits, got):
    both = got.shape[2]
    rows = hits.shape[1]
    out = jax.ShapeDtypeStruct((rows, both // 2), F32)
    return pl.pallas_call(
        sums_kernel,
        out_shape=(out, out),
        in_specs=[VMEM, ANY],
        out_specs=(ANY, ANY),
        scratch_shapes=[
            pltpu.VMEM(got.shape, BF16),
            pltpu.VMEM((rows, both), F32),
            DMA((8,)),
            DMA((8,)),
        ],
        compiler_params=params(12),
        cost_estimate=cost(2 * 256 * 256 * 2048, 4 * 10**6),
        name="sums",
    )(hits, stay(got))


def final_kernel(
    mine, c0, c1, c2, c3, p0, p1, p2, p3, d0, d1, d2, d3, out_hbm, coef, rows, out, d_sems, out_sems
):
    core = lax.axis_index("core")
    which = core if mine else 1 - core
    half = out.shape[0]
    slots = coef.shape[0] // N_Y
    topk = c0.shape[0]
    loads = []
    start = 0
    for i, d in enumerate((d0, d1, d2, d3)):
        loads.append(copy(d, rows.at[pl.ds(start, d.shape[0]), :], d_sems.at[i]))
        start += d.shape[0]
    for c in loads:
        c.start()
    cols = pl.ds(pl.multiple_of(which * half, half), half)
    for r, (small, places) in enumerate(((c0, p0), (c1, p1), (c2, p2), (c3, p3))):
        values = small[:, cols].astype(F32)
        slot = places[:, cols]
        for s in range(0, slots, 64):
            row = iota((64, half), 0) + s
            total = jnp.zeros((64, half), F32)
            for k in range(topk):
                total = jnp.where(row == slot[k : k + 1, :], values[k : k + 1, :], total)
            coef[r * slots + s : r * slots + s + 64, :] = total.astype(BF16)
    for c in loads:
        c.wait()
    width = out.shape[1]
    block = width // 4
    sent = []
    for j in range(4):
        cols = pl.ds(j * block, block)
        out[:, cols] = dot(coef[...], rows[:, cols], TN).astype(BF16)
        c = copy(out.at[:, cols], out_hbm.at[:, cols], out_sems.at[j])
        c.start()
        sent.append(c)
    for c in sent:
        c.wait()


def final_product(mine, coef, places, rows):
    slots, width = rows[0].shape
    half = coef[0].shape[1] // N_CORE
    return pl.pallas_call(
        functools.partial(final_kernel, mine),
        out_shape=jax.ShapeDtypeStruct((half, width), BF16),
        in_specs=[VMEM] * 8 + [ANY] * 4,
        out_specs=ANY,
        scratch_shapes=[
            pltpu.VMEM((N_Y * slots, half), BF16),
            pltpu.VMEM((N_Y * slots, width), BF16),
            pltpu.VMEM((half, width), BF16),
            DMA((4,)), DMA((4,)),
        ],
        compiler_params=params(16),
        cost_estimate=cost(2 * half * 1024 * 2048, 6 << 20),
        name="keep" if mine else "give",
    )(*coef, *places, *rows)


def turn(x, r):
    return lax.ppermute(x, "y", [(i, (i - r) % N_Y) for i in range(N_Y)])


def gathered(blocks):
    return (blocks[0],) + tuple(turn(blocks[N_Y - r], r) for r in range(1, N_Y))


def exchange(x, axes):
    return lax.all_to_all(x, axes, split_axis=0, concat_axis=0, tiled=True)


def program(tokens, out_grad, down_rows, up_rows, requests, places, gate_weights):
    row_count, width = down_rows.shape
    _, devices, capacity = requests.shape
    slots = devices * capacity
    peers = devices // N_Y
    y = lax.axis_index("y")

    def column(x):
        wide = x.reshape(peers, slots // peers, x.shape[1])
        return exchange(wide, ("dp", "core")).reshape(x.shape)

    down_tables = gathered([down_rows] * N_Y)
    asked = column(expand_ids(requests[0]))
    up_tables = gathered([up_rows] * N_Y)
    slot_of = jnp.transpose(places[0])
    slot_of = (slot_of & ~15) | ((slot_of & 2) << 2) | ((slot_of & 12) >> 1) | (slot_of & 1)
    weight = build_weight(slot_of, jnp.transpose(gate_weights[0]), slots)
    down = column(gather_rows(asked, down_tables, width))
    lists = gathered([asked] * N_Y)
    block = slot_of.shape[1] // N_Y
    blocks = [
        lax.dynamic_slice_in_dim(slot_of, ((y + r) & (N_Y - 1)) * block, block, 1) for r in range(N_Y)
    ]
    chip_places = gathered(blocks)
    up = column(gather_rows(asked, up_tables, width))
    down_all = gathered([down] * N_Y)
    hits = hit_rows(lists, row_count)
    slope, parts = half_terms(tokens, out_grad, down, weight, devices)
    coef, parts = half_terms(out_grad, tokens, up, slope, devices, parts)
    got = exchange(parts, ("dp", "core", "y"))
    small = compact(coef, slot_of)
    chip_coef = gathered(small)
    give = final_product(False, chip_coef, chip_places, down_all)
    other = lax.ppermute(give, "core", [(0, 1), (1, 0)])
    keep = final_product(True, chip_coef, chip_places, down_all)
    input_grad = (keep.astype(F32) + other.astype(F32)).astype(BF16)
    down_grad, up_grad = sum_rows(hits, got)
    return (input_grad, down_grad, up_grad)


def solution(mesh):
    axes = ("dp", "y", "core")
    fine = Mesh(mesh.devices.reshape(mesh.devices.shape[0], N_Y, N_CORE), axes)
    in_specs = (
        P("dp", None),
        P("dp", None),
        P(axes, None),
        P(axes, None),
        P(axes, None, None),
        P(("y", "core"), "dp", None),
        P(("y", "core"), "dp", None),
    )
    out_specs = (P(axes, None), P(axes, None), P(axes, None))
    return jax.shard_map(program, mesh=fine, in_specs=in_specs, out_specs=out_specs, check_vma=False)
```

```python
import functools
import jax
import jax.numpy as jnp
from jax import lax
from jax.experimental import pallas as pl
from jax.experimental.pallas import tpu as pltpu
from jax.sharding import Mesh, PartitionSpec as P

SQRT_HALF = 0.7071067811865476
INV_ROOT_TAU = 0.3989422804014327
N_Y = 4
N_CORE = 2
F32 = jnp.float32
BF16 = jnp.bfloat16
NT = (((1,), (1,)), ((), ()))
NN = (((1,), (0,)), ((), ()))
TN = (((0,), (0,)), ((), ()))
ANY = pl.BlockSpec(memory_space=pl.ANY)
VMEM = pl.BlockSpec(memory_space=pltpu.VMEM)
DMA = pltpu.SemaphoreType.DMA


def dot(a, b, dims):
    return lax.dot_general(a, b, dims, preferred_element_type=F32)


def iota(shape, axis):
    return lax.broadcasted_iota(jnp.int32, shape, axis)


def cost(flops, bytes_accessed, transcendentals=0):
    return pl.CostEstimate(flops=flops, bytes_accessed=bytes_accessed, transcendentals=transcendentals)


def copy(src, dst, sem):
    return pltpu.make_async_copy(src, dst, sem)


def params(mib):
    return pltpu.CompilerParams(vmem_limit_bytes=mib << 20)


def stay(x):
    return pltpu.with_memory_space_constraint(x, pltpu.HBM)


def load_rows(src, dst, sems, pieces):
    rows = src.shape[0] // pieces
    return [
        copy(src.at[pl.ds(i * rows, rows), :], dst.at[pl.ds(i * rows, rows), :], sems.at[i])
        for i in range(pieces)
    ]


def ids_kernel(req_ref, out_ref):
    capacity, owners = req_ref.shape
    slots = out_ref.shape[0]
    row = iota((slots, owners), 0)
    lane = iota((slots, owners), 1)
    per_peer = N_Y * capacity
    peer = row // per_peer
    owner = (peer // N_CORE) * (N_Y * N_CORE) + ((row % per_peer) // capacity) * N_CORE + peer % N_CORE
    total = jnp.zeros((slots, 1), jnp.int32)
    for r in range(capacity):
        hit = (lane == owner) & (row % capacity == r)
        picked = jnp.where(hit, req_ref[r : r + 1, :], 0)
        total = total + jnp.sum(picked, axis=1, keepdims=True)
    out_ref[...] = jnp.broadcast_to(total, out_ref.shape)


def expand_ids(wanted):
    owners, capacity = wanted.shape
    slots = owners * capacity
    return pl.pallas_call(
        ids_kernel,
        out_shape=jax.ShapeDtypeStruct((slots, 128), jnp.int32),
        in_specs=[VMEM],
        out_specs=VMEM,
        cost_estimate=cost(10**5, 10**5),
        name="ids",
    )(jnp.transpose(wanted))


def column_hits(asked, rows):
    y = lax.axis_index("y")
    slots = asked.shape[0]
    shape = (slots, N_Y * rows)
    at = iota(shape, 1)
    owner_y = (iota(shape, 0) % (N_Y * 2)) // 2
    twice = jnp.concatenate([asked] * (N_Y * rows // asked.shape[1]), axis=1)
    hit = (twice == at % rows) & (owner_y == (y + at // rows) % N_Y)
    return hit.astype(F32).astype(BF16)


def gather_kernel(asked_ref, t0, t1, t2, t3, out_hbm, table, out, sems, out_sems):
    rows = t0.shape[0]
    width = out.shape[1]
    copies = [
        copy(t.at[:, pl.ds(0, width)], table.at[pl.ds(r * rows, rows), :], sems.at[r])
        for r, t in enumerate((t0, t1, t2, t3))
    ]
    for c in copies:
        c.start()
    hits = column_hits(asked_ref[...], rows)
    for c in copies:
        c.wait()
    block = width // 4
    sent = []
    for j in range(4):
        cols = pl.ds(j * block, block)
        out[:, cols] = dot(hits, table[:, cols], NN).astype(BF16)
        c = copy(out.at[:, cols], out_hbm.at[:, cols], out_sems.at[j])
        c.start()
        sent.append(c)
    for c in sent:
        c.wait()


def gather_rows(asked, tables, width):
    slots = asked.shape[0]
    rows = tables[0].shape[0]
    return pl.pallas_call(
        gather_kernel,
        out_shape=jax.ShapeDtypeStruct((slots, width), BF16),
        in_specs=[VMEM] + [ANY] * 4,
        out_specs=ANY,
        scratch_shapes=[
            pltpu.VMEM((N_Y * rows, width), BF16),
            pltpu.VMEM((slots, width), BF16),
            DMA((4,)),
            DMA((4,)),
        ],
        compiler_params=params(8),
        cost_estimate=cost(2 * 256 * 256 * 2048, 3 * 10**6),
    )(asked, stay(tables[0]), *tables[1:])


def weight_kernel(places_ref, gates_ref, out_ref):
    topk, block = places_ref.shape
    slots = out_ref.shape[1]
    slot = places_ref[...]
    gates = gates_ref[...]
    for s in range(0, slots, 32):
        row = iota((32, block), 0) + s
        total = jnp.zeros((32, block), F32)
        for k in range(topk):
            total = jnp.where(row == slot[k : k + 1, :], gates[k : k + 1, :], total)
        out_ref[0, s : s + 32, :] = total


def build_weight(places, gates, slots):
    topk, tokens = places.shape
    block = tokens // N_Y
    return pl.pallas_call(
        weight_kernel,
        grid=(N_Y,),
        out_shape=jax.ShapeDtypeStruct((N_Y, slots, block), F32),
        in_specs=[pl.BlockSpec((topk, block), lambda i: (0, i))] * 2,
        out_specs=pl.BlockSpec((1, slots, block), lambda i: (i, 0, 0)),
        compiler_params=params(8),
        cost_estimate=cost(3 * topk * slots * tokens, 4 * slots * tokens),
        name="weight",
    )(places, gates)


def at_places(left, here, slot):
    topk, block = slot.shape
    row = iota((16, block), 0)
    lines = []
    for k in range(topk):
        want = slot[k : k + 1, :] - row
        found = jnp.zeros((16, block), F32)
        for g in range(0, left.shape[0], 16):
            found = jnp.where(want == g, left[g : g + 16, here].astype(F32), found)
        lines.append(jnp.sum(found, axis=0, keepdims=True))
    return jnp.concatenate(lines, axis=0).astype(BF16)


def half_kernel(
    first, lead_hbm, other_hbm, rows_hbm, side_hbm, *refs
):
    places = None if first else refs[0]
    extra_hbm = refs[:1] if first else refs[2 : 2 + N_Y]
    (
        part_hbm, lead, other, rows, side, left, extra, half, part,
        lead_sems, other_sems, row_sem, side_sems, extra_sems, part_sems,
    ) = refs[-15:]
    block = side.shape[2]
    width = lead.shape[1]
    step = width // N_Y
    chunk = part.shape[:2] + (step,)
    rows_in = copy(rows_hbm, rows, row_sem)
    side_in = [copy(side_hbm.at[c], side.at[c], side_sems.at[c]) for c in range(N_Y)]
    lead_in = load_rows(lead_hbm, lead, lead_sems, 8)
    other_in = load_rows(other_hbm, other, other_sems, 8)
    sent = []

    def begin(c):
        for i in (2 * c, 2 * c + 1):
            lead_in[i].start()
        side_in[c].start()
        for i in (2 * c, 2 * c + 1):
            other_in[i].start()

    def parts(c, last):
        tokens = pl.ds((c - 1) * block, 2 * block)
        for i in range(2 * c - 2, 2 * c + 2):
            other_in[i].wait()
        for j in range(N_Y):
            cols = pl.ds(j * step, step)
            here = dot(left[:, tokens], other[tokens, cols], NN)
            if not first and j % 2 == 0:
                at_chunk = c - 1 + j // 2
                mine = pl.ds(at_chunk * block, block)
                extra[at_chunk] = at_places(left, mine, places[:, mine])
            if not last:
                half[:, cols] = here
                continue
            part[:, :, cols] = (half[:, cols] + here).astype(BF16).reshape(chunk)
            there = pl.ds((width if first else 0) + j * step, step)
            out = copy(part.at[:, :, cols], part_hbm.at[:, :, there], part_sems.at[j])
            out.start()
            sent.append(out)

    rows_in.start()
    begin(0)
    begin(1)
    rows_in.wait()
    for c in range(N_Y):
        here = pl.ds(c * block, block)
        lead_in[2 * c].wait()
        lead_in[2 * c + 1].wait()
        side_in[c].wait()
        if c + 2 < N_Y:
            begin(c + 2)
        found = dot(rows[...], lead[here, :], NT)
        if first:
            cdf = 0.5 * (1.0 + lax.erf(found * SQRT_HALF))
            density = INV_ROOT_TAU * jnp.exp(-0.5 * found * found)
            left[:, here] = (side[c] * (found * cdf)).astype(BF16)
            extra[c] = side[c] * (cdf + found * density)
            out = copy(extra.at[c], extra_hbm[0].at[c], extra_sems.at[c])
            out.start()
            sent.append(out)
        else:
            left[:, here] = (side[c] * found).astype(BF16)
        if c == N_Y // 2 - 1:
            parts(c, False)
    parts(N_Y - 1, True)
    if not first:
        y = lax.axis_index("y")
        for r in range(N_Y):
            out = copy(extra.at[(y + r) % N_Y], extra_hbm[r], extra_sems.at[r])
            out.start()
            sent.append(out)
    for out in sent:
        out.wait()


def half_terms(lead, other, rows, side, devices, places=None, parts=None):
    first = parts is None
    count, width = lead.shape
    slots = rows.shape[0]
    capacity = slots // devices
    if first:
        extra = (jax.ShapeDtypeStruct(side.shape, F32),)
        held = pltpu.VMEM(side.shape, F32)
    else:
        topk = places.shape[0]
        extra = (jax.ShapeDtypeStruct((topk, count // N_Y), BF16),) * N_Y
        held = pltpu.VMEM((N_Y, topk, count // N_Y), BF16)
    return pl.pallas_call(
        functools.partial(half_kernel, first),
        out_shape=extra + (jax.ShapeDtypeStruct((devices, capacity, 2 * width), BF16),),
        in_specs=[ANY] * 4 + ([] if first else [VMEM, ANY]),
        out_specs=(ANY,) * (len(extra) + 1),
        scratch_shapes=[
            pltpu.VMEM((count, width), BF16),
            pltpu.VMEM((count, width), BF16),
            pltpu.VMEM((slots, width), BF16),
            pltpu.VMEM(side.shape, F32),
            pltpu.VMEM((slots, count), BF16),
            held,
            pltpu.VMEM((slots, width), F32),
            pltpu.VMEM((devices, capacity, width), BF16),
            DMA((8,)), DMA((8,)), DMA, DMA((4,)), DMA((4,)), DMA((4,)),
        ],
        input_output_aliases={} if first else {5: N_Y},
        compiler_params=params(56),
        cost_estimate=cost(4 * count * width * slots, 24 << 20),
        name="first" if first else "second",
    )(lead, other, stay(rows), stay(side), *(() if first else (places, parts)))


def own_hits(lists, rows):
    y = lax.axis_index("y")
    slots = lists[0].shape[0]
    i = iota((slots, slots), 0)
    j = iota((slots, slots), 1)
    source = ((i >> 3) << 3) + 2 * y + (i & 1)
    total = jnp.zeros((slots, rows), F32)
    for k, ids in enumerate(lists):
        take = (j == source) & (((i >> 1) & 3) == (y + k) % N_Y)
        hit = (ids[:, :rows] == iota((slots, rows), 1)).astype(F32).astype(BF16)
        total = total + dot(take.astype(F32).astype(BF16), hit, NN)
    return total.astype(BF16)


def hits_kernel(a0, a1, a2, a3, out_ref):
    out_ref[...] = own_hits([a[...] for a in (a0, a1, a2, a3)], out_ref.shape[1])


def hit_rows(lists, rows):
    return pl.pallas_call(
        hits_kernel,
        out_shape=jax.ShapeDtypeStruct((lists[0].shape[0], rows), BF16),
        in_specs=[VMEM] * N_Y,
        out_specs=VMEM,
        compiler_params=params(8),
        cost_estimate=cost(10**7, 10**6),
        name="hits",
    )(*lists)


def sums_kernel(hits_ref, got_hbm, down_hbm, up_hbm, got, sums, sems, out_sems):
    width = down_hbm.shape[1]
    devices, capacity, both = got.shape
    block = 512
    pieces = both // block
    copies = []
    for j in range(pieces):
        cols = pl.ds(j * block, block)
        copies.append(copy(got_hbm.at[:, :, cols], got.at[:, :, cols], sems.at[j]))
        copies[j].start()
    hits = hits_ref[...]
    sent = []
    for j in range(pieces):
        copies[j].wait()
        cols = pl.ds(j * block, block)
        sums[:, cols] = dot(hits, got[:, :, cols].reshape(devices * capacity, block), TN)
        out = (down_hbm, up_hbm)[2 * j // pieces]
        c = copy(sums.at[:, cols], out.at[:, pl.ds(j * block % width, block)], out_sems.at[j])
        c.start()
        sent.append(c)
    for c in sent:
        c.wait()


def sum_rows(hits, got):
    both = got.shape[2]
    rows = hits.shape[1]
    out = jax.ShapeDtypeStruct((rows, both // 2), F32)
    return pl.pallas_call(
        sums_kernel,
        out_shape=(out, out),
        in_specs=[VMEM, ANY],
        out_specs=(ANY, ANY),
        scratch_shapes=[
            pltpu.VMEM(got.shape, BF16),
            pltpu.VMEM((rows, both), F32),
            DMA((8,)),
            DMA((8,)),
        ],
        compiler_params=params(12),
        cost_estimate=cost(2 * 256 * 256 * 2048, 4 * 10**6),
        name="sums",
    )(hits, stay(got))


def final_kernel(
    mine, c0, c1, c2, c3, p0, p1, p2, p3, d0, d1, d2, d3, out_hbm, coef, rows, out, d_sems, out_sems
):
    core = lax.axis_index("core")
    which = core if mine else 1 - core
    half = out.shape[0]
    slots = coef.shape[0] // N_Y
    topk = c0.shape[0]
    loads = []
    start = 0
    for i, d in enumerate((d0, d1, d2, d3)):
        loads.append(copy(d, rows.at[pl.ds(start, d.shape[0]), :], d_sems.at[i]))
        start += d.shape[0]
    for c in loads:
        c.start()
    cols = pl.ds(pl.multiple_of(which * half, half), half)
    for r, (small, places) in enumerate(((c0, p0), (c1, p1), (c2, p2), (c3, p3))):
        values = small[:, cols].astype(F32)
        slot = places[:, cols]
        for s in range(0, slots, 64):
            row = iota((64, half), 0) + s
            total = jnp.zeros((64, half), F32)
            for k in range(topk):
                total = jnp.where(row == slot[k : k + 1, :], values[k : k + 1, :], total)
            coef[r * slots + s : r * slots + s + 64, :] = total.astype(BF16)
    for c in loads:
        c.wait()
    width = out.shape[1]
    block = width // 4
    sent = []
    for j in range(4):
        cols = pl.ds(j * block, block)
        out[:, cols] = dot(coef[...], rows[:, cols], TN).astype(BF16)
        c = copy(out.at[:, cols], out_hbm.at[:, cols], out_sems.at[j])
        c.start()
        sent.append(c)
    for c in sent:
        c.wait()


def final_product(mine, coef, places, rows):
    slots, width = rows[0].shape
    half = coef[0].shape[1] // N_CORE
    return pl.pallas_call(
        functools.partial(final_kernel, mine),
        out_shape=jax.ShapeDtypeStruct((half, width), BF16),
        in_specs=[VMEM] * 8 + [ANY] * 4,
        out_specs=ANY,
        scratch_shapes=[
            pltpu.VMEM((N_Y * slots, half), BF16),
            pltpu.VMEM((N_Y * slots, width), BF16),
            pltpu.VMEM((half, width), BF16),
            DMA((4,)), DMA((4,)),
        ],
        compiler_params=params(16),
        cost_estimate=cost(2 * half * 1024 * 2048, 6 << 20),
        name="keep" if mine else "give",
    )(*coef, *places, *rows)


def turn(x, r):
    return lax.ppermute(x, "y", [(i, (i - r) % N_Y) for i in range(N_Y)])


def gathered(blocks):
    return (blocks[0],) + tuple(turn(blocks[N_Y - r], r) for r in range(1, N_Y))


def exchange(x, axes):
    return lax.all_to_all(x, axes, split_axis=0, concat_axis=0, tiled=True)


def program(tokens, out_grad, down_rows, up_rows, requests, places, gate_weights):
    row_count, width = down_rows.shape
    _, devices, capacity = requests.shape
    slots = devices * capacity
    peers = devices // N_Y
    y = lax.axis_index("y")

    def column(x):
        wide = x.reshape(peers, slots // peers, x.shape[1])
        return exchange(wide, ("dp", "core")).reshape(x.shape)

    down_tables = gathered([down_rows] * N_Y)
    asked = column(expand_ids(requests[0]))
    up_tables = gathered([up_rows] * N_Y)
    slot_of = jnp.transpose(places[0])
    slot_of = (slot_of & ~15) | ((slot_of & 2) << 2) | ((slot_of & 12) >> 1) | (slot_of & 1)
    weight = build_weight(slot_of, jnp.transpose(gate_weights[0]), slots)
    down = column(gather_rows(asked, down_tables, width))
    lists = gathered([asked] * N_Y)
    block = slot_of.shape[1] // N_Y
    blocks = [
        lax.dynamic_slice_in_dim(slot_of, ((y + r) & (N_Y - 1)) * block, block, 1) for r in range(N_Y)
    ]
    chip_places = gathered(blocks)
    up = column(gather_rows(asked, up_tables, width))
    down_all = gathered([down] * N_Y)
    hits = hit_rows(lists, row_count)
    slope, parts = half_terms(tokens, out_grad, down, weight, devices)
    *small, parts = half_terms(out_grad, tokens, up, slope, devices, slot_of, parts)
    chip_coef = gathered(small)
    got = exchange(parts, ("dp", "core", "y"))
    give = final_product(False, chip_coef, chip_places, down_all)
    other = lax.ppermute(give, "core", [(0, 1), (1, 0)])
    keep = final_product(True, chip_coef, chip_places, down_all)
    input_grad = (keep.astype(F32) + other.astype(F32)).astype(BF16)
    down_grad, up_grad = sum_rows(hits, got)
    return (input_grad, down_grad, up_grad)


def solution(mesh):
    axes = ("dp", "y", "core")
    fine = Mesh(mesh.devices.reshape(mesh.devices.shape[0], N_Y, N_CORE), axes)
    in_specs = (
        P("dp", None),
        P("dp", None),
        P(axes, None),
        P(axes, None),
        P(axes, None, None),
        P(("y", "core"), "dp", None),
        P(("y", "core"), "dp", None),
    )
    out_specs = (P(axes, None), P(axes, None), P(axes, None))
    return jax.shard_map(program, mesh=fine, in_specs=in_specs, out_specs=out_specs, check_vma=False)
```

```python
import functools
import jax
import jax.numpy as jnp
from jax import lax
from jax.experimental import pallas as pl
from jax.experimental.pallas import tpu as pltpu
from jax.sharding import Mesh, PartitionSpec as P

SQRT_HALF = 0.7071067811865476
INV_ROOT_TAU = 0.3989422804014327
N_Y = 4
N_CORE = 2
F32 = jnp.float32
BF16 = jnp.bfloat16
NT = (((1,), (1,)), ((), ()))
NN = (((1,), (0,)), ((), ()))
TN = (((0,), (0,)), ((), ()))
ANY = pl.BlockSpec(memory_space=pl.ANY)
VMEM = pl.BlockSpec(memory_space=pltpu.VMEM)
DMA = pltpu.SemaphoreType.DMA


def dot(a, b, dims):
    return lax.dot_general(a, b, dims, preferred_element_type=F32)


def iota(shape, axis):
    return lax.broadcasted_iota(jnp.int32, shape, axis)


def cost(flops, bytes_accessed, transcendentals=0):
    return pl.CostEstimate(flops=flops, bytes_accessed=bytes_accessed, transcendentals=transcendentals)


def copy(src, dst, sem):
    return pltpu.make_async_copy(src, dst, sem)


def params(mib):
    return pltpu.CompilerParams(vmem_limit_bytes=mib << 20)


def stay(x):
    return pltpu.with_memory_space_constraint(x, pltpu.HBM)


def load_rows(src, dst, sems, pieces):
    rows = src.shape[0] // pieces
    return [
        copy(src.at[pl.ds(i * rows, rows), :], dst.at[pl.ds(i * rows, rows), :], sems.at[i])
        for i in range(pieces)
    ]


def ids_kernel(req_ref, out_ref):
    capacity, owners = req_ref.shape
    slots = out_ref.shape[0]
    row = iota((slots, owners), 0)
    lane = iota((slots, owners), 1)
    per_peer = N_Y * capacity
    peer = row // per_peer
    owner = (peer // N_CORE) * (N_Y * N_CORE) + ((row % per_peer) // capacity) * N_CORE + peer % N_CORE
    total = jnp.zeros((slots, 1), jnp.int32)
    for r in range(capacity):
        hit = (lane == owner) & (row % capacity == r)
        picked = jnp.where(hit, req_ref[r : r + 1, :], 0)
        total = total + jnp.sum(picked, axis=1, keepdims=True)
    out_ref[...] = jnp.broadcast_to(total, out_ref.shape)


def expand_ids(wanted):
    owners, capacity = wanted.shape
    slots = owners * capacity
    return pl.pallas_call(
        ids_kernel,
        out_shape=jax.ShapeDtypeStruct((slots, 128), jnp.int32),
        in_specs=[VMEM],
        out_specs=VMEM,
        cost_estimate=cost(10**5, 10**5),
        name="ids",
    )(jnp.transpose(wanted))


def column_hits(asked, rows):
    y = lax.axis_index("y")
    slots = asked.shape[0]
    shape = (slots, N_Y * rows)
    at = iota(shape, 1)
    owner_y = (iota(shape, 0) % (N_Y * 2)) // 2
    twice = jnp.concatenate([asked] * (N_Y * rows // asked.shape[1]), axis=1)
    hit = (twice == at % rows) & (owner_y == (y + at // rows) % N_Y)
    return hit.astype(F32).astype(BF16)


def gather_kernel(asked_ref, t0, t1, t2, t3, out_hbm, table, out, sems, out_sems):
    rows = t0.shape[0]
    width = out.shape[1]
    copies = [
        copy(t.at[:, pl.ds(0, width)], table.at[pl.ds(r * rows, rows), :], sems.at[r])
        for r, t in enumerate((t0, t1, t2, t3))
    ]
    for c in copies:
        c.start()
    hits = column_hits(asked_ref[...], rows)
    for c in copies:
        c.wait()
    block = width // 4
    sent = []
    for j in range(4):
        cols = pl.ds(j * block, block)
        out[:, cols] = dot(hits, table[:, cols], NN).astype(BF16)
        c = copy(out.at[:, cols], out_hbm.at[:, cols], out_sems.at[j])
        c.start()
        sent.append(c)
    for c in sent:
        c.wait()


def gather_rows(asked, tables, width):
    slots = asked.shape[0]
    rows = tables[0].shape[0]
    return pl.pallas_call(
        gather_kernel,
        out_shape=jax.ShapeDtypeStruct((slots, width), BF16),
        in_specs=[VMEM] + [ANY] * 4,
        out_specs=ANY,
        scratch_shapes=[
            pltpu.VMEM((N_Y * rows, width), BF16),
            pltpu.VMEM((slots, width), BF16),
            DMA((4,)),
            DMA((4,)),
        ],
        compiler_params=params(8),
        cost_estimate=cost(2 * 256 * 256 * 2048, 3 * 10**6),
    )(asked, stay(tables[0]), *tables[1:])


def weight_kernel(places_ref, gates_ref, out_ref):
    topk, block = places_ref.shape
    slots = out_ref.shape[1]
    slot = places_ref[...]
    gates = gates_ref[...]
    for s in range(0, slots, 32):
        row = iota((32, block), 0) + s
        total = jnp.zeros((32, block), F32)
        for k in range(topk):
            total = jnp.where(row == slot[k : k + 1, :], gates[k : k + 1, :], total)
        out_ref[0, s : s + 32, :] = total


def build_weight(places, gates, slots):
    topk, tokens = places.shape
    block = tokens // N_Y
    return pl.pallas_call(
        weight_kernel,
        grid=(N_Y,),
        out_shape=jax.ShapeDtypeStruct((N_Y, slots, block), F32),
        in_specs=[pl.BlockSpec((topk, block), lambda i: (0, i))] * 2,
        out_specs=pl.BlockSpec((1, slots, block), lambda i: (i, 0, 0)),
        compiler_params=params(8),
        cost_estimate=cost(3 * topk * slots * tokens, 4 * slots * tokens),
        name="weight",
    )(places, gates)


def at_places(left, here, slot):
    topk, block = slot.shape
    row = iota((16, block), 0)
    lines = []
    for k in range(topk):
        want = (slot[k : k + 1, :] - row).astype(jnp.int16)
        found = jnp.zeros((16, block), BF16)
        for g in range(0, left.shape[0], 16):
            found = jnp.where(want == jnp.int16(g), left[g : g + 16, here], found)
        lines.append(jnp.sum(found.astype(F32), axis=0, keepdims=True))
    return jnp.concatenate(lines, axis=0).astype(BF16)


def half_kernel(
    first, lead_hbm, other_hbm, rows_hbm, side_hbm, *refs
):
    places = None if first else refs[0]
    extra_hbm = refs[:1] if first else refs[2 : 2 + N_Y]
    (
        part_hbm, lead, other, rows, side, left, extra, half, part,
        lead_sems, other_sems, row_sem, side_sems, extra_sems, part_sems,
    ) = refs[-15:]
    block = side.shape[2]
    width = lead.shape[1]
    step = width // N_Y
    chunk = part.shape[:2] + (step,)
    rows_in = copy(rows_hbm, rows, row_sem)
    side_in = [copy(side_hbm.at[c], side.at[c], side_sems.at[c]) for c in range(N_Y)]
    lead_in = load_rows(lead_hbm, lead, lead_sems, 8)
    other_in = load_rows(other_hbm, other, other_sems, 8)
    sent = []

    def begin(c):
        for i in (2 * c, 2 * c + 1):
            lead_in[i].start()
        side_in[c].start()
        for i in (2 * c, 2 * c + 1):
            other_in[i].start()

    def parts(c, last):
        tokens = pl.ds((c - 1) * block, 2 * block)
        for i in range(2 * c - 2, 2 * c + 2):
            other_in[i].wait()
        for j in range(N_Y):
            cols = pl.ds(j * step, step)
            here = dot(left[:, tokens], other[tokens, cols], NN)
            if not first and j % 2 == 0:
                at_chunk = c - 1 + j // 2
                mine = pl.ds(at_chunk * block, block)
                extra[at_chunk] = at_places(left, mine, places[:, mine])
            if not last:
                half[:, cols] = here
                continue
            part[:, :, cols] = (half[:, cols] + here).astype(BF16).reshape(chunk)
            there = pl.ds((width if first else 0) + j * step, step)
            out = copy(part.at[:, :, cols], part_hbm.at[:, :, there], part_sems.at[j])
            out.start()
            sent.append(out)

    rows_in.start()
    begin(0)
    begin(1)
    rows_in.wait()
    for c in range(N_Y):
        here = pl.ds(c * block, block)
        lead_in[2 * c].wait()
        lead_in[2 * c + 1].wait()
        side_in[c].wait()
        if c + 2 < N_Y:
            begin(c + 2)
        found = dot(rows[...], lead[here, :], NT)
        if first:
            cdf = 0.5 * (1.0 + lax.erf(found * SQRT_HALF))
            density = INV_ROOT_TAU * jnp.exp(-0.5 * found * found)
            left[:, here] = (side[c] * (found * cdf)).astype(BF16)
            extra[c] = side[c] * (cdf + found * density)
            out = copy(extra.at[c], extra_hbm[0].at[c], extra_sems.at[c])
            out.start()
            sent.append(out)
        else:
            left[:, here] = (side[c] * found).astype(BF16)
        if c == N_Y // 2 - 1:
            parts(c, False)
    parts(N_Y - 1, True)
    if not first:
        y = lax.axis_index("y")
        for r in range(N_Y):
            out = copy(extra.at[(y + r) % N_Y], extra_hbm[r], extra_sems.at[r])
            out.start()
            sent.append(out)
    for out in sent:
        out.wait()


def half_terms(lead, other, rows, side, devices, places=None, parts=None):
    first = parts is None
    count, width = lead.shape
    slots = rows.shape[0]
    capacity = slots // devices
    if first:
        extra = (jax.ShapeDtypeStruct(side.shape, F32),)
        held = pltpu.VMEM(side.shape, F32)
    else:
        topk = places.shape[0]
        extra = (jax.ShapeDtypeStruct((topk, count // N_Y), BF16),) * N_Y
        held = pltpu.VMEM((N_Y, topk, count // N_Y), BF16)
    return pl.pallas_call(
        functools.partial(half_kernel, first),
        out_shape=extra + (jax.ShapeDtypeStruct((devices, capacity, 2 * width), BF16),),
        in_specs=[ANY] * 4 + ([] if first else [VMEM, ANY]),
        out_specs=(ANY,) * (len(extra) + 1),
        scratch_shapes=[
            pltpu.VMEM((count, width), BF16),
            pltpu.VMEM((count, width), BF16),
            pltpu.VMEM((slots, width), BF16),
            pltpu.VMEM(side.shape, F32),
            pltpu.VMEM((slots, count), BF16),
            held,
            pltpu.VMEM((slots, width), F32),
            pltpu.VMEM((devices, capacity, width), BF16),
            DMA((8,)), DMA((8,)), DMA, DMA((4,)), DMA((4,)), DMA((4,)),
        ],
        input_output_aliases={} if first else {5: N_Y},
        compiler_params=params(56),
        cost_estimate=cost(4 * count * width * slots, 24 << 20),
        name="first" if first else "second",
    )(lead, other, stay(rows), stay(side), *(() if first else (places, parts)))


def own_hits(lists, rows):
    y = lax.axis_index("y")
    slots = lists[0].shape[0]
    i = iota((slots, slots), 0)
    j = iota((slots, slots), 1)
    source = ((i >> 3) << 3) + 2 * y + (i & 1)
    total = jnp.zeros((slots, rows), F32)
    for k, ids in enumerate(lists):
        take = (j == source) & (((i >> 1) & 3) == (y + k) % N_Y)
        hit = (ids[:, :rows] == iota((slots, rows), 1)).astype(F32).astype(BF16)
        total = total + dot(take.astype(F32).astype(BF16), hit, NN)
    return total.astype(BF16)


def hits_kernel(a0, a1, a2, a3, out_ref):
    out_ref[...] = own_hits([a[...] for a in (a0, a1, a2, a3)], out_ref.shape[1])


def hit_rows(lists, rows):
    return pl.pallas_call(
        hits_kernel,
        out_shape=jax.ShapeDtypeStruct((lists[0].shape[0], rows), BF16),
        in_specs=[VMEM] * N_Y,
        out_specs=VMEM,
        compiler_params=params(8),
        cost_estimate=cost(10**7, 10**6),
        name="hits",
    )(*lists)


def sums_kernel(hits_ref, got_hbm, down_hbm, up_hbm, got, sums, sems, out_sems):
    width = down_hbm.shape[1]
    devices, capacity, both = got.shape
    block = 512
    pieces = both // block
    copies = []
    for j in range(pieces):
        cols = pl.ds(j * block, block)
        copies.append(copy(got_hbm.at[:, :, cols], got.at[:, :, cols], sems.at[j]))
        copies[j].start()
    hits = hits_ref[...]
    sent = []
    for j in range(pieces):
        copies[j].wait()
        cols = pl.ds(j * block, block)
        sums[:, cols] = dot(hits, got[:, :, cols].reshape(devices * capacity, block), TN)
        out = (down_hbm, up_hbm)[2 * j // pieces]
        c = copy(sums.at[:, cols], out.at[:, pl.ds(j * block % width, block)], out_sems.at[j])
        c.start()
        sent.append(c)
    for c in sent:
        c.wait()


def sum_rows(hits, got):
    both = got.shape[2]
    rows = hits.shape[1]
    out = jax.ShapeDtypeStruct((rows, both // 2), F32)
    return pl.pallas_call(
        sums_kernel,
        out_shape=(out, out),
        in_specs=[VMEM, ANY],
        out_specs=(ANY, ANY),
        scratch_shapes=[
            pltpu.VMEM(got.shape, BF16),
            pltpu.VMEM((rows, both), F32),
            DMA((8,)),
            DMA((8,)),
        ],
        compiler_params=params(12),
        cost_estimate=cost(2 * 256 * 256 * 2048, 4 * 10**6),
        name="sums",
    )(hits, stay(got))


def final_kernel(
    mine, c0, c1, c2, c3, p0, p1, p2, p3, *refs
):
    blocks = refs[:-6]
    out_hbm, coef, rows, out, d_sems, out_sems = refs[-6:]
    core = lax.axis_index("core")
    which = core if mine else 1 - core
    half = out.shape[0]
    slots = coef.shape[0] // N_Y
    topk = c0.shape[0]
    loads = []
    start = 0
    for i, d in enumerate(blocks):
        loads.append(copy(d, rows.at[pl.ds(start, d.shape[0]), :], d_sems.at[i]))
        start += d.shape[0]
    for c in loads:
        c.start()
    cols = pl.ds(pl.multiple_of(which * half, half), half)
    for r, (small, places) in enumerate(((c0, p0), (c1, p1), (c2, p2), (c3, p3))):
        values = small[:, cols].astype(F32)
        slot = places[:, cols]
        for s in range(0, slots, 64):
            row = iota((64, half), 0) + s
            total = jnp.zeros((64, half), F32)
            for k in range(topk):
                total = jnp.where(row == slot[k : k + 1, :], values[k : k + 1, :], total)
            coef[r * slots + s : r * slots + s + 64, :] = total.astype(BF16)
    for c in loads:
        c.wait()
    width = out.shape[1]
    block = width // 4
    sent = []
    for j in range(4):
        cols = pl.ds(j * block, block)
        out[:, cols] = dot(coef[...], rows[:, cols], TN).astype(BF16)
        c = copy(out.at[:, cols], out_hbm.at[:, cols], out_sems.at[j])
        c.start()
        sent.append(c)
    for c in sent:
        c.wait()


def final_product(mine, coef, places, rows):
    slots, width = rows[0].shape
    half = coef[0].shape[1] // N_CORE
    return pl.pallas_call(
        functools.partial(final_kernel, mine),
        out_shape=jax.ShapeDtypeStruct((half, width), BF16),
        in_specs=[VMEM] * 8 + [ANY] * len(rows),
        out_specs=ANY,
        scratch_shapes=[
            pltpu.VMEM((N_Y * slots, half), BF16),
            pltpu.VMEM((N_Y * slots, width), BF16),
            pltpu.VMEM((half, width), BF16),
            DMA((len(rows),)), DMA((4,)),
        ],
        compiler_params=params(16),
        cost_estimate=cost(2 * half * 1024 * 2048, 6 << 20),
        name="keep" if mine else "give",
    )(*coef, *places, *rows)


def turn(x, r):
    return lax.ppermute(x, "y", [(i, (i - r) % N_Y) for i in range(N_Y)])


def gathered(blocks):
    return (blocks[0],) + tuple(turn(blocks[N_Y - r], r) for r in range(1, N_Y))


def exchange(x, axes):
    return lax.all_to_all(x, axes, split_axis=0, concat_axis=0, tiled=True)


def program(tokens, out_grad, down_rows, up_rows, requests, places, gate_weights):
    row_count, width = down_rows.shape
    _, devices, capacity = requests.shape
    slots = devices * capacity
    peers = devices // N_Y
    y = lax.axis_index("y")

    def column(x):
        wide = x.reshape(peers, slots // peers, x.shape[1])
        return exchange(wide, ("dp", "core")).reshape(x.shape)

    down_tables = gathered([down_rows] * N_Y)
    asked = column(expand_ids(requests[0]))
    up_tables = gathered([up_rows] * N_Y)
    slot_of = jnp.transpose(places[0])
    slot_of = (slot_of & ~15) | ((slot_of & 2) << 2) | ((slot_of & 12) >> 1) | (slot_of & 1)
    weight = build_weight(slot_of, jnp.transpose(gate_weights[0]), slots)
    down = column(gather_rows(asked, down_tables, width))
    lists = gathered([asked] * N_Y)
    block = slot_of.shape[1] // N_Y
    blocks = [
        lax.dynamic_slice_in_dim(slot_of, ((y + r) & (N_Y - 1)) * block, block, 1) for r in range(N_Y)
    ]
    chip_places = gathered(blocks)
    up = column(gather_rows(asked, up_tables, width))
    head, tail = down[: slots // 2], down[slots // 2 :]
    above_head, below_tail = turn(head, 1), turn(tail, 3)
    above_tail, below_head = turn(tail, 1), turn(head, 3)
    far_head, far_tail = turn(above_head, 1), turn(below_tail, 3)
    down_all = (down, above_head, above_tail, far_head, far_tail, below_head, below_tail)
    hits = hit_rows(lists, row_count)
    slope, parts = half_terms(tokens, out_grad, down, weight, devices)
    *small, parts = half_terms(out_grad, tokens, up, slope, devices, slot_of, parts)
    chip_coef = gathered(small)
    got = exchange(parts, ("dp", "core", "y"))
    give = final_product(False, chip_coef, chip_places, down_all)
    other = lax.ppermute(give, "core", [(0, 1), (1, 0)])
    keep = final_product(True, chip_coef, chip_places, down_all)
    input_grad = (keep.astype(F32) + other.astype(F32)).astype(BF16)
    down_grad, up_grad = sum_rows(hits, got)
    return (input_grad, down_grad, up_grad)


def solution(mesh):
    axes = ("dp", "y", "core")
    fine = Mesh(mesh.devices.reshape(mesh.devices.shape[0], N_Y, N_CORE), axes)
    in_specs = (
        P("dp", None),
        P("dp", None),
        P(axes, None),
        P(axes, None),
        P(axes, None, None),
        P(("y", "core"), "dp", None),
        P(("y", "core"), "dp", None),
    )
    out_specs = (P(axes, None), P(axes, None), P(axes, None))
    return jax.shard_map(program, mesh=fine, in_specs=in_specs, out_specs=out_specs, check_vma=False)
```

```python
import functools
import jax
import jax.numpy as jnp
from jax import lax
from jax.experimental import pallas as pl
from jax.experimental.pallas import tpu as pltpu
from jax.sharding import Mesh, PartitionSpec as P

SQRT_HALF = 0.7071067811865476
INV_ROOT_TAU = 0.3989422804014327
N_Y = 4
N_CORE = 2
F32 = jnp.float32
BF16 = jnp.bfloat16
NT = (((1,), (1,)), ((), ()))
NN = (((1,), (0,)), ((), ()))
TN = (((0,), (0,)), ((), ()))
ANY = pl.BlockSpec(memory_space=pl.ANY)
VMEM = pl.BlockSpec(memory_space=pltpu.VMEM)
DMA = pltpu.SemaphoreType.DMA


def dot(a, b, dims):
    return lax.dot_general(a, b, dims, preferred_element_type=F32)


def iota(shape, axis):
    return lax.broadcasted_iota(jnp.int32, shape, axis)


def cost(flops, bytes_accessed, transcendentals=0):
    return pl.CostEstimate(flops=flops, bytes_accessed=bytes_accessed, transcendentals=transcendentals)


def copy(src, dst, sem):
    return pltpu.make_async_copy(src, dst, sem)


def params(mib):
    return pltpu.CompilerParams(vmem_limit_bytes=mib << 20)


def stay(x):
    return pltpu.with_memory_space_constraint(x, pltpu.HBM)


def load_rows(src, dst, sems, pieces):
    rows = src.shape[0] // pieces
    return [
        copy(src.at[pl.ds(i * rows, rows), :], dst.at[pl.ds(i * rows, rows), :], sems.at[i])
        for i in range(pieces)
    ]


def ids_kernel(req_ref, out_ref):
    capacity, owners = req_ref.shape
    slots = out_ref.shape[0]
    row = iota((slots, owners), 0)
    lane = iota((slots, owners), 1)
    per_peer = N_Y * capacity
    peer = row // per_peer
    owner = (peer // N_CORE) * (N_Y * N_CORE) + ((row % per_peer) // capacity) * N_CORE + peer % N_CORE
    total = jnp.zeros((slots, 1), jnp.int32)
    for r in range(capacity):
        hit = (lane == owner) & (row % capacity == r)
        picked = jnp.where(hit, req_ref[r : r + 1, :], 0)
        total = total + jnp.sum(picked, axis=1, keepdims=True)
    out_ref[...] = jnp.broadcast_to(total, out_ref.shape)


def expand_ids(wanted):
    owners, capacity = wanted.shape
    slots = owners * capacity
    return pl.pallas_call(
        ids_kernel,
        out_shape=jax.ShapeDtypeStruct((slots, 128), jnp.int32),
        in_specs=[VMEM],
        out_specs=VMEM,
        cost_estimate=cost(10**5, 10**5),
        name="ids",
    )(jnp.transpose(wanted))


def column_hits(asked, rows):
    y = lax.axis_index("y")
    slots = asked.shape[0]
    shape = (slots, N_Y * rows)
    at = iota(shape, 1)
    owner_y = (iota(shape, 0) % (N_Y * 2)) // 2
    twice = jnp.concatenate([asked] * (N_Y * rows // asked.shape[1]), axis=1)
    hit = (twice == at % rows) & (owner_y == (y + at // rows) % N_Y)
    return hit.astype(F32).astype(BF16)


def gather_kernel(asked_ref, t0, t1, t2, t3, out_hbm, table, out, sems, out_sems):
    rows = t0.shape[0]
    width = out.shape[1]
    copies = [
        copy(t.at[:, pl.ds(0, width)], table.at[pl.ds(r * rows, rows), :], sems.at[r])
        for r, t in enumerate((t0, t1, t2, t3))
    ]
    for c in copies:
        c.start()
    hits = column_hits(asked_ref[...], rows)
    for c in copies:
        c.wait()
    block = width // 4
    sent = []
    for j in range(4):
        cols = pl.ds(j * block, block)
        out[:, cols] = dot(hits, table[:, cols], NN).astype(BF16)
        c = copy(out.at[:, cols], out_hbm.at[:, cols], out_sems.at[j])
        c.start()
        sent.append(c)
    for c in sent:
        c.wait()


def gather_rows(asked, tables, width):
    slots = asked.shape[0]
    rows = tables[0].shape[0]
    return pl.pallas_call(
        gather_kernel,
        out_shape=jax.ShapeDtypeStruct((slots, width), BF16),
        in_specs=[VMEM] + [ANY] * 4,
        out_specs=ANY,
        scratch_shapes=[
            pltpu.VMEM((N_Y * rows, width), BF16),
            pltpu.VMEM((slots, width), BF16),
            DMA((4,)),
            DMA((4,)),
        ],
        compiler_params=params(8),
        cost_estimate=cost(2 * 256 * 256 * 2048, 3 * 10**6),
    )(asked, stay(tables[0]), *tables[1:])


def weight_kernel(places_ref, gates_ref, out_ref):
    topk, block = places_ref.shape
    slots = out_ref.shape[1]
    slot = places_ref[...]
    gates = gates_ref[...]
    for s in range(0, slots, 32):
        row = iota((32, block), 0) + s
        total = jnp.zeros((32, block), F32)
        for k in range(topk):
            total = jnp.where(row == slot[k : k + 1, :], gates[k : k + 1, :], total)
        out_ref[0, s : s + 32, :] = total


def build_weight(places, gates, slots):
    topk, tokens = places.shape
    block = tokens // N_Y
    return pl.pallas_call(
        weight_kernel,
        grid=(N_Y,),
        out_shape=jax.ShapeDtypeStruct((N_Y, slots, block), F32),
        in_specs=[pl.BlockSpec((topk, block), lambda i: (0, i))] * 2,
        out_specs=pl.BlockSpec((1, slots, block), lambda i: (i, 0, 0)),
        compiler_params=params(8),
        cost_estimate=cost(3 * topk * slots * tokens, 4 * slots * tokens),
        name="weight",
    )(places, gates)


def at_places(left, here, slot):
    topk, block = slot.shape
    row = iota((16, block), 0)
    lines = []
    for k in range(topk):
        want = (slot[k : k + 1, :] - row).astype(jnp.int16)
        found = jnp.zeros((16, block), BF16)
        for g in range(0, left.shape[0], 16):
            found = jnp.where(want == jnp.int16(g), left[g : g + 16, here], found)
        lines.append(jnp.sum(found.astype(F32), axis=0, keepdims=True))
    return jnp.concatenate(lines, axis=0).astype(BF16)


def half_kernel(
    first, lead_hbm, other_hbm, rows_hbm, side_hbm, *refs
):
    places = None if first else refs[0]
    extra_hbm = refs[:1] if first else refs[1 : 1 + N_Y]
    (
        part_hbm, lead, other, rows, side, left, extra, half, part,
        lead_sems, other_sems, row_sem, side_sems, extra_sems, part_sems,
    ) = refs[-15:]
    block = side.shape[2]
    width = lead.shape[1]
    step = width // N_Y
    chunk = part.shape[:2] + (step,)
    rows_in = copy(rows_hbm, rows, row_sem)
    side_in = [copy(side_hbm.at[c], side.at[c], side_sems.at[c]) for c in range(N_Y)]
    lead_in = load_rows(lead_hbm, lead, lead_sems, 8)
    other_in = load_rows(other_hbm, other, other_sems, 8)
    sent = []

    def begin(c):
        for i in (2 * c, 2 * c + 1):
            lead_in[i].start()
        side_in[c].start()
        for i in (2 * c, 2 * c + 1):
            other_in[i].start()

    def parts(c, last):
        tokens = pl.ds((c - 1) * block, 2 * block)
        for i in range(2 * c - 2, 2 * c + 2):
            other_in[i].wait()
        for j in range(N_Y):
            cols = pl.ds(j * step, step)
            here = dot(left[:, tokens], other[tokens, cols], NN)
            if not first and j % 2 == 0:
                at_chunk = c - 1 + j // 2
                mine = pl.ds(at_chunk * block, block)
                extra[at_chunk] = at_places(left, mine, places[:, mine])
            if not last:
                half[:, cols] = here
                continue
            part[:, :, cols] = (half[:, cols] + here).astype(BF16).reshape(chunk)
            out = copy(part.at[:, :, cols], part_hbm.at[:, :, cols], part_sems.at[j])
            out.start()
            sent.append(out)

    rows_in.start()
    begin(0)
    begin(1)
    rows_in.wait()
    for c in range(N_Y):
        here = pl.ds(c * block, block)
        lead_in[2 * c].wait()
        lead_in[2 * c + 1].wait()
        side_in[c].wait()
        if c + 2 < N_Y:
            begin(c + 2)
        found = dot(rows[...], lead[here, :], NT)
        if first:
            cdf = 0.5 * (1.0 + lax.erf(found * SQRT_HALF))
            density = INV_ROOT_TAU * jnp.exp(-0.5 * found * found)
            left[:, here] = (side[c] * (found * cdf)).astype(BF16)
            extra[c] = side[c] * (cdf + found * density)
            out = copy(extra.at[c], extra_hbm[0].at[c], extra_sems.at[c])
            out.start()
            sent.append(out)
        else:
            left[:, here] = (side[c] * found).astype(BF16)
        if c == N_Y // 2 - 1:
            parts(c, False)
    parts(N_Y - 1, True)
    if not first:
        y = lax.axis_index("y")
        for r in range(N_Y):
            out = copy(extra.at[(y + r) % N_Y], extra_hbm[r], extra_sems.at[r])
            out.start()
            sent.append(out)
    for out in sent:
        out.wait()


def half_terms(lead, other, rows, side, devices, places=None):
    first = places is None
    count, width = lead.shape
    slots = rows.shape[0]
    capacity = slots // devices
    if first:
        extra = (jax.ShapeDtypeStruct(side.shape, F32),)
        held = pltpu.VMEM(side.shape, F32)
    else:
        topk = places.shape[0]
        extra = (jax.ShapeDtypeStruct((topk, count // N_Y), BF16),) * N_Y
        held = pltpu.VMEM((N_Y, topk, count // N_Y), BF16)
    return pl.pallas_call(
        functools.partial(half_kernel, first),
        out_shape=extra + (jax.ShapeDtypeStruct((devices, capacity, width), BF16),),
        in_specs=[ANY] * 4 + ([] if first else [VMEM]),
        out_specs=(ANY,) * (len(extra) + 1),
        scratch_shapes=[
            pltpu.VMEM((count, width), BF16),
            pltpu.VMEM((count, width), BF16),
            pltpu.VMEM((slots, width), BF16),
            pltpu.VMEM(side.shape, F32),
            pltpu.VMEM((slots, count), BF16),
            held,
            pltpu.VMEM((slots, width), F32),
            pltpu.VMEM((devices, capacity, width), BF16),
            DMA((8,)), DMA((8,)), DMA, DMA((4,)), DMA((4,)), DMA((4,)),
        ],
        compiler_params=params(56),
        cost_estimate=cost(4 * count * width * slots, 24 << 20),
        name="first" if first else "second",
    )(lead, other, stay(rows), stay(side), *(() if first else (places,)))


def own_hits(lists, rows):
    y = lax.axis_index("y")
    slots = lists[0].shape[0]
    i = iota((slots, slots), 0)
    j = iota((slots, slots), 1)
    source = ((i >> 3) << 3) + 2 * y + (i & 1)
    total = jnp.zeros((slots, rows), F32)
    for k, ids in enumerate(lists):
        take = (j == source) & (((i >> 1) & 3) == (y + k) % N_Y)
        hit = (ids[:, :rows] == iota((slots, rows), 1)).astype(F32).astype(BF16)
        total = total + dot(take.astype(F32).astype(BF16), hit, NN)
    return total.astype(BF16)


def hits_kernel(a0, a1, a2, a3, out_ref):
    out_ref[...] = own_hits([a[...] for a in (a0, a1, a2, a3)], out_ref.shape[1])


def hit_rows(lists, rows):
    return pl.pallas_call(
        hits_kernel,
        out_shape=jax.ShapeDtypeStruct((lists[0].shape[0], rows), BF16),
        in_specs=[VMEM] * N_Y,
        out_specs=VMEM,
        compiler_params=params(8),
        cost_estimate=cost(10**7, 10**6),
        name="hits",
    )(*lists)


def sums_kernel(hits_ref, got_hbm, out_hbm, got, sums, sems, out_sems):
    _, width = sums.shape
    devices, capacity, _ = got.shape
    block = 512
    copies = []
    for j in range(width // block):
        cols = pl.ds(j * block, block)
        copies.append(copy(got_hbm.at[:, :, cols], got.at[:, :, cols], sems.at[j]))
        copies[j].start()
    hits = hits_ref[...]
    sent = []
    for j in range(width // block):
        copies[j].wait()
        cols = pl.ds(j * block, block)
        sums[:, cols] = dot(hits, got[:, :, cols].reshape(devices * capacity, block), TN)
        c = copy(sums.at[:, cols], out_hbm.at[:, cols], out_sems.at[j])
        c.start()
        sent.append(c)
    for c in sent:
        c.wait()


def sum_rows(hits, got):
    width = got.shape[2]
    rows = hits.shape[1]
    return pl.pallas_call(
        sums_kernel,
        out_shape=jax.ShapeDtypeStruct((rows, width), F32),
        in_specs=[VMEM, ANY],
        out_specs=ANY,
        scratch_shapes=[
            pltpu.VMEM(got.shape, BF16),
            pltpu.VMEM((rows, width), F32),
            DMA((4,)),
            DMA((4,)),
        ],
        compiler_params=params(12),
        cost_estimate=cost(2 * 256 * 256 * 2048, 2 * 10**6),
    )(hits, stay(got))


def final_kernel(
    mine, c0, c1, c2, c3, p0, p1, p2, p3, *refs
):
    blocks = refs[:-6]
    out_hbm, coef, rows, out, d_sems, out_sems = refs[-6:]
    core = lax.axis_index("core")
    which = core if mine else 1 - core
    half = out.shape[0]
    slots = coef.shape[0] // N_Y
    topk = c0.shape[0]
    loads = []
    start = 0
    for i, d in enumerate(blocks):
        loads.append(copy(d, rows.at[pl.ds(start, d.shape[0]), :], d_sems.at[i]))
        start += d.shape[0]
    for c in loads:
        c.start()
    cols = pl.ds(pl.multiple_of(which * half, half), half)
    for r, (small, places) in enumerate(((c0, p0), (c1, p1), (c2, p2), (c3, p3))):
        values = small[:, cols].astype(F32)
        slot = places[:, cols]
        for s in range(0, slots, 64):
            row = iota((64, half), 0) + s
            total = jnp.zeros((64, half), F32)
            for k in range(topk):
                total = jnp.where(row == slot[k : k + 1, :], values[k : k + 1, :], total)
            coef[r * slots + s : r * slots + s + 64, :] = total.astype(BF16)
    for c in loads:
        c.wait()
    width = out.shape[1]
    block = width // 4
    sent = []
    for j in range(4):
        cols = pl.ds(j * block, block)
        out[:, cols] = dot(coef[...], rows[:, cols], TN).astype(BF16)
        c = copy(out.at[:, cols], out_hbm.at[:, cols], out_sems.at[j])
        c.start()
        sent.append(c)
    for c in sent:
        c.wait()


def final_product(mine, coef, places, rows):
    slots, width = rows[0].shape
    half = coef[0].shape[1] // N_CORE
    return pl.pallas_call(
        functools.partial(final_kernel, mine),
        out_shape=jax.ShapeDtypeStruct((half, width), BF16),
        in_specs=[VMEM] * 8 + [ANY] * len(rows),
        out_specs=ANY,
        scratch_shapes=[
            pltpu.VMEM((N_Y * slots, half), BF16),
            pltpu.VMEM((N_Y * slots, width), BF16),
            pltpu.VMEM((half, width), BF16),
            DMA((len(rows),)), DMA((4,)),
        ],
        compiler_params=params(16),
        cost_estimate=cost(2 * half * 1024 * 2048, 6 << 20),
        name="keep" if mine else "give",
    )(*coef, *places, *rows)


def turn(x, r):
    return lax.ppermute(x, "y", [(i, (i - r) % N_Y) for i in range(N_Y)])


def gathered(blocks):
    return (blocks[0],) + tuple(turn(blocks[N_Y - r], r) for r in range(1, N_Y))


def exchange(x, axes):
    return lax.all_to_all(x, axes, split_axis=0, concat_axis=0, tiled=True)


def program(tokens, out_grad, down_rows, up_rows, requests, places, gate_weights):
    row_count, width = down_rows.shape
    _, devices, capacity = requests.shape
    slots = devices * capacity
    peers = devices // N_Y
    y = lax.axis_index("y")

    def column(x):
        wide = x.reshape(peers, slots // peers, x.shape[1])
        return exchange(wide, ("dp", "core")).reshape(x.shape)

    down_tables = gathered([down_rows] * N_Y)
    asked = column(expand_ids(requests[0]))
    up_tables = gathered([up_rows] * N_Y)
    slot_of = jnp.transpose(places[0])
    slot_of = (slot_of & ~15) | ((slot_of & 2) << 2) | ((slot_of & 12) >> 1) | (slot_of & 1)
    weight = build_weight(slot_of, jnp.transpose(gate_weights[0]), slots)
    down = column(gather_rows(asked, down_tables, width))
    lists = gathered([asked] * N_Y)
    block = slot_of.shape[1] // N_Y
    blocks = [
        lax.dynamic_slice_in_dim(slot_of, ((y + r) & (N_Y - 1)) * block, block, 1) for r in range(N_Y)
    ]
    chip_places = gathered(blocks)
    up = column(gather_rows(asked, up_tables, width))
    head, tail = down[: slots // 2], down[slots // 2 :]
    above_head, below_tail = turn(head, 1), turn(tail, 3)
    above_tail, below_head = turn(tail, 1), turn(head, 3)
    far_head, far_tail = turn(above_head, 1), turn(below_tail, 3)
    down_all = (down, above_head, above_tail, far_head, far_tail, below_head, below_tail)
    hits = hit_rows(lists, row_count)
    slope, part_up = half_terms(tokens, out_grad, down, weight, devices)
    got_up = exchange(part_up, ("dp", "core", "y"))
    *small, part_down = half_terms(out_grad, tokens, up, slope, devices, slot_of)
    chip_coef = gathered(small)
    got_down = exchange(part_down, ("dp", "core", "y"))
    up_grad = sum_rows(hits, got_up)
    give = final_product(False, chip_coef, chip_places, down_all)
    other = lax.ppermute(give, "core", [(0, 1), (1, 0)])
    keep = final_product(True, chip_coef, chip_places, down_all)
    input_grad = (keep.astype(F32) + other.astype(F32)).astype(BF16)
    down_grad = sum_rows(hits, got_down)
    return (input_grad, down_grad, up_grad)


def solution(mesh):
    axes = ("dp", "y", "core")
    fine = Mesh(mesh.devices.reshape(mesh.devices.shape[0], N_Y, N_CORE), axes)
    in_specs = (
        P("dp", None),
        P("dp", None),
        P(axes, None),
        P(axes, None),
        P(axes, None, None),
        P(("y", "core"), "dp", None),
        P(("y", "core"), "dp", None),
    )
    out_specs = (P(axes, None), P(axes, None), P(axes, None))
    return jax.shard_map(program, mesh=fine, in_specs=in_specs, out_specs=out_specs, check_vma=False)
```
